32 devices in a mesh: gz: 2 (over x), gy: 4 (over z), gx: 4 (over y, core).
Axes of the slice: x: 2, y: 2, z: 4, core: 2. Of those that a mesh axis runs over, the one named last changes fastest.
Arguments:
- images: bfloat16 [2, 640, 640], P('gz', 'gy', 'gx'), may hold values from -6 to 6
- tissue_mask: int32 [2, 16, 16], P('gz', 'gy', 'gx'), may hold values 0 or 1
Outputs:
- flow_fields: float32 [4, 2, 16, 16], P(None, 'gz', 'gy', 'gx')
- mesh_offsets: float32 [2, 2, 16, 16], P(None, 'gz', 'gy', 'gx')
The draws below stay inside these ranges and needn't reach their ends.
Inputs may be any that keep to these rules, and one draw needn't show every extreme that they name: `tissue_mask`: 0 or 1 for each patch.
All inputs are finite; a program needn't handle non-finite values. No bound on the sum of `tissue_mask` on one device may be relied on, other than what follows from the above.
Results may differ from the reference program's by a relative error of at most 0.0003.
Values may be sent and summed in bfloat16 or wider, within the bound.
No kernel may reach another device: no remote copies, remote signals or barrier semaphores. Data moves between devices by JAX's collectives and lax.ppermute only.
A program may use at most 128 MiB of HBM per device.

```python
import jax
import jax.numpy as jnp
from jax import lax

PATCH = 160
STRIDE = 40
RELAX = 4
SECTIONS = 2
HEIGHT = 640
WIDTH = 640
NODES_Y = 16
NODES_X = 16


def plant(result, rng, least, top_value):
    index_at = [jax.random.randint(jax.random.fold_in(rng, axis), (), 0, length) for axis, length in enumerate(result.shape)]
    main_axis = result.shape.index(max(result.shape))
    beside = index_at[:main_axis] + [(index_at[main_axis] + 1) % result.shape[main_axis]] + index_at[main_axis + 1:]
    return result.at[tuple(index_at)].set(least).at[tuple(beside)].set(top_value)


def level_of(key, dims, cuts, least, largest):
    level = 1.0
    for dim, blocks in cuts:
        draws = jax.random.uniform(jax.random.fold_in(jax.random.fold_in(key, 6), dim), (blocks,), jnp.float32, least / len(cuts), largest / len(cuts))
        level = level * jnp.repeat(jnp.exp(draws), dims[dim] // blocks).reshape((-1,) + (1,) * (len(dims) - 1 - dim))
    return level


def normal_values(key, shape, width, limit, shards=(), held_as=jnp.bfloat16):
    values = width * jax.random.normal(key, shape, jnp.float32)
    if shards:
        values = values * level_of(key, shape, shards, -0.22, 0.18)
    return jnp.clip(values, -limit, limit).astype(held_as)


def setup_inputs(seed: int = 0) -> dict:
    keys = jax.random.split(jax.random.key(seed), 3)
    return {
        "images": normal_values(keys[0], (SECTIONS, HEIGHT, WIDTH), 1.0, 6.0, ((0, 2), (1, 4), (2, 4))),
        "tissue_mask": plant((jax.random.randint(keys[1], (SECTIONS, NODES_Y, NODES_X), 0, 4) < 3).astype(jnp.int32), jax.random.fold_in(keys[1], 1), 0, 1),
    }


EPSILON = 1e-6
STIFFNESS = 0.5
STEP_SIZE = 0.2


def windows(section):
    repeats = PATCH // STRIDE
    count_y = section.shape[0] // STRIDE - repeats + 1
    count_x = section.shape[1] // STRIDE - repeats + 1
    blocks = section.reshape(section.shape[0] // STRIDE, STRIDE, section.shape[1] // STRIDE, STRIDE)
    pieces = []
    for first in range(repeats):
        row_pieces = [blocks[first:first + count_y, :, second:second + count_x, :] for second in range(repeats)]
        pieces.append(jnp.stack(row_pieces, 0))
    stacked = jnp.stack(pieces, 0)
    stacked = jnp.transpose(stacked, (2, 4, 0, 3, 1, 5))
    return stacked.reshape(count_y * count_x, PATCH, PATCH)


def centroid(correl):
    squared = correl * correl
    weights = squared * squared
    totals = jnp.sum(weights, axis=(1, 2)) + EPSILON
    shifts = ((jnp.arange(PATCH, dtype=jnp.int32) + PATCH // 2) % PATCH - PATCH // 2).astype(jnp.float32)
    flow_y = jnp.sum(weights * shifts[None, :, None], axis=(1, 2)) / totals
    flow_x = jnp.sum(weights * shifts[None, None, :], axis=(1, 2)) / totals
    return flow_y, flow_x


def upward(fields, distance):
    return jnp.pad(fields[:, distance:], ((0, 0), (0, distance), (0, 0), (0, 0)))


def downward(fields, distance):
    return jnp.pad(fields[:, :SECTIONS - distance], ((0, 0), (distance, 0), (0, 0), (0, 0)))


def reference(images, tissue_mask):
    margin = (PATCH - STRIDE) // 2
    nodes_y = HEIGHT // STRIDE
    nodes_x = WIDTH // STRIDE
    padded = jnp.pad(images.astype(jnp.float32), ((0, 2), (margin, margin), (margin, margin)))

    def spectra_of(position):
        section = lax.dynamic_index_in_dim(padded, position, 0, keepdims=False)
        return jnp.fft.fft2(windows(section))

    def section_flows(position):
        own_spec = spectra_of(position)
        results = []
        for distance in (1, 2):
            others = spectra_of(position + distance)
            correl = jnp.real(jnp.fft.ifft2(others * jnp.conj(own_spec))).astype(jnp.float32)
            flow_y, flow_x = centroid(correl)
            results.append(flow_y)
            results.append(flow_x)
        return jnp.stack(results, 0)

    flow_all = lax.map(section_flows, jnp.arange(SECTIONS, dtype=jnp.int32))
    flow_fields = jnp.transpose(flow_all, (1, 0, 2)).reshape(4, SECTIONS, nodes_y, nodes_x)
    mask_float = tissue_mask.astype(jnp.float32)
    mask_padded = jnp.pad(mask_float, ((0, 2), (0, 0), (0, 0)))
    weight_one = (mask_float * mask_padded[1:SECTIONS + 1])[None]
    weight_two = (mask_float * mask_padded[2:SECTIONS + 2])[None]
    flow_one = flow_fields[0:2]
    flow_two = flow_fields[2:4]
    low_weight_one = downward(weight_one, 1)
    low_weight_two = downward(weight_two, 2)
    low_flow_one = downward(flow_one, 1)
    low_flow_two = downward(flow_two, 2)
    offsets = jnp.zeros((2, SECTIONS, nodes_y, nodes_x), jnp.float32)
    for _ in range(RELAX):
        widened = jnp.pad(offsets, ((0, 0), (0, 0), (1, 1), (1, 1)))
        laplace = (widened[:, :, :-2, 1:-1] + widened[:, :, 2:, 1:-1] + widened[:, :, 1:-1, :-2]
                   + widened[:, :, 1:-1, 2:] - 4.0 * offsets)
        forces = STIFFNESS * laplace
        forces = forces + weight_one * (upward(offsets, 1) - offsets - flow_one)
        forces = forces + weight_two * (upward(offsets, 2) - offsets - flow_two)
        forces = forces - low_weight_one * (offsets - downward(offsets, 1) - low_flow_one)
        forces = forces - low_weight_two * (offsets - downward(offsets, 2) - low_flow_two)
        offsets = offsets + STEP_SIZE * forces
    return flow_fields, offsets
```

```python
import functools
import math

import jax
import jax.numpy as jnp
import numpy as np
from jax import lax
from jax.experimental import pallas as pl
from jax.experimental.pallas import tpu as pltpu
from jax.sharding import PartitionSpec as P

PATCH = 160
STRIDE = 40
RELAX = 4


EPSILON = 1e-06
STIFFNESS = 0.5
STEP_SIZE = 0.2


def shifted(value, axis, steps):
    count = lax.axis_size(axis)
    initial, last = (max(0, -steps), min(count, count - steps))
    return lax.ppermute(value, axis, [(source, source + steps) for source in range(initial, last)])


def padded_2(x, sides, width):
    for axis, dim in sides:
        size, length = (lax.axis_size(axis), x.shape[dim])
        up = [(i, (i + 1) % size) for i in range(size - 1)]
        down = [(j, i) for i, j in up]
        last = lax.slice_in_dim(x, length - width, length, axis=dim)
        initial = lax.slice_in_dim(x, 0, width, axis=dim)
        before = lax.ppermute(last, axis, up)
        after = lax.ppermute(initial, axis, down)
        x = jnp.concatenate([before, x, after], axis=dim)
    return x


def windows(section):
    repeats = PATCH // STRIDE
    count_y = section.shape[0] // STRIDE - repeats + 1
    count_x = section.shape[1] // STRIDE - repeats + 1
    blocks = section.reshape(section.shape[0] // STRIDE, STRIDE, section.shape[1] // STRIDE, STRIDE)
    pieces = []
    for first in range(repeats):
        row_pieces = [
            blocks[first : first + count_y, :, second : second + count_x, :]
            for second in range(repeats)
        ]
        pieces.append(jnp.stack(row_pieces, 0))
    stacked = jnp.stack(pieces, 0)
    stacked = jnp.transpose(stacked, (2, 4, 0, 3, 1, 5))
    return stacked.reshape(count_y * count_x, PATCH, PATCH)


def tables():
    indices = jnp.arange(PATCH, dtype=jnp.int32)
    phases = indices[:, None] * indices[None, :] % PATCH
    angles = phases.astype(jnp.float32) * (2.0 * math.pi / PATCH)
    cosine_table = jnp.cos(angles)
    sine_table = jnp.sin(angles)
    left_table = jnp.concatenate([cosine_table, sine_table], 0)
    right_table = jnp.concatenate([cosine_table, sine_table], 1)
    return (left_table, right_table)


def spectrum(section, left_table, right_table):
    patches = windows(section)
    halfway = jnp.einsum("pnm,mk->pnk", patches, right_table, precision=lax.Precision.HIGHEST)
    products = jnp.einsum("kn,pnm->pkm", left_table, halfway, precision=lax.Precision.HIGHEST)
    cos_a = products[:, :PATCH, :PATCH]
    cos_b = products[:, :PATCH, PATCH:]
    sin_a = products[:, PATCH:, :PATCH]
    sin_b = products[:, PATCH:, PATCH:]
    return (cos_a - sin_b, -(cos_b + sin_a))


def flow_between(own_re, own_im, next_re, next_im, left_table, count_y, count_x):
    cross_re = next_re * own_re + next_im * own_im
    cross_im = next_im * own_re - next_re * own_im
    stacked = jnp.concatenate([cross_re, cross_im], 2)
    products = jnp.einsum("kn,pnm->pkm", left_table, stacked, precision=lax.Precision.HIGHEST)
    mixed_re = products[:, :PATCH, :PATCH] - products[:, PATCH:, PATCH:]
    mixed_im = products[:, :PATCH, PATCH:] + products[:, PATCH:, :PATCH]
    joined = jnp.concatenate([mixed_re, -mixed_im], 2)
    correl = jnp.einsum("pnm,mk->pnk", joined, left_table, precision=lax.Precision.HIGHEST) / (
        PATCH * PATCH
    )
    squared = correl * correl
    weights = squared * squared
    totals = jnp.sum(weights, axis=(1, 2)) + EPSILON
    shifts = ((jnp.arange(PATCH, dtype=jnp.int32) + PATCH // 2) % PATCH - PATCH // 2).astype(
        jnp.float32
    )
    flow_y = jnp.sum(weights * shifts[None, :, None], axis=(1, 2)) / totals
    flow_x = jnp.sum(weights * shifts[None, None, :], axis=(1, 2)) / totals
    return jnp.stack([flow_y, flow_x], 0).reshape(2, count_y, count_x)


def laplacian(widened, offsets):
    return (
        widened[:, :, :-2, 1:-1]
        + widened[:, :, 2:, 1:-1]
        + widened[:, :, 1:-1, :-2]
        + widened[:, :, 1:-1, 2:]
        - 4.0 * offsets
    )


def remote_neighbours(offsets):
    up_one = shifted(offsets, "gz", -1)
    up_two = shifted(offsets, "gz", -2)
    down_one = shifted(offsets, "gz", 1)
    down_two = shifted(offsets, "gz", 2)
    return (up_one, up_two, down_one, down_two)


def mesh_step(offsets, laplace, coeffs):
    up_one, up_two, down_one, down_two = remote_neighbours(offsets)
    forces = STIFFNESS * laplace
    forces = forces + coeffs[2:3] * (up_one - offsets - coeffs[0:2])
    forces = forces + coeffs[5:6] * (up_two - offsets - coeffs[3:5])
    forces = forces - coeffs[8:9] * (offsets - down_one - coeffs[6:8])
    forces = forces - coeffs[11:12] * (offsets - down_two - coeffs[9:11])
    return offsets + STEP_SIZE * forces


def general_body(images, tissue_mask):
    margin = (PATCH - STRIDE) // 2
    count_y = images.shape[1] // STRIDE
    count_x = images.shape[2] // STRIDE
    padded = padded_2(images, (("gy", 1), ("gx", 2)), margin)
    left_table, right_table = tables()
    own_mask = tissue_mask.astype(jnp.float32)
    own_re, own_im = spectrum(padded[0].astype(jnp.float32), left_table, right_table)
    next_re, next_im, next_mask = shifted((own_re, own_im, own_mask), "gz", -1)
    far_re, far_im, far_mask = shifted((own_re, own_im, own_mask), "gz", -2)
    flow_one = flow_between(own_re, own_im, next_re, next_im, left_table, count_y, count_x)
    flow_two = flow_between(own_re, own_im, far_re, far_im, left_table, count_y, count_x)
    weight_one = own_mask * next_mask
    weight_two = own_mask * far_mask
    low_flow_one, low_weight_one = shifted((flow_one, weight_one), "gz", 1)
    low_flow_two, low_weight_two = shifted((flow_two, weight_two), "gz", 2)
    coeffs = jnp.concatenate(
        [
            flow_one,
            weight_one,
            flow_two,
            weight_two,
            low_flow_one,
            low_weight_one,
            low_flow_two,
            low_weight_two,
        ],
        0,
    )[:, None]
    spread = padded_2(coeffs, (("gy", 2), ("gx", 3)), RELAX)
    global_y = lax.axis_index("gy") * count_y + jnp.arange(-RELAX, count_y + RELAX, dtype=jnp.int32)
    global_x = lax.axis_index("gx") * count_x + jnp.arange(-RELAX, count_x + RELAX, dtype=jnp.int32)
    inside_y = (global_y >= 0) & (global_y < count_y * lax.axis_size("gy"))
    inside_x = (global_x >= 0) & (global_x < count_x * lax.axis_size("gx"))
    inside = (inside_y[:, None] & inside_x[None, :]).astype(jnp.float32)
    offsets = jnp.zeros((2, 1, count_y + 2 * RELAX, count_x + 2 * RELAX), jnp.float32)
    for _ in range(RELAX):
        widened = jnp.pad(offsets, ((0, 0), (0, 0), (1, 1), (1, 1)))
        offsets = mesh_step(offsets, laplacian(widened, offsets), spread) * inside[None, None]
    offsets = offsets[:, :, RELAX : RELAX + count_y, RELAX : RELAX + count_x]
    flow_fields = jnp.concatenate([flow_one, flow_two], 0)[:, None]
    return (flow_fields, offsets)


MARGIN = (PATCH - STRIDE) // 2
HALF = PATCH // 2 + 1
LANES = 128
SUBLANES = 8
ROWS_K = -(-HALF // SUBLANES) * SUBLANES
HALO = -(-MARGIN // 16) * 16
RADIUS = RELAX - 1


def split_table(table):
    high = table.astype(jnp.bfloat16)
    low = (table - high.astype(np.float64)).astype(jnp.bfloat16)
    return np.stack([high, low])


def trig(first, second):
    angle = 2.0 * np.pi / PATCH * ((first[:, None] * second[None, :]) % PATCH)
    return np.cos(angle), np.sin(angle)


def column_table():
    cosine, sine = trig(np.arange(PATCH), np.arange(HALF))
    table = np.zeros((PATCH, 2 * LANES))
    table[:, :HALF] = cosine
    table[:, LANES : LANES + HALF] = sine
    return split_table(table)


def row_table(halves, rows):
    table = np.zeros((halves, rows, 2 * ROWS_K, PATCH + HALO))
    for half in range(halves):
        halo_first = PATCH - HALO if half == 0 else 0
        position = np.concatenate([np.arange(PATCH), halo_first + np.arange(HALO)])
        cosine, sine = trig(np.arange(HALF), position)
        for row in range(rows):
            start = (half * rows + row) * STRIDE - MARGIN
            own = (np.arange(PATCH) >= start) & (np.arange(PATCH) < start + PATCH)
            offset = -PATCH if half == 0 else PATCH
            outer = halo_first + np.arange(HALO) + offset
            outer = (outer >= start) & (outer < start + PATCH)
            used = np.concatenate([own, outer])
            table[half, row, :HALF] = cosine * used
            table[half, row, ROWS_K : ROWS_K + HALF] = sine * used
    table = table.reshape(halves, rows * 2 * ROWS_K, PATCH + HALO)
    return np.stack([split_table(table[half]) for half in range(halves)])


def inverse_tables():
    cosine, sine = trig(np.arange(PATCH), np.arange(HALF))
    weight = np.full((HALF,), 2.0 / PATCH)
    weight[0] = weight[-1] = 1.0 / PATCH
    left = np.zeros((PATCH, 2 * ROWS_K))
    left[:, :HALF] = cosine * weight
    left[:, ROWS_K : ROWS_K + HALF] = -sine * weight
    right = np.zeros((2 * LANES, PATCH))
    right[:HALF] = (cosine * weight).T
    right[LANES : LANES + HALF] = -(sine * weight).T
    return split_table(left), split_table(right)


def dot(left, right):
    return jnp.dot(left, right, preferred_element_type=jnp.float32)


def halves_of(value):
    high = value.astype(jnp.bfloat16)
    return high, (value - high.astype(jnp.float32)).astype(jnp.bfloat16)


def table_first(table, value):
    high, low = halves_of(value)
    return dot(table[0], high) + dot(table[1], high) + dot(table[0], low)


def table_last(value, table):
    high, low = halves_of(value)
    return dot(high, table[0]) + dot(high, table[1]) + dot(low, table[0])


def flow_kernel(rows, columns, where_ref, own_ref, other_ref, diagonal_ref, first_ref, second_ref,
                mask_ref, column_ref, row_ref, left_ref, right_ref, out_ref, rows_ref):
    half = where_ref[0]
    odd = where_ref[1] == 1
    lane = lax.broadcasted_iota(jnp.int32, (PATCH + HALO, LANES), 1)
    wide = lax.broadcasted_iota(jnp.int32, (PATCH + HALO, PATCH), 1)
    held = []
    for image in range(2):
        tile = own_ref[0] if image == 0 else other_ref[0]
        mine = jnp.concatenate([tile, diagonal_ref[1 - image]], 0).astype(jnp.float32)
        one = first_ref[image].astype(jnp.float32)
        two = second_ref[image].astype(jnp.float32)
        before = jnp.where(odd, one, two)
        after = jnp.where(odd, two, one)
        beside = jnp.concatenate(
            [jnp.where(lane < LANES // 2, after, before), before[:, : PATCH - LANES]], 1
        )
        held.append((mine, beside))
    sign = jnp.where(half == 0, 1.0, -1.0).astype(jnp.float32)
    window_rows = 2 * ROWS_K
    count = rows * columns
    for column in range(columns):
        start = column * STRIDE - MARGIN
        inside = wide < start + PATCH if start < 0 else wide >= start
        spectra = []
        for mine, beside in held:
            pixels = jnp.where(inside, mine, beside).astype(jnp.bfloat16)
            partial = dot(pixels, column_ref[0]) + dot(pixels, column_ref[1])
            high, low = halves_of(partial)
            spectra.append(
                dot(row_ref[half, 0], high) + dot(row_ref[half, 1], high) + dot(row_ref[half, 0], low)
            )
        for row in range(rows):
            parts = []
            for spectrum_of in spectra:
                top = spectrum_of[row * window_rows : row * window_rows + ROWS_K]
                low = spectrum_of[row * window_rows + ROWS_K : (row + 1) * window_rows]
                parts.append((top[:, :LANES], top[:, LANES:], low[:, :LANES], low[:, LANES:]))
            (acc, acs, asc, ass), (bcc, bcs, bsc, bss) = parts
            even = acc * bcc + asc * bsc + acs * bcs + ass * bss
            by_row = sign * (asc * bcc - acc * bsc + ass * bcs - acs * bss)
            by_column = sign * (acs * bcc - acc * bcs + ass * bsc - asc * bss)
            both = acc * bss + ass * bcc - asc * bcs - acs * bsc
            cross = jnp.concatenate(
                [jnp.concatenate([even, by_column], 1), jnp.concatenate([by_row, both], 1)], 0
            )
            correl = table_last(table_first(left_ref, cross), right_ref)
            squared = correl * correl
            weights = squared * squared
            total = weights[:SUBLANES]
            based = jnp.zeros_like(total)
            for group in range(1, PATCH // SUBLANES):
                piece = weights[group * SUBLANES : (group + 1) * SUBLANES]
                base = group * SUBLANES
                base = base - PATCH if base >= PATCH // 2 else base
                total = total + piece
                based = based + piece * float(base)
            step = lax.broadcasted_iota(jnp.int32, (SUBLANES, PATCH), 0).astype(jnp.float32)
            based = based + step * total
            patch = row * columns + column
            rows_ref[0, pl.ds(patch, 1)] = jnp.sum(total, 0, keepdims=True)
            rows_ref[1, pl.ds(patch, 1)] = jnp.sum(based, 0, keepdims=True)
    totals = rows_ref[0]
    shift = lax.broadcasted_iota(jnp.int32, (count, PATCH), 1)
    shift = jnp.where(shift >= PATCH // 2, shift - PATCH, shift).astype(jnp.float32)
    below = jnp.sum(totals, 1, keepdims=True) + EPSILON
    flow_y = jnp.sum(rows_ref[1], 1, keepdims=True) / below
    flow_x = jnp.sum(totals * shift, 1, keepdims=True) / below
    at = lax.broadcasted_iota(jnp.int32, (count, LANES), 1)
    patch = lax.broadcasted_iota(jnp.int32, (count, LANES), 0)
    line = jnp.where(at == patch, flow_y, 0.0) + jnp.where(at == patch + count, flow_x, 0.0)
    line = jnp.sum(line, 0, keepdims=True)
    lanes = lax.broadcasted_iota(jnp.int32, (1, LANES), 1)
    mask = mask_ref[0].astype(jnp.float32)
    for row in range(mask.shape[0]):
        for column in range(columns):
            spot = 2 * count + row * columns + column
            line = jnp.where(lanes == spot, mask[row : row + 1, column : column + 1], line)
    out_ref[...] = jnp.broadcast_to(line, out_ref.shape)


def relax_kernel(rows, columns, grid_shape, where_ref, got_ref, flow_ref, offsets_ref):
    _, size_y, size_x = grid_shape
    half, at_y, at_x = where_ref[0], where_ref[2], where_ref[3]
    count = rows * columns
    tile_rows = 2 * rows
    width = columns + 2 * RADIUS
    height = tile_rows + 2 * RADIUS
    devices = got_ref.shape[0]
    lane = lax.broadcasted_iota(jnp.int32, (1, LANES), 1).astype(jnp.float32)
    line = jnp.floor((lane + 0.5) * (1.0 / width))
    across = lane - line * width
    node_y = line.astype(jnp.int32) - RADIUS + at_y * tile_rows
    node_x = across.astype(jnp.int32) - RADIUS + at_x * columns
    inside = (node_y >= 0) & (node_y < tile_rows * size_y) & (node_x >= 0)
    inside = inside & (node_x < columns * size_x) & (line < height)

    def parts(value, size):
        whole = jnp.floor((value.astype(jnp.float32) + 0.5) * (1.0 / size)).astype(jnp.int32)
        return whole, value - whole * size

    tile_y, in_y = parts(node_y, tile_rows)
    tile_x, in_x = parts(node_x, columns)
    side, in_half = parts(in_y, rows)
    tile = tile_y * size_x + tile_x
    per_section = size_y * size_x
    flow_key = jnp.where(inside, (side * per_section + tile) * count + in_half * columns + in_x, -1)
    mask_key = jnp.where(inside, tile * (2 * count) + in_y * columns + in_x, -1)
    got = got_ref[...]
    source = lax.broadcasted_iota(jnp.int32, (devices, LANES), 0)
    sums = [jnp.zeros((devices, LANES), jnp.float32) for _ in range(2)]
    for node in range(count):
        hit = source * count + node == flow_key
        for axis in range(2):
            spot = axis * count + node
            sums[axis] = sums[axis] + jnp.where(hit, got[:, spot : spot + 1], 0.0)
    masks = [jnp.zeros((per_section, LANES), jnp.float32) for _ in range(2)]
    source = source[:per_section]
    for node in range(2 * count):
        hit = source * (2 * count) + node == mask_key
        spot = 2 * count + node
        for section in range(2):
            piece = got[section * per_section : (section + 1) * per_section, spot : spot + 1]
            masks[section] = masks[section] + jnp.where(hit, piece, 0.0)
    flows = jnp.concatenate([jnp.sum(total, 0, keepdims=True) for total in sums], 0)
    weight = jnp.sum(masks[0], 0, keepdims=True) * jnp.sum(masks[1], 0, keepdims=True)
    kept = inside.astype(jnp.float32)
    upper = jnp.zeros((2, LANES), jnp.float32)
    lower = jnp.zeros((2, LANES), jnp.float32)

    def laplacian_of(value):
        left = jnp.where(across < 0.5, 0.0, pltpu.roll(value, 1, 1))
        right = jnp.where(across > width - 1.5, 0.0, pltpu.roll(value, LANES - 1, 1))
        return pltpu.roll(value, width, 1) + pltpu.roll(value, LANES - width, 1) + left + right - 4.0 * value

    for _ in range(RELAX):
        pull = weight * (upper - lower - flows)
        lower, upper = (
            (lower + STEP_SIZE * (STIFFNESS * laplacian_of(lower) + pull)) * kept,
            (upper + STEP_SIZE * (STIFFNESS * laplacian_of(upper) - pull)) * kept,
        )
    first = half == 0
    result = jnp.where(first, lower, upper)
    flows = jnp.where(first, flows, 0.0)
    flow_ref[...] = jnp.zeros_like(flow_ref)
    for row in range(tile_rows):
        start = (RADIUS + row) * width + RADIUS
        for axis in range(2):
            offsets_ref[axis, 0, pl.ds(row, 1)] = result[axis : axis + 1, start : start + columns]
            flow_ref[axis, 0, pl.ds(row, 1)] = flows[axis : axis + 1, start : start + columns]


def vmem(count):
    return [pl.BlockSpec(memory_space=pltpu.VMEM)] * count


def pair_body(images, tissue_mask):
    sections, size_y, size_x = (lax.axis_size(name) for name in ("gz", "gy", "gx"))
    count_y = images.shape[1] // STRIDE
    count_x = images.shape[2] // STRIDE
    rows = count_y // 2
    half, at_y, at_x = (lax.axis_index(name) for name in ("gz", "gy", "gx"))
    odd = at_x % 2
    where = jnp.stack([half, odd, at_y, at_x]).astype(jnp.int32)
    other = lax.ppermute(images, "gz", [(0, 1), (1, 0)])
    both = jnp.concatenate([images, other], 0)
    edge = jnp.where(half == 1, both[:, PATCH - HALO :], both[:, :HALO])
    diagonal = []
    for tile in range(1, size_y):
        diagonal += [(size_y + tile - 1, tile), (tile, size_y + tile - 1)]
    beyond = lax.ppermute(edge, ("gz", "gy"), diagonal)
    tall = jnp.concatenate([both, beyond[::-1]], 1)
    low_side = tall[:, :, :LANES]
    high_side = jnp.concatenate([tall[:, :, LANES:], tall[:, :, PATCH - LANES : LANES]], 2)
    is_odd = odd == 1
    swaps = [
        [pair for left in range(offset, size_x - 1, 2) for pair in ((left, left + 1), (left + 1, left))]
        for offset in range(2)
    ]
    first = lax.ppermute(jnp.where(is_odd, low_side, high_side), "gx", swaps[0])
    second = lax.ppermute(jnp.where(is_odd, high_side, low_side), "gx", swaps[1])
    devices = sections * size_y * size_x
    left, right = inverse_tables()
    scalars = pl.BlockSpec(memory_space=pltpu.SMEM)
    lines = pl.pallas_call(
        functools.partial(flow_kernel, rows, count_x),
        out_shape=jax.ShapeDtypeStruct((devices, LANES), jnp.float32),
        in_specs=[scalars] + vmem(10),
        out_specs=vmem(1)[0],
        scratch_shapes=[pltpu.VMEM((2, rows * count_x, PATCH), jnp.float32)],
        name="flows",
    )(
        where,
        images,
        other,
        beyond,
        first,
        second,
        tissue_mask,
        jnp.asarray(column_table()),
        jnp.asarray(row_table(2, rows)),
        jnp.asarray(left),
        jnp.asarray(right),
    )
    got = lax.all_to_all(lines, ("gz", "gy", "gx"), 0, 0, tiled=True)
    return pl.pallas_call(
        functools.partial(relax_kernel, rows, count_x, (sections, size_y, size_x)),
        out_shape=(
            jax.ShapeDtypeStruct((4, 1, count_y, count_x), jnp.float32),
            jax.ShapeDtypeStruct((2, 1, count_y, count_x), jnp.float32),
        ),
        in_specs=[scalars] + vmem(1),
        out_specs=tuple(vmem(2)),
        name="relax",
    )(where, got)


def body(images, tissue_mask):
    paired = lax.axis_size("gz") == 2 and images.shape == (1, PATCH, PATCH)
    return (pair_body if paired else general_body)(images, tissue_mask)


def solution(mesh):
    placed = (P("gz", "gy", "gx"), P("gz", "gy", "gx"))
    return jax.shard_map(
        body,
        mesh=mesh,
        in_specs=placed,
        out_specs=(P(None, "gz", "gy", "gx"), P(None, "gz", "gy", "gx")),
        check_vma=False,
    )
```

```python
import functools
import math

import jax
import jax.numpy as jnp
import numpy as np
from jax import lax
from jax.experimental import pallas as pl
from jax.experimental.pallas import tpu as pltpu
from jax.sharding import PartitionSpec as P

PATCH = 160
STRIDE = 40
RELAX = 4


EPSILON = 1e-06
STIFFNESS = 0.5
STEP_SIZE = 0.2


def shifted(value, axis, steps):
    count = lax.axis_size(axis)
    initial, last = (max(0, -steps), min(count, count - steps))
    return lax.ppermute(value, axis, [(source, source + steps) for source in range(initial, last)])


def padded_2(x, sides, width):
    for axis, dim in sides:
        size, length = (lax.axis_size(axis), x.shape[dim])
        up = [(i, (i + 1) % size) for i in range(size - 1)]
        down = [(j, i) for i, j in up]
        last = lax.slice_in_dim(x, length - width, length, axis=dim)
        initial = lax.slice_in_dim(x, 0, width, axis=dim)
        before = lax.ppermute(last, axis, up)
        after = lax.ppermute(initial, axis, down)
        x = jnp.concatenate([before, x, after], axis=dim)
    return x


def windows(section):
    repeats = PATCH // STRIDE
    count_y = section.shape[0] // STRIDE - repeats + 1
    count_x = section.shape[1] // STRIDE - repeats + 1
    blocks = section.reshape(section.shape[0] // STRIDE, STRIDE, section.shape[1] // STRIDE, STRIDE)
    pieces = []
    for first in range(repeats):
        row_pieces = [
            blocks[first : first + count_y, :, second : second + count_x, :]
            for second in range(repeats)
        ]
        pieces.append(jnp.stack(row_pieces, 0))
    stacked = jnp.stack(pieces, 0)
    stacked = jnp.transpose(stacked, (2, 4, 0, 3, 1, 5))
    return stacked.reshape(count_y * count_x, PATCH, PATCH)


def tables():
    indices = jnp.arange(PATCH, dtype=jnp.int32)
    phases = indices[:, None] * indices[None, :] % PATCH
    angles = phases.astype(jnp.float32) * (2.0 * math.pi / PATCH)
    cosine_table = jnp.cos(angles)
    sine_table = jnp.sin(angles)
    left_table = jnp.concatenate([cosine_table, sine_table], 0)
    right_table = jnp.concatenate([cosine_table, sine_table], 1)
    return (left_table, right_table)


def spectrum(section, left_table, right_table):
    patches = windows(section)
    halfway = jnp.einsum("pnm,mk->pnk", patches, right_table, precision=lax.Precision.HIGHEST)
    products = jnp.einsum("kn,pnm->pkm", left_table, halfway, precision=lax.Precision.HIGHEST)
    cos_a = products[:, :PATCH, :PATCH]
    cos_b = products[:, :PATCH, PATCH:]
    sin_a = products[:, PATCH:, :PATCH]
    sin_b = products[:, PATCH:, PATCH:]
    return (cos_a - sin_b, -(cos_b + sin_a))


def flow_between(own_re, own_im, next_re, next_im, left_table, count_y, count_x):
    cross_re = next_re * own_re + next_im * own_im
    cross_im = next_im * own_re - next_re * own_im
    stacked = jnp.concatenate([cross_re, cross_im], 2)
    products = jnp.einsum("kn,pnm->pkm", left_table, stacked, precision=lax.Precision.HIGHEST)
    mixed_re = products[:, :PATCH, :PATCH] - products[:, PATCH:, PATCH:]
    mixed_im = products[:, :PATCH, PATCH:] + products[:, PATCH:, :PATCH]
    joined = jnp.concatenate([mixed_re, -mixed_im], 2)
    correl = jnp.einsum("pnm,mk->pnk", joined, left_table, precision=lax.Precision.HIGHEST) / (
        PATCH * PATCH
    )
    squared = correl * correl
    weights = squared * squared
    totals = jnp.sum(weights, axis=(1, 2)) + EPSILON
    shifts = ((jnp.arange(PATCH, dtype=jnp.int32) + PATCH // 2) % PATCH - PATCH // 2).astype(
        jnp.float32
    )
    flow_y = jnp.sum(weights * shifts[None, :, None], axis=(1, 2)) / totals
    flow_x = jnp.sum(weights * shifts[None, None, :], axis=(1, 2)) / totals
    return jnp.stack([flow_y, flow_x], 0).reshape(2, count_y, count_x)


def laplacian(widened, offsets):
    return (
        widened[:, :, :-2, 1:-1]
        + widened[:, :, 2:, 1:-1]
        + widened[:, :, 1:-1, :-2]
        + widened[:, :, 1:-1, 2:]
        - 4.0 * offsets
    )


def remote_neighbours(offsets):
    up_one = shifted(offsets, "gz", -1)
    up_two = shifted(offsets, "gz", -2)
    down_one = shifted(offsets, "gz", 1)
    down_two = shifted(offsets, "gz", 2)
    return (up_one, up_two, down_one, down_two)


def mesh_step(offsets, laplace, coeffs):
    up_one, up_two, down_one, down_two = remote_neighbours(offsets)
    forces = STIFFNESS * laplace
    forces = forces + coeffs[2:3] * (up_one - offsets - coeffs[0:2])
    forces = forces + coeffs[5:6] * (up_two - offsets - coeffs[3:5])
    forces = forces - coeffs[8:9] * (offsets - down_one - coeffs[6:8])
    forces = forces - coeffs[11:12] * (offsets - down_two - coeffs[9:11])
    return offsets + STEP_SIZE * forces


def general_body(images, tissue_mask):
    margin = (PATCH - STRIDE) // 2
    count_y = images.shape[1] // STRIDE
    count_x = images.shape[2] // STRIDE
    padded = padded_2(images, (("gy", 1), ("gx", 2)), margin)
    left_table, right_table = tables()
    own_mask = tissue_mask.astype(jnp.float32)
    own_re, own_im = spectrum(padded[0].astype(jnp.float32), left_table, right_table)
    next_re, next_im, next_mask = shifted((own_re, own_im, own_mask), "gz", -1)
    far_re, far_im, far_mask = shifted((own_re, own_im, own_mask), "gz", -2)
    flow_one = flow_between(own_re, own_im, next_re, next_im, left_table, count_y, count_x)
    flow_two = flow_between(own_re, own_im, far_re, far_im, left_table, count_y, count_x)
    weight_one = own_mask * next_mask
    weight_two = own_mask * far_mask
    low_flow_one, low_weight_one = shifted((flow_one, weight_one), "gz", 1)
    low_flow_two, low_weight_two = shifted((flow_two, weight_two), "gz", 2)
    coeffs = jnp.concatenate(
        [
            flow_one,
            weight_one,
            flow_two,
            weight_two,
            low_flow_one,
            low_weight_one,
            low_flow_two,
            low_weight_two,
        ],
        0,
    )[:, None]
    spread = padded_2(coeffs, (("gy", 2), ("gx", 3)), RELAX)
    global_y = lax.axis_index("gy") * count_y + jnp.arange(-RELAX, count_y + RELAX, dtype=jnp.int32)
    global_x = lax.axis_index("gx") * count_x + jnp.arange(-RELAX, count_x + RELAX, dtype=jnp.int32)
    inside_y = (global_y >= 0) & (global_y < count_y * lax.axis_size("gy"))
    inside_x = (global_x >= 0) & (global_x < count_x * lax.axis_size("gx"))
    inside = (inside_y[:, None] & inside_x[None, :]).astype(jnp.float32)
    offsets = jnp.zeros((2, 1, count_y + 2 * RELAX, count_x + 2 * RELAX), jnp.float32)
    for _ in range(RELAX):
        widened = jnp.pad(offsets, ((0, 0), (0, 0), (1, 1), (1, 1)))
        offsets = mesh_step(offsets, laplacian(widened, offsets), spread) * inside[None, None]
    offsets = offsets[:, :, RELAX : RELAX + count_y, RELAX : RELAX + count_x]
    flow_fields = jnp.concatenate([flow_one, flow_two], 0)[:, None]
    return (flow_fields, offsets)


MARGIN = (PATCH - STRIDE) // 2
HALF = PATCH // 2 + 1
LANES = 128
SUBLANES = 8
ROWS_K = -(-HALF // SUBLANES) * SUBLANES
HALO = -(-MARGIN // 16) * 16
RADIUS = RELAX - 1


def split_table(table):
    high = table.astype(jnp.bfloat16)
    low = (table - high.astype(np.float64)).astype(jnp.bfloat16)
    return np.stack([high, low])


def trig(first, second):
    angle = 2.0 * np.pi / PATCH * ((first[:, None] * second[None, :]) % PATCH)
    return np.cos(angle), np.sin(angle)


def column_table():
    cosine, sine = trig(np.arange(PATCH), np.arange(HALF))
    table = np.zeros((PATCH, 2 * LANES))
    table[:, :HALF] = cosine
    table[:, LANES : LANES + HALF] = sine
    return split_table(table)


def row_table(halves, rows):
    table = np.zeros((halves, rows, 2 * ROWS_K, PATCH + HALO))
    for half in range(halves):
        halo_first = PATCH - HALO if half == 0 else 0
        position = np.concatenate([np.arange(PATCH), halo_first + np.arange(HALO)])
        cosine, sine = trig(np.arange(HALF), position)
        for row in range(rows):
            start = (half * rows + row) * STRIDE - MARGIN
            own = (np.arange(PATCH) >= start) & (np.arange(PATCH) < start + PATCH)
            offset = -PATCH if half == 0 else PATCH
            outer = halo_first + np.arange(HALO) + offset
            outer = (outer >= start) & (outer < start + PATCH)
            used = np.concatenate([own, outer])
            table[half, row, :HALF] = cosine * used
            table[half, row, ROWS_K : ROWS_K + HALF] = sine * used
    table = table.reshape(halves, rows * 2 * ROWS_K, PATCH + HALO)
    return np.stack([split_table(table[half]) for half in range(halves)])


def inverse_tables():
    cosine, sine = trig(np.arange(PATCH), np.arange(HALF))
    weight = np.full((HALF,), 2.0 / PATCH)
    weight[0] = weight[-1] = 1.0 / PATCH
    left = np.zeros((PATCH, 2 * ROWS_K))
    left[:, :HALF] = cosine * weight
    left[:, ROWS_K : ROWS_K + HALF] = -sine * weight
    right = np.zeros((2 * LANES, PATCH))
    right[:HALF] = (cosine * weight).T
    right[LANES : LANES + HALF] = -(sine * weight).T
    return split_table(left), split_table(right)


def dot(left, right):
    return jnp.dot(left, right, preferred_element_type=jnp.float32)


def halves_of(value):
    high = value.astype(jnp.bfloat16)
    return high, (value - high.astype(jnp.float32)).astype(jnp.bfloat16)


def table_first(table, value):
    high, low = halves_of(value)
    return dot(table[0], high) + dot(table[1], high) + dot(table[0], low)


def table_last(value, table):
    high, low = halves_of(value)
    return dot(high, table[0]) + dot(high, table[1]) + dot(low, table[0])


def flow_kernel(rows, columns, where_ref, own_ref, other_ref, diagonal_ref, first_ref, second_ref,
                mask_ref, column_ref, row_ref, left_ref, right_ref, out_ref, rows_ref):
    half = where_ref[0]
    odd = where_ref[1] == 1
    lane = lax.broadcasted_iota(jnp.int32, (PATCH + HALO, LANES), 1)
    wide = lax.broadcasted_iota(jnp.int32, (PATCH + HALO, PATCH), 1)
    held = []
    for image in range(2):
        tile = own_ref[0] if image == 0 else other_ref[0]
        mine = jnp.concatenate([tile, diagonal_ref[1 - image]], 0).astype(jnp.float32)
        one = first_ref[image].astype(jnp.float32)
        two = second_ref[image].astype(jnp.float32)
        before = jnp.where(odd, one, two)
        after = jnp.where(odd, two, one)
        beside = jnp.concatenate(
            [jnp.where(lane < LANES // 2, after, before), before[:, : PATCH - LANES]], 1
        )
        held.append((mine, beside))
    sign = jnp.where(half == 0, 1.0, -1.0).astype(jnp.float32)
    window_rows = 2 * ROWS_K
    count = rows * columns
    for column in range(columns):
        start = column * STRIDE - MARGIN
        inside = wide < start + PATCH if start < 0 else wide >= start
        spectra = []
        for mine, beside in held:
            pixels = jnp.where(inside, mine, beside).astype(jnp.bfloat16)
            partial = dot(pixels, column_ref[0]) + dot(pixels, column_ref[1])
            high, low = halves_of(partial)
            spectra.append(
                dot(row_ref[half, 0], high) + dot(row_ref[half, 1], high) + dot(row_ref[half, 0], low)
            )
        for row in range(rows):
            parts = []
            for spectrum_of in spectra:
                top = spectrum_of[row * window_rows : row * window_rows + ROWS_K]
                low = spectrum_of[row * window_rows + ROWS_K : (row + 1) * window_rows]
                parts.append((top[:, :LANES], top[:, LANES:], low[:, :LANES], low[:, LANES:]))
            (acc, acs, asc, ass), (bcc, bcs, bsc, bss) = parts
            even = acc * bcc + asc * bsc + acs * bcs + ass * bss
            by_row = sign * (asc * bcc - acc * bsc + ass * bcs - acs * bss)
            by_column = sign * (acs * bcc - acc * bcs + ass * bsc - asc * bss)
            both = acc * bss + ass * bcc - asc * bcs - acs * bsc
            cross = jnp.concatenate(
                [jnp.concatenate([even, by_column], 1), jnp.concatenate([by_row, both], 1)], 0
            )
            correl = table_last(table_first(left_ref, cross), right_ref)
            squared = correl * correl
            weights = squared * squared
            total = weights[:SUBLANES]
            based = jnp.zeros_like(total)
            for group in range(1, PATCH // SUBLANES):
                piece = weights[group * SUBLANES : (group + 1) * SUBLANES]
                base = group * SUBLANES
                base = base - PATCH if base >= PATCH // 2 else base
                total = total + piece
                based = based + piece * float(base)
            step = lax.broadcasted_iota(jnp.int32, (SUBLANES, PATCH), 0).astype(jnp.float32)
            based = based + step * total
            patch = row * columns + column
            rows_ref[0, pl.ds(patch, 1)] = jnp.sum(total, 0, keepdims=True)
            rows_ref[1, pl.ds(patch, 1)] = jnp.sum(based, 0, keepdims=True)
    totals = rows_ref[0]
    shift = lax.broadcasted_iota(jnp.int32, (count, PATCH), 1)
    shift = jnp.where(shift >= PATCH // 2, shift - PATCH, shift).astype(jnp.float32)
    below = jnp.sum(totals, 1, keepdims=True) + EPSILON
    flow_y = jnp.sum(rows_ref[1], 1, keepdims=True) / below
    flow_x = jnp.sum(totals * shift, 1, keepdims=True) / below
    at = lax.broadcasted_iota(jnp.int32, (count, LANES), 1)
    patch = lax.broadcasted_iota(jnp.int32, (count, LANES), 0)
    line = jnp.where(at == patch, flow_y, 0.0) + jnp.where(at == patch + count, flow_x, 0.0)
    line = jnp.sum(line, 0, keepdims=True)
    lanes = lax.broadcasted_iota(jnp.int32, (1, LANES), 1)
    mask = mask_ref[0].astype(jnp.float32)
    for row in range(mask.shape[0]):
        for column in range(columns):
            spot = 2 * count + row * columns + column
            line = jnp.where(lanes == spot, mask[row : row + 1, column : column + 1], line)
    out_ref[...] = jnp.broadcast_to(line, out_ref.shape)


def relax_kernel(rows, columns, grid_shape, where_ref, got_ref, flow_ref, offsets_ref):
    _, size_y, size_x = grid_shape
    half, at_y, at_x = where_ref[0], where_ref[2], where_ref[3]
    count = rows * columns
    tile_rows = 2 * rows
    width = columns + 2 * RADIUS
    height = tile_rows + 2 * RADIUS
    devices = got_ref.shape[0]
    lane = lax.broadcasted_iota(jnp.int32, (1, LANES), 1).astype(jnp.float32)
    line = jnp.floor((lane + 0.5) * (1.0 / width))
    across = lane - line * width
    node_y = line.astype(jnp.int32) - RADIUS + at_y * tile_rows
    node_x = across.astype(jnp.int32) - RADIUS + at_x * columns
    inside = (node_y >= 0) & (node_y < tile_rows * size_y) & (node_x >= 0)
    inside = inside & (node_x < columns * size_x) & (line < height)

    def parts(value, size):
        whole = jnp.floor((value.astype(jnp.float32) + 0.5) * (1.0 / size)).astype(jnp.int32)
        return whole, value - whole * size

    tile_y, in_y = parts(node_y, tile_rows)
    tile_x, in_x = parts(node_x, columns)
    side, in_half = parts(in_y, rows)
    tile = tile_y * size_x + tile_x
    per_section = size_y * size_x
    flow_key = jnp.where(inside, (side * per_section + tile) * count + in_half * columns + in_x, -1)
    mask_key = jnp.where(inside, tile * (2 * count) + in_y * columns + in_x, -1)
    got = got_ref[...]
    source = lax.broadcasted_iota(jnp.int32, (devices, LANES), 0)
    sums = [jnp.zeros((devices, LANES), jnp.float32) for _ in range(2)]
    for node in range(count):
        hit = source * count + node == flow_key
        for axis in range(2):
            spot = axis * count + node
            sums[axis] = sums[axis] + jnp.where(hit, got[:, spot : spot + 1], 0.0)
    masks = [jnp.zeros((per_section, LANES), jnp.float32) for _ in range(2)]
    source = source[:per_section]
    for node in range(2 * count):
        hit = source * (2 * count) + node == mask_key
        spot = 2 * count + node
        for section in range(2):
            piece = got[section * per_section : (section + 1) * per_section, spot : spot + 1]
            masks[section] = masks[section] + jnp.where(hit, piece, 0.0)
    flows = jnp.concatenate([jnp.sum(total, 0, keepdims=True) for total in sums], 0)
    weight = jnp.sum(masks[0], 0, keepdims=True) * jnp.sum(masks[1], 0, keepdims=True)
    kept = inside.astype(jnp.float32)
    upper = jnp.zeros((2, LANES), jnp.float32)
    lower = jnp.zeros((2, LANES), jnp.float32)

    def laplacian_of(value):
        left = jnp.where(across < 0.5, 0.0, pltpu.roll(value, 1, 1))
        right = jnp.where(across > width - 1.5, 0.0, pltpu.roll(value, LANES - 1, 1))
        return pltpu.roll(value, width, 1) + pltpu.roll(value, LANES - width, 1) + left + right - 4.0 * value

    for _ in range(RELAX):
        pull = weight * (upper - lower - flows)
        lower, upper = (
            (lower + STEP_SIZE * (STIFFNESS * laplacian_of(lower) + pull)) * kept,
            (upper + STEP_SIZE * (STIFFNESS * laplacian_of(upper) - pull)) * kept,
        )
    first = half == 0
    result = jnp.where(first, lower, upper)
    flows = jnp.where(first, flows, 0.0)
    flow_ref[...] = jnp.zeros_like(flow_ref)
    for row in range(tile_rows):
        start = (RADIUS + row) * width + RADIUS
        for axis in range(2):
            offsets_ref[axis, 0, pl.ds(row, 1)] = result[axis : axis + 1, start : start + columns]
            flow_ref[axis, 0, pl.ds(row, 1)] = flows[axis : axis + 1, start : start + columns]


def vmem(count):
    return [pl.BlockSpec(memory_space=pltpu.VMEM)] * count


def pair_body(images, tissue_mask):
    sections, size_y, size_x = (lax.axis_size(name) for name in ("gz", "gy", "gx"))
    count_y = images.shape[1] // STRIDE
    count_x = images.shape[2] // STRIDE
    rows = count_y // 2
    half, at_y, at_x = (lax.axis_index(name) for name in ("gz", "gy", "gx"))
    odd = at_x % 2
    where = jnp.stack([half, odd, at_y, at_x]).astype(jnp.int32)
    other = lax.ppermute(images, "gz", [(0, 1), (1, 0)])
    both = jnp.concatenate([images, other], 0)
    edge = jnp.where(half == 1, both[:, PATCH - HALO :], both[:, :HALO])
    diagonal = []
    for tile in range(1, size_y):
        diagonal += [(size_y + tile - 1, tile), (tile, size_y + tile - 1)]
    beyond = lax.ppermute(edge, ("gz", "gy"), diagonal)
    tall = jnp.concatenate([both, beyond[::-1]], 1)
    low_side = tall[:, :, :LANES]
    high_side = jnp.concatenate([tall[:, :, LANES:], tall[:, :, PATCH - LANES : LANES]], 2)
    is_odd = odd == 1
    swaps = [
        [pair for left in range(offset, size_x - 1, 2) for pair in ((left, left + 1), (left + 1, left))]
        for offset in range(2)
    ]
    first = lax.ppermute(jnp.where(is_odd, low_side, high_side), "gx", swaps[0])
    second = lax.ppermute(jnp.where(is_odd, high_side, low_side), "gx", swaps[1])
    devices = sections * size_y * size_x
    left, right = inverse_tables()
    scalars = pl.BlockSpec(memory_space=pltpu.SMEM)
    lines = pl.pallas_call(
        functools.partial(flow_kernel, rows, count_x),
        out_shape=jax.ShapeDtypeStruct((devices, LANES), jnp.float32),
        in_specs=[scalars] + vmem(10),
        out_specs=vmem(1)[0],
        scratch_shapes=[pltpu.VMEM((2, rows * count_x, PATCH), jnp.float32)],
        compiler_params=pltpu.CompilerParams(vmem_limit_bytes=24 * 2**20),
        name="flows",
    )(
        where,
        images,
        other,
        beyond,
        first,
        second,
        tissue_mask,
        jnp.asarray(column_table()),
        jnp.asarray(row_table(2, rows)),
        jnp.asarray(left),
        jnp.asarray(right),
    )
    got = lax.all_to_all(lines, ("gz", "gy", "gx"), 0, 0, tiled=True)
    return pl.pallas_call(
        functools.partial(relax_kernel, rows, count_x, (sections, size_y, size_x)),
        out_shape=(
            jax.ShapeDtypeStruct((4, 1, count_y, count_x), jnp.float32),
            jax.ShapeDtypeStruct((2, 1, count_y, count_x), jnp.float32),
        ),
        in_specs=[scalars] + vmem(1),
        out_specs=tuple(vmem(2)),
        compiler_params=pltpu.CompilerParams(vmem_limit_bytes=4 * 2**20),
        name="relax",
    )(where, got)


def body(images, tissue_mask):
    paired = lax.axis_size("gz") == 2 and images.shape == (1, PATCH, PATCH)
    return (pair_body if paired else general_body)(images, tissue_mask)


def solution(mesh):
    placed = (P("gz", "gy", "gx"), P("gz", "gy", "gx"))
    return jax.shard_map(
        body,
        mesh=mesh,
        in_specs=placed,
        out_specs=(P(None, "gz", "gy", "gx"), P(None, "gz", "gy", "gx")),
        check_vma=False,
    )
```

```python
import functools
import math

import jax
import jax.numpy as jnp
import numpy as np
from jax import lax
from jax.experimental import pallas as pl
from jax.experimental.pallas import tpu as pltpu
from jax.sharding import PartitionSpec as P

PATCH = 160
STRIDE = 40
RELAX = 4


EPSILON = 1e-06
STIFFNESS = 0.5
STEP_SIZE = 0.2


def shifted(value, axis, steps):
    count = lax.axis_size(axis)
    initial, last = (max(0, -steps), min(count, count - steps))
    return lax.ppermute(value, axis, [(source, source + steps) for source in range(initial, last)])


def padded_2(x, sides, width):
    for axis, dim in sides:
        size, length = (lax.axis_size(axis), x.shape[dim])
        up = [(i, (i + 1) % size) for i in range(size - 1)]
        down = [(j, i) for i, j in up]
        last = lax.slice_in_dim(x, length - width, length, axis=dim)
        initial = lax.slice_in_dim(x, 0, width, axis=dim)
        before = lax.ppermute(last, axis, up)
        after = lax.ppermute(initial, axis, down)
        x = jnp.concatenate([before, x, after], axis=dim)
    return x


def windows(section):
    repeats = PATCH // STRIDE
    count_y = section.shape[0] // STRIDE - repeats + 1
    count_x = section.shape[1] // STRIDE - repeats + 1
    blocks = section.reshape(section.shape[0] // STRIDE, STRIDE, section.shape[1] // STRIDE, STRIDE)
    pieces = []
    for first in range(repeats):
        row_pieces = [
            blocks[first : first + count_y, :, second : second + count_x, :]
            for second in range(repeats)
        ]
        pieces.append(jnp.stack(row_pieces, 0))
    stacked = jnp.stack(pieces, 0)
    stacked = jnp.transpose(stacked, (2, 4, 0, 3, 1, 5))
    return stacked.reshape(count_y * count_x, PATCH, PATCH)


def tables():
    indices = jnp.arange(PATCH, dtype=jnp.int32)
    phases = indices[:, None] * indices[None, :] % PATCH
    angles = phases.astype(jnp.float32) * (2.0 * math.pi / PATCH)
    cosine_table = jnp.cos(angles)
    sine_table = jnp.sin(angles)
    left_table = jnp.concatenate([cosine_table, sine_table], 0)
    right_table = jnp.concatenate([cosine_table, sine_table], 1)
    return (left_table, right_table)


def spectrum(section, left_table, right_table):
    patches = windows(section)
    halfway = jnp.einsum("pnm,mk->pnk", patches, right_table, precision=lax.Precision.HIGHEST)
    products = jnp.einsum("kn,pnm->pkm", left_table, halfway, precision=lax.Precision.HIGHEST)
    cos_a = products[:, :PATCH, :PATCH]
    cos_b = products[:, :PATCH, PATCH:]
    sin_a = products[:, PATCH:, :PATCH]
    sin_b = products[:, PATCH:, PATCH:]
    return (cos_a - sin_b, -(cos_b + sin_a))


def flow_between(own_re, own_im, next_re, next_im, left_table, count_y, count_x):
    cross_re = next_re * own_re + next_im * own_im
    cross_im = next_im * own_re - next_re * own_im
    stacked = jnp.concatenate([cross_re, cross_im], 2)
    products = jnp.einsum("kn,pnm->pkm", left_table, stacked, precision=lax.Precision.HIGHEST)
    mixed_re = products[:, :PATCH, :PATCH] - products[:, PATCH:, PATCH:]
    mixed_im = products[:, :PATCH, PATCH:] + products[:, PATCH:, :PATCH]
    joined = jnp.concatenate([mixed_re, -mixed_im], 2)
    correl = jnp.einsum("pnm,mk->pnk", joined, left_table, precision=lax.Precision.HIGHEST) / (
        PATCH * PATCH
    )
    squared = correl * correl
    weights = squared * squared
    totals = jnp.sum(weights, axis=(1, 2)) + EPSILON
    shifts = ((jnp.arange(PATCH, dtype=jnp.int32) + PATCH // 2) % PATCH - PATCH // 2).astype(
        jnp.float32
    )
    flow_y = jnp.sum(weights * shifts[None, :, None], axis=(1, 2)) / totals
    flow_x = jnp.sum(weights * shifts[None, None, :], axis=(1, 2)) / totals
    return jnp.stack([flow_y, flow_x], 0).reshape(2, count_y, count_x)


def laplacian(widened, offsets):
    return (
        widened[:, :, :-2, 1:-1]
        + widened[:, :, 2:, 1:-1]
        + widened[:, :, 1:-1, :-2]
        + widened[:, :, 1:-1, 2:]
        - 4.0 * offsets
    )


def remote_neighbours(offsets):
    up_one = shifted(offsets, "gz", -1)
    up_two = shifted(offsets, "gz", -2)
    down_one = shifted(offsets, "gz", 1)
    down_two = shifted(offsets, "gz", 2)
    return (up_one, up_two, down_one, down_two)


def mesh_step(offsets, laplace, coeffs):
    up_one, up_two, down_one, down_two = remote_neighbours(offsets)
    forces = STIFFNESS * laplace
    forces = forces + coeffs[2:3] * (up_one - offsets - coeffs[0:2])
    forces = forces + coeffs[5:6] * (up_two - offsets - coeffs[3:5])
    forces = forces - coeffs[8:9] * (offsets - down_one - coeffs[6:8])
    forces = forces - coeffs[11:12] * (offsets - down_two - coeffs[9:11])
    return offsets + STEP_SIZE * forces


def general_body(images, tissue_mask):
    margin = (PATCH - STRIDE) // 2
    count_y = images.shape[1] // STRIDE
    count_x = images.shape[2] // STRIDE
    padded = padded_2(images, (("gy", 1), ("gx", 2)), margin)
    left_table, right_table = tables()
    own_mask = tissue_mask.astype(jnp.float32)
    own_re, own_im = spectrum(padded[0].astype(jnp.float32), left_table, right_table)
    next_re, next_im, next_mask = shifted((own_re, own_im, own_mask), "gz", -1)
    far_re, far_im, far_mask = shifted((own_re, own_im, own_mask), "gz", -2)
    flow_one = flow_between(own_re, own_im, next_re, next_im, left_table, count_y, count_x)
    flow_two = flow_between(own_re, own_im, far_re, far_im, left_table, count_y, count_x)
    weight_one = own_mask * next_mask
    weight_two = own_mask * far_mask
    low_flow_one, low_weight_one = shifted((flow_one, weight_one), "gz", 1)
    low_flow_two, low_weight_two = shifted((flow_two, weight_two), "gz", 2)
    coeffs = jnp.concatenate(
        [
            flow_one,
            weight_one,
            flow_two,
            weight_two,
            low_flow_one,
            low_weight_one,
            low_flow_two,
            low_weight_two,
        ],
        0,
    )[:, None]
    spread = padded_2(coeffs, (("gy", 2), ("gx", 3)), RELAX)
    global_y = lax.axis_index("gy") * count_y + jnp.arange(-RELAX, count_y + RELAX, dtype=jnp.int32)
    global_x = lax.axis_index("gx") * count_x + jnp.arange(-RELAX, count_x + RELAX, dtype=jnp.int32)
    inside_y = (global_y >= 0) & (global_y < count_y * lax.axis_size("gy"))
    inside_x = (global_x >= 0) & (global_x < count_x * lax.axis_size("gx"))
    inside = (inside_y[:, None] & inside_x[None, :]).astype(jnp.float32)
    offsets = jnp.zeros((2, 1, count_y + 2 * RELAX, count_x + 2 * RELAX), jnp.float32)
    for _ in range(RELAX):
        widened = jnp.pad(offsets, ((0, 0), (0, 0), (1, 1), (1, 1)))
        offsets = mesh_step(offsets, laplacian(widened, offsets), spread) * inside[None, None]
    offsets = offsets[:, :, RELAX : RELAX + count_y, RELAX : RELAX + count_x]
    flow_fields = jnp.concatenate([flow_one, flow_two], 0)[:, None]
    return (flow_fields, offsets)


MARGIN = (PATCH - STRIDE) // 2
HALF = PATCH // 2 + 1
LANES = 128
SUBLANES = 8
ROWS_K = -(-HALF // SUBLANES) * SUBLANES
HALO = -(-MARGIN // 16) * 16
RADIUS = RELAX - 1


def split_table(table):
    high = table.astype(jnp.bfloat16)
    low = (table - high.astype(np.float64)).astype(jnp.bfloat16)
    return np.stack([high, low])


def trig(first, second):
    angle = 2.0 * np.pi / PATCH * ((first[:, None] * second[None, :]) % PATCH)
    return np.cos(angle), np.sin(angle)


def column_table():
    cosine, sine = trig(np.arange(PATCH), np.arange(HALF))
    table = np.zeros((PATCH, 2 * LANES))
    table[:, :HALF] = cosine
    table[:, LANES : LANES + HALF] = sine
    return split_table(table)


def row_table(halves, rows):
    table = np.zeros((halves, rows, 2 * ROWS_K, PATCH + HALO))
    for half in range(halves):
        halo_first = PATCH - HALO if half == 0 else 0
        position = np.concatenate([np.arange(PATCH), halo_first + np.arange(HALO)])
        cosine, sine = trig(np.arange(HALF), position)
        for row in range(rows):
            start = (half * rows + row) * STRIDE - MARGIN
            own = (np.arange(PATCH) >= start) & (np.arange(PATCH) < start + PATCH)
            offset = -PATCH if half == 0 else PATCH
            outer = halo_first + np.arange(HALO) + offset
            outer = (outer >= start) & (outer < start + PATCH)
            used = np.concatenate([own, outer])
            table[half, row, :HALF] = cosine * used
            table[half, row, ROWS_K : ROWS_K + HALF] = sine * used
    table = table.reshape(halves, rows * 2 * ROWS_K, PATCH + HALO)
    return np.stack([split_table(table[half]) for half in range(halves)])


def inverse_tables():
    cosine, sine = trig(np.arange(PATCH), np.arange(HALF))
    weight = np.full((HALF,), 2.0 / PATCH)
    weight[0] = weight[-1] = 1.0 / PATCH
    left = np.zeros((PATCH, 2 * ROWS_K))
    left[:, :HALF] = cosine * weight
    left[:, ROWS_K : ROWS_K + HALF] = -sine * weight
    right = np.zeros((2 * LANES, PATCH))
    right[:HALF] = (cosine * weight).T
    right[LANES : LANES + HALF] = -(sine * weight).T
    return split_table(left), split_table(right)


def dot(left, right):
    return jnp.dot(left, right, preferred_element_type=jnp.float32)


def halves_of(value):
    high = value.astype(jnp.bfloat16)
    return high, (value - high.astype(jnp.float32)).astype(jnp.bfloat16)


def table_first(table, value):
    high, low = halves_of(value)
    return dot(table[0], high) + dot(table[1], high) + dot(table[0], low)


def table_last(value, table):
    high, low = halves_of(value)
    return dot(high, table[0]) + dot(high, table[1]) + dot(low, table[0])


def flow_kernel(rows, columns, late, where_ref, own_ref, other_ref, diagonal_ref, beside_ref,
                before_ref, column_ref, row_ref, left_ref, right_ref, out_ref, rows_ref):
    half = where_ref[0]
    side = where_ref[1] if late else 1 - where_ref[1]
    lane = lax.broadcasted_iota(jnp.int32, (PATCH + HALO, PATCH), 1)
    group = columns // 2
    base = side * group
    held = []
    for image in range(2):
        tile = own_ref[0] if image == 0 else other_ref[0]
        mine = jnp.concatenate([tile, diagonal_ref[1 - image]], 0).astype(jnp.float32)
        halo = beside_ref[image].astype(jnp.float32)
        halo = jnp.concatenate([halo, halo[:, : PATCH - LANES]], 1)
        held.append((mine, halo))
    sign = jnp.where(half == 0, 1.0, -1.0).astype(jnp.float32)
    window_rows = 2 * ROWS_K
    count = rows * group
    for column in range(group):
        start = (base + column) * STRIDE - MARGIN
        low_lane = jnp.where(side == 0, 0, start)
        high_lane = jnp.where(side == 0, start + PATCH, PATCH)
        inside = (lane >= low_lane) & (lane < high_lane)
        spectra = []
        for mine, halo in held:
            pixels = jnp.where(inside, mine, halo).astype(jnp.bfloat16)
            partial = dot(pixels, column_ref[0]) + dot(pixels, column_ref[1])
            high, low = halves_of(partial)
            spectra.append(
                dot(row_ref[half, 0], high) + dot(row_ref[half, 1], high) + dot(row_ref[half, 0], low)
            )
        for row in range(rows):
            parts = []
            for spectrum_of in spectra:
                top = spectrum_of[row * window_rows : row * window_rows + ROWS_K]
                low = spectrum_of[row * window_rows + ROWS_K : (row + 1) * window_rows]
                parts.append((top[:, :LANES], top[:, LANES:], low[:, :LANES], low[:, LANES:]))
            (acc, acs, asc, ass), (bcc, bcs, bsc, bss) = parts
            even = acc * bcc + asc * bsc + acs * bcs + ass * bss
            by_row = sign * (asc * bcc - acc * bsc + ass * bcs - acs * bss)
            by_column = sign * (acs * bcc - acc * bcs + ass * bsc - asc * bss)
            both = acc * bss + ass * bcc - asc * bcs - acs * bsc
            cross = jnp.concatenate(
                [jnp.concatenate([even, by_column], 1), jnp.concatenate([by_row, both], 1)], 0
            )
            correl = table_last(table_first(left_ref, cross), right_ref)
            squared = correl * correl
            weights = squared * squared
            total = weights[:SUBLANES]
            based = jnp.zeros_like(total)
            for piece_at in range(1, PATCH // SUBLANES):
                piece = weights[piece_at * SUBLANES : (piece_at + 1) * SUBLANES]
                shift = piece_at * SUBLANES
                shift = shift - PATCH if shift >= PATCH // 2 else shift
                total = total + piece
                based = based + piece * float(shift)
            step = lax.broadcasted_iota(jnp.int32, (SUBLANES, PATCH), 0).astype(jnp.float32)
            based = based + step * total
            patch = row * group + column
            rows_ref[0, pl.ds(patch, 1)] = jnp.sum(total, 0, keepdims=True)
            rows_ref[1, pl.ds(patch, 1)] = jnp.sum(based, 0, keepdims=True)
    totals = rows_ref[0]
    shift = lax.broadcasted_iota(jnp.int32, (count, PATCH), 1)
    shift = jnp.where(shift >= PATCH // 2, shift - PATCH, shift).astype(jnp.float32)
    below = jnp.sum(totals, 1, keepdims=True) + EPSILON
    flow_y = jnp.sum(rows_ref[1], 1, keepdims=True) / below
    flow_x = jnp.sum(totals * shift, 1, keepdims=True) / below
    at = lax.broadcasted_iota(jnp.int32, (count, LANES), 1)
    patch = lax.broadcasted_iota(jnp.int32, (count, LANES), 0)
    spot = patch + group * (patch >= group).astype(jnp.int32) + base
    line = jnp.where(at == spot, flow_y, 0.0) + jnp.where(at == spot + 2 * count, flow_x, 0.0)
    line = jnp.sum(line, 0, keepdims=True)
    if late:
        line = line + before_ref[...]
    else:
        lanes = lax.broadcasted_iota(jnp.int32, (1, LANES), 1)
        mask = before_ref[0].astype(jnp.float32)
        for row in range(mask.shape[0]):
            for column in range(columns):
                spot = 4 * count + row * columns + column
                line = jnp.where(lanes == spot, mask[row : row + 1, column : column + 1], line)
    out_ref[...] = jnp.broadcast_to(line, out_ref.shape)


def relax_kernel(rows, columns, grid_shape, where_ref, got_ref, flow_ref, offsets_ref):
    _, size_y, size_x = grid_shape
    half, at_y, at_x = where_ref[0], where_ref[2], where_ref[3]
    count = rows * columns
    tile_rows = 2 * rows
    width = columns + 2 * RADIUS
    height = tile_rows + 2 * RADIUS
    devices = got_ref.shape[0]
    lane = lax.broadcasted_iota(jnp.int32, (1, LANES), 1).astype(jnp.float32)
    line = jnp.floor((lane + 0.5) * (1.0 / width))
    across = lane - line * width
    node_y = line.astype(jnp.int32) - RADIUS + at_y * tile_rows
    node_x = across.astype(jnp.int32) - RADIUS + at_x * columns
    inside = (node_y >= 0) & (node_y < tile_rows * size_y) & (node_x >= 0)
    inside = inside & (node_x < columns * size_x) & (line < height)

    def parts(value, size):
        whole = jnp.floor((value.astype(jnp.float32) + 0.5) * (1.0 / size)).astype(jnp.int32)
        return whole, value - whole * size

    tile_y, in_y = parts(node_y, tile_rows)
    tile_x, in_x = parts(node_x, columns)
    side, in_half = parts(in_y, rows)
    tile = tile_y * size_x + tile_x
    per_section = size_y * size_x
    flow_key = jnp.where(inside, (side * per_section + tile) * count + in_half * columns + in_x, -1)
    mask_key = jnp.where(inside, tile * (2 * count) + in_y * columns + in_x, -1)
    got = got_ref[...]
    source = lax.broadcasted_iota(jnp.int32, (devices, LANES), 0)
    sums = [jnp.zeros((devices, LANES), jnp.float32) for _ in range(2)]
    for node in range(count):
        hit = source * count + node == flow_key
        for axis in range(2):
            spot = axis * count + node
            sums[axis] = sums[axis] + jnp.where(hit, got[:, spot : spot + 1], 0.0)
    masks = [jnp.zeros((per_section, LANES), jnp.float32) for _ in range(2)]
    source = source[:per_section]
    for node in range(2 * count):
        hit = source * (2 * count) + node == mask_key
        spot = 2 * count + node
        for section in range(2):
            piece = got[section * per_section : (section + 1) * per_section, spot : spot + 1]
            masks[section] = masks[section] + jnp.where(hit, piece, 0.0)
    flows = jnp.concatenate([jnp.sum(total, 0, keepdims=True) for total in sums], 0)
    weight = jnp.sum(masks[0], 0, keepdims=True) * jnp.sum(masks[1], 0, keepdims=True)
    kept = inside.astype(jnp.float32)
    upper = jnp.zeros((2, LANES), jnp.float32)
    lower = jnp.zeros((2, LANES), jnp.float32)

    def laplacian_of(value):
        left = jnp.where(across < 0.5, 0.0, pltpu.roll(value, 1, 1))
        right = jnp.where(across > width - 1.5, 0.0, pltpu.roll(value, LANES - 1, 1))
        return pltpu.roll(value, width, 1) + pltpu.roll(value, LANES - width, 1) + left + right - 4.0 * value

    for _ in range(RELAX):
        pull = weight * (upper - lower - flows)
        lower, upper = (
            (lower + STEP_SIZE * (STIFFNESS * laplacian_of(lower) + pull)) * kept,
            (upper + STEP_SIZE * (STIFFNESS * laplacian_of(upper) - pull)) * kept,
        )
    first = half == 0
    result = jnp.where(first, lower, upper)
    flows = jnp.where(first, flows, 0.0)
    flow_ref[...] = jnp.zeros_like(flow_ref)
    for row in range(tile_rows):
        start = (RADIUS + row) * width + RADIUS
        for axis in range(2):
            offsets_ref[axis, 0, pl.ds(row, 1)] = result[axis : axis + 1, start : start + columns]
            flow_ref[axis, 0, pl.ds(row, 1)] = flows[axis : axis + 1, start : start + columns]


def vmem(count):
    return [pl.BlockSpec(memory_space=pltpu.VMEM)] * count


def pair_body(images, tissue_mask):
    sections, size_y, size_x = (lax.axis_size(name) for name in ("gz", "gy", "gx"))
    count_y = images.shape[1] // STRIDE
    count_x = images.shape[2] // STRIDE
    rows = count_y // 2
    half, at_y, at_x = (lax.axis_index(name) for name in ("gz", "gy", "gx"))
    odd = at_x % 2
    where = jnp.stack([half, odd, at_y, at_x]).astype(jnp.int32)
    other = lax.ppermute(images, "gz", [(0, 1), (1, 0)])
    both = jnp.concatenate([images, other], 0)
    edge = jnp.where(half == 1, both[:, PATCH - HALO :], both[:, :HALO])
    diagonal = []
    for tile in range(1, size_y):
        diagonal += [(size_y + tile - 1, tile), (tile, size_y + tile - 1)]
    beyond = lax.ppermute(edge, ("gz", "gy"), diagonal)
    tall = jnp.concatenate([both, beyond[::-1]], 1)
    low_side = tall[:, :, :LANES]
    high_side = jnp.concatenate([tall[:, :, LANES:], tall[:, :, PATCH - LANES : LANES]], 2)
    is_odd = odd == 1
    swaps = [
        [pair for left in range(offset, size_x - 1, 2) for pair in ((left, left + 1), (left + 1, left))]
        for offset in range(2)
    ]
    first = lax.ppermute(jnp.where(is_odd, low_side, high_side), "gx", swaps[0])
    second = lax.ppermute(jnp.where(is_odd, high_side, low_side), "gx", swaps[1])
    devices = sections * size_y * size_x
    left, right = inverse_tables()
    scalars = pl.BlockSpec(memory_space=pltpu.SMEM)
    tables = [jnp.asarray(column_table()), jnp.asarray(row_table(2, rows)), jnp.asarray(left), jnp.asarray(right)]

    def flows(late, beside, before, lines):
        patches = rows * count_x // 2
        return pl.pallas_call(
            functools.partial(flow_kernel, rows, count_x, late),
            out_shape=jax.ShapeDtypeStruct((lines, LANES), jnp.float32),
            in_specs=[scalars] + vmem(9),
            out_specs=vmem(1)[0],
            scratch_shapes=[pltpu.VMEM((2, patches, PATCH), jnp.float32)],
            compiler_params=pltpu.CompilerParams(vmem_limit_bytes=16 * 2**20),
            cost_estimate=pl.CostEstimate(
                flops=patches * 2 * 2400 * 256 * 256, bytes_accessed=2**21, transcendentals=0
            ),
            name="flows",
        )(where, images, other, beyond, beside, before, *tables)

    lines = flows(True, second, flows(False, first, tissue_mask, 1), devices)
    got = lax.all_to_all(lines, ("gz", "gy", "gx"), 0, 0, tiled=True)
    return pl.pallas_call(
        functools.partial(relax_kernel, rows, count_x, (sections, size_y, size_x)),
        out_shape=(
            jax.ShapeDtypeStruct((4, 1, count_y, count_x), jnp.float32),
            jax.ShapeDtypeStruct((2, 1, count_y, count_x), jnp.float32),
        ),
        in_specs=[scalars] + vmem(1),
        out_specs=tuple(vmem(2)),
        compiler_params=pltpu.CompilerParams(vmem_limit_bytes=4 * 2**20),
        name="relax",
    )(where, got)


def body(images, tissue_mask):
    paired = lax.axis_size("gz") == 2 and images.shape == (1, PATCH, PATCH)
    return (pair_body if paired else general_body)(images, tissue_mask)


def solution(mesh):
    placed = (P("gz", "gy", "gx"), P("gz", "gy", "gx"))
    return jax.shard_map(
        body,
        mesh=mesh,
        in_specs=placed,
        out_specs=(P(None, "gz", "gy", "gx"), P(None, "gz", "gy", "gx")),
        check_vma=False,
    )
```

```python
import functools
import math

import jax
import jax.numpy as jnp
import numpy as np
from jax import lax
from jax.experimental import pallas as pl
from jax.experimental.pallas import tpu as pltpu
from jax.sharding import PartitionSpec as P

PATCH = 160
STRIDE = 40
RELAX = 4


EPSILON = 1e-06
STIFFNESS = 0.5
STEP_SIZE = 0.2


def shifted(value, axis, steps):
    count = lax.axis_size(axis)
    initial, last = (max(0, -steps), min(count, count - steps))
    return lax.ppermute(value, axis, [(source, source + steps) for source in range(initial, last)])


def padded_2(x, sides, width):
    for axis, dim in sides:
        size, length = (lax.axis_size(axis), x.shape[dim])
        up = [(i, (i + 1) % size) for i in range(size - 1)]
        down = [(j, i) for i, j in up]
        last = lax.slice_in_dim(x, length - width, length, axis=dim)
        initial = lax.slice_in_dim(x, 0, width, axis=dim)
        before = lax.ppermute(last, axis, up)
        after = lax.ppermute(initial, axis, down)
        x = jnp.concatenate([before, x, after], axis=dim)
    return x


def windows(section):
    repeats = PATCH // STRIDE
    count_y = section.shape[0] // STRIDE - repeats + 1
    count_x = section.shape[1] // STRIDE - repeats + 1
    blocks = section.reshape(section.shape[0] // STRIDE, STRIDE, section.shape[1] // STRIDE, STRIDE)
    pieces = []
    for first in range(repeats):
        row_pieces = [
            blocks[first : first + count_y, :, second : second + count_x, :]
            for second in range(repeats)
        ]
        pieces.append(jnp.stack(row_pieces, 0))
    stacked = jnp.stack(pieces, 0)
    stacked = jnp.transpose(stacked, (2, 4, 0, 3, 1, 5))
    return stacked.reshape(count_y * count_x, PATCH, PATCH)


def tables():
    indices = jnp.arange(PATCH, dtype=jnp.int32)
    phases = indices[:, None] * indices[None, :] % PATCH
    angles = phases.astype(jnp.float32) * (2.0 * math.pi / PATCH)
    cosine_table = jnp.cos(angles)
    sine_table = jnp.sin(angles)
    left_table = jnp.concatenate([cosine_table, sine_table], 0)
    right_table = jnp.concatenate([cosine_table, sine_table], 1)
    return (left_table, right_table)


def spectrum(section, left_table, right_table):
    patches = windows(section)
    halfway = jnp.einsum("pnm,mk->pnk", patches, right_table, precision=lax.Precision.HIGHEST)
    products = jnp.einsum("kn,pnm->pkm", left_table, halfway, precision=lax.Precision.HIGHEST)
    cos_a = products[:, :PATCH, :PATCH]
    cos_b = products[:, :PATCH, PATCH:]
    sin_a = products[:, PATCH:, :PATCH]
    sin_b = products[:, PATCH:, PATCH:]
    return (cos_a - sin_b, -(cos_b + sin_a))


def flow_between(own_re, own_im, next_re, next_im, left_table, count_y, count_x):
    cross_re = next_re * own_re + next_im * own_im
    cross_im = next_im * own_re - next_re * own_im
    stacked = jnp.concatenate([cross_re, cross_im], 2)
    products = jnp.einsum("kn,pnm->pkm", left_table, stacked, precision=lax.Precision.HIGHEST)
    mixed_re = products[:, :PATCH, :PATCH] - products[:, PATCH:, PATCH:]
    mixed_im = products[:, :PATCH, PATCH:] + products[:, PATCH:, :PATCH]
    joined = jnp.concatenate([mixed_re, -mixed_im], 2)
    correl = jnp.einsum("pnm,mk->pnk", joined, left_table, precision=lax.Precision.HIGHEST) / (
        PATCH * PATCH
    )
    squared = correl * correl
    weights = squared * squared
    totals = jnp.sum(weights, axis=(1, 2)) + EPSILON
    shifts = ((jnp.arange(PATCH, dtype=jnp.int32) + PATCH // 2) % PATCH - PATCH // 2).astype(
        jnp.float32
    )
    flow_y = jnp.sum(weights * shifts[None, :, None], axis=(1, 2)) / totals
    flow_x = jnp.sum(weights * shifts[None, None, :], axis=(1, 2)) / totals
    return jnp.stack([flow_y, flow_x], 0).reshape(2, count_y, count_x)


def laplacian(widened, offsets):
    return (
        widened[:, :, :-2, 1:-1]
        + widened[:, :, 2:, 1:-1]
        + widened[:, :, 1:-1, :-2]
        + widened[:, :, 1:-1, 2:]
        - 4.0 * offsets
    )


def remote_neighbours(offsets):
    up_one = shifted(offsets, "gz", -1)
    up_two = shifted(offsets, "gz", -2)
    down_one = shifted(offsets, "gz", 1)
    down_two = shifted(offsets, "gz", 2)
    return (up_one, up_two, down_one, down_two)


def mesh_step(offsets, laplace, coeffs):
    up_one, up_two, down_one, down_two = remote_neighbours(offsets)
    forces = STIFFNESS * laplace
    forces = forces + coeffs[2:3] * (up_one - offsets - coeffs[0:2])
    forces = forces + coeffs[5:6] * (up_two - offsets - coeffs[3:5])
    forces = forces - coeffs[8:9] * (offsets - down_one - coeffs[6:8])
    forces = forces - coeffs[11:12] * (offsets - down_two - coeffs[9:11])
    return offsets + STEP_SIZE * forces


def general_body(images, tissue_mask):
    margin = (PATCH - STRIDE) // 2
    count_y = images.shape[1] // STRIDE
    count_x = images.shape[2] // STRIDE
    padded = padded_2(images, (("gy", 1), ("gx", 2)), margin)
    left_table, right_table = tables()
    own_mask = tissue_mask.astype(jnp.float32)
    own_re, own_im = spectrum(padded[0].astype(jnp.float32), left_table, right_table)
    next_re, next_im, next_mask = shifted((own_re, own_im, own_mask), "gz", -1)
    far_re, far_im, far_mask = shifted((own_re, own_im, own_mask), "gz", -2)
    flow_one = flow_between(own_re, own_im, next_re, next_im, left_table, count_y, count_x)
    flow_two = flow_between(own_re, own_im, far_re, far_im, left_table, count_y, count_x)
    weight_one = own_mask * next_mask
    weight_two = own_mask * far_mask
    low_flow_one, low_weight_one = shifted((flow_one, weight_one), "gz", 1)
    low_flow_two, low_weight_two = shifted((flow_two, weight_two), "gz", 2)
    coeffs = jnp.concatenate(
        [
            flow_one,
            weight_one,
            flow_two,
            weight_two,
            low_flow_one,
            low_weight_one,
            low_flow_two,
            low_weight_two,
        ],
        0,
    )[:, None]
    spread = padded_2(coeffs, (("gy", 2), ("gx", 3)), RELAX)
    global_y = lax.axis_index("gy") * count_y + jnp.arange(-RELAX, count_y + RELAX, dtype=jnp.int32)
    global_x = lax.axis_index("gx") * count_x + jnp.arange(-RELAX, count_x + RELAX, dtype=jnp.int32)
    inside_y = (global_y >= 0) & (global_y < count_y * lax.axis_size("gy"))
    inside_x = (global_x >= 0) & (global_x < count_x * lax.axis_size("gx"))
    inside = (inside_y[:, None] & inside_x[None, :]).astype(jnp.float32)
    offsets = jnp.zeros((2, 1, count_y + 2 * RELAX, count_x + 2 * RELAX), jnp.float32)
    for _ in range(RELAX):
        widened = jnp.pad(offsets, ((0, 0), (0, 0), (1, 1), (1, 1)))
        offsets = mesh_step(offsets, laplacian(widened, offsets), spread) * inside[None, None]
    offsets = offsets[:, :, RELAX : RELAX + count_y, RELAX : RELAX + count_x]
    flow_fields = jnp.concatenate([flow_one, flow_two], 0)[:, None]
    return (flow_fields, offsets)


MARGIN = (PATCH - STRIDE) // 2
HALF = PATCH // 2 + 1
LANES = 128
SUBLANES = 8
BAND = HALF - 1
HALO = -(-MARGIN // 16) * 16
RADIUS = RELAX - 1
STEP_ROWS = (PATCH - MARGIN, MARGIN - STRIDE)
STEP_HELD = STRIDE + SUBLANES
TOP_CUT = PATCH - HALO
LOW_CUT = HALO - SUBLANES


def split_table(table):
    high = table.astype(jnp.bfloat16)
    low = (table - high.astype(np.float64)).astype(jnp.bfloat16)
    return np.stack([high, low])


def trig(first, second):
    angle = 2.0 * np.pi / PATCH * ((first[:, None] * second[None, :]) % PATCH)
    return np.cos(angle), np.sin(angle)


def column_table():
    cosine, sine = trig(np.arange(PATCH), np.arange(HALF))
    table = np.zeros((PATCH, 2 * LANES))
    table[:, :HALF] = cosine
    table[:, LANES : LANES + HALF] = sine
    return split_table(table)


def stacked(table):
    high, low = split_table(table)
    return np.concatenate([high, low, high], 1)


def frequency_rows(positions):
    cosine, sine = trig(np.arange(HALF), positions)
    return np.concatenate([cosine[:BAND], cosine[BAND:], sine[1:BAND]], 0)


def row_tables():
    whole = stacked(frequency_rows(np.arange(PATCH)))
    changes = []
    for half in range(2):
        first = (STEP_ROWS[half] // SUBLANES) * SUBLANES
        positions = first + np.arange(STEP_HELD)
        used = (positions >= STEP_ROWS[half]) & (positions < STEP_ROWS[half] + STRIDE)
        changes.append(stacked(frequency_rows(positions) * used))
    return whole, np.stack(changes)


def inverse_tables():
    cosine, sine = trig(np.arange(PATCH), np.arange(HALF))
    weight = np.full((HALF,), 2.0 / PATCH)
    weight[0] = weight[-1] = 1.0 / PATCH
    cosine, sine = cosine * weight, sine * weight
    left = np.concatenate([cosine[:, :BAND], cosine[:, BAND:], -sine[:, 1:BAND]], 1)
    right = np.zeros((2 * LANES, PATCH))
    right[:HALF] = cosine.T
    right[LANES : LANES + HALF] = -sine.T
    return stacked(left), split_table(right)


def dot(left, right):
    return jnp.dot(left, right, preferred_element_type=jnp.float32)


def halves_of(value):
    high = value.astype(jnp.bfloat16)
    return high, (value - high.astype(jnp.float32)).astype(jnp.bfloat16)


def table_first(table, value):
    high, low = halves_of(value)
    return dot(table, jnp.concatenate([high, high, low], 0))


def cross_spectrum(first, second, sign):
    (acc, acs, asc, ass), (bcc, bcs, bsc, bss) = (
        (value[:BAND, :LANES], value[:BAND, LANES:], value[BAND:, :LANES], value[BAND:, LANES:])
        for value in (first, second)
    )
    even_0 = acc * bcc + acs * bcs
    even_1 = asc * bsc + ass * bss
    column_0 = acs * bcc - acc * bcs
    column_1 = ass * bsc - asc * bss
    by_row = sign * (asc * bcc - acc * bsc + ass * bcs - acs * bss)
    both = acc * bss + ass * bcc - asc * bcs - acs * bsc
    top = SUBLANES
    lone = lax.broadcasted_iota(jnp.int32, (top, LANES), 0) == 0

    def with_top(usual, single):
        return jnp.concatenate([jnp.where(lone, single[:top], usual[:top]), usual[top:]], 0)

    even = with_top(even_0 + even_1, even_0)
    by_row = with_top(by_row, even_1)
    by_column = sign * with_top(column_0 + column_1, column_0)
    both = with_top(both, sign * column_1[:top])
    return jnp.concatenate(
        [jnp.concatenate([even, by_column], 1), jnp.concatenate([by_row, both], 1)], 0
    )


def flow_kernel(columns, late, own_ref, other_ref, diagonal_ref, beside_ref, before_ref, column_ref,
                whole_ref, change_ref, left_ref, right_ref, out_ref, pixel_ref, partial_ref,
                high_ref, low_ref, rows_ref):
    half = lax.axis_index("gz")
    odd = lax.rem(lax.axis_index("gx"), 2)
    side = odd if late else 1 - odd
    held = PATCH + HALO
    lane = lax.broadcasted_iota(jnp.int32, (held, PATCH), 1)
    group = columns // 2
    base = side * group
    for image in range(2):
        tile = own_ref[0] if image == 0 else other_ref[0]
        mine = jnp.concatenate([tile, diagonal_ref[1 - image]], 0).astype(jnp.float32)
        halo = beside_ref[image].astype(jnp.float32)
        halo = jnp.concatenate([halo, halo[:, : PATCH - LANES]], 1)
        for column in range(group):
            start = (base + column) * STRIDE - MARGIN
            low_lane = jnp.where(side == 0, 0, start)
            high_lane = jnp.where(side == 0, start + PATCH, PATCH)
            inside = (lane >= low_lane) & (lane < high_lane)
            spot = (2 * column + image) * held
            pixel_ref[spot : spot + held] = jnp.where(inside, mine, halo).astype(jnp.bfloat16)
    pixels = pixel_ref[...]
    partial_ref[...] = dot(pixels, column_ref[0]) + dot(pixels, column_ref[1])
    sign = jnp.where(half == 0, 1.0, -1.0).astype(jnp.float32)
    upper = half == 0
    inner = lax.broadcasted_iota(jnp.int32, (SUBLANES, 2 * LANES), 0) < PATCH - MARGIN - TOP_CUT
    for column in range(group):
        spectra = []
        for image in range(2):
            spot = (2 * column + image) * held
            halo_spot = spot + PATCH

            def rows_at(upper_start, lower_start, size):
                start = pl.multiple_of(jnp.where(upper, upper_start, lower_start), SUBLANES)
                return partial_ref[pl.ds(start, size)]

            low_mix = jnp.where(
                inner & (half == 1),
                partial_ref[halo_spot + LOW_CUT : halo_spot + HALO],
                partial_ref[spot + LOW_CUT : spot + HALO],
            )
            top_mix = jnp.where(
                inner | (half == 1),
                partial_ref[spot + TOP_CUT : spot + TOP_CUT + SUBLANES],
                partial_ref[halo_spot : halo_spot + SUBLANES],
            )
            window = jnp.concatenate(
                [
                    rows_at(spot, halo_spot, LOW_CUT),
                    low_mix,
                    partial_ref[spot + HALO : spot + TOP_CUT],
                    top_mix,
                    rows_at(halo_spot + SUBLANES, spot + TOP_CUT + SUBLANES, HALO - SUBLANES),
                ],
                0,
            )
            change = rows_at(spot + TOP_CUT, spot + HALO - STEP_HELD, STEP_HELD)
            change = change - rows_at(halo_spot, halo_spot + HALO - STEP_HELD, STEP_HELD)
            near = table_first(whole_ref[...], window)
            spectra.append((near, near + table_first(change_ref[half], change)))
        for row in range(2):
            cross = cross_spectrum(spectra[0][row], spectra[1][row], sign)
            high, low = halves_of(table_first(left_ref[...], cross))
            spot = (row * group + column) * PATCH
            high_ref[spot : spot + PATCH] = high
            low_ref[spot : spot + PATCH] = low
    correl = dot(high_ref[...], right_ref[0]) + dot(high_ref[...], right_ref[1])
    correl = correl + dot(low_ref[...], right_ref[0])
    count = 2 * group
    for patch in range(count):
        squared = correl[patch * PATCH : (patch + 1) * PATCH]
        squared = squared * squared
        weights = squared * squared
        total = weights[:SUBLANES]
        based = jnp.zeros_like(total)
        for piece_at in range(1, PATCH // SUBLANES):
            piece = weights[piece_at * SUBLANES : (piece_at + 1) * SUBLANES]
            shift = piece_at * SUBLANES
            shift = shift - PATCH if shift >= PATCH // 2 else shift
            total = total + piece
            based = based + piece * float(shift)
        step = lax.broadcasted_iota(jnp.int32, (SUBLANES, PATCH), 0).astype(jnp.float32)
        based = based + step * total
        rows_ref[0, pl.ds(patch, 1)] = jnp.sum(total, 0, keepdims=True)
        rows_ref[1, pl.ds(patch, 1)] = jnp.sum(based, 0, keepdims=True)
    totals = rows_ref[0]
    shift = lax.broadcasted_iota(jnp.int32, (count, PATCH), 1)
    shift = jnp.where(shift >= PATCH // 2, shift - PATCH, shift).astype(jnp.float32)
    below = jnp.sum(totals, 1, keepdims=True) + EPSILON
    flow_y = jnp.sum(rows_ref[1], 1, keepdims=True) / below
    flow_x = jnp.sum(totals * shift, 1, keepdims=True) / below
    at = lax.broadcasted_iota(jnp.int32, (count, LANES), 1)
    patch = lax.broadcasted_iota(jnp.int32, (count, LANES), 0)
    second_row = (patch >= group).astype(jnp.int32)
    row = jnp.where(upper, second_row, 1 - second_row)
    spot = patch - group * second_row + columns * row + base
    line = jnp.where(at == spot, flow_y, 0.0) + jnp.where(at == spot + 2 * count, flow_x, 0.0)
    line = jnp.sum(line, 0, keepdims=True)
    if late:
        line = line + before_ref[...]
    else:
        lanes = lax.broadcasted_iota(jnp.int32, (1, LANES), 1)
        mask = before_ref[0].astype(jnp.float32)
        for row in range(mask.shape[0]):
            for column in range(columns):
                spot = 4 * count + row * columns + column
                line = jnp.where(lanes == spot, mask[row : row + 1, column : column + 1], line)
    out_ref[...] = jnp.broadcast_to(line, out_ref.shape)


def relax_kernel(rows, columns, got_ref, flow_ref, offsets_ref):
    size_y, size_x = lax.axis_size("gy"), lax.axis_size("gx")
    half, at_y, at_x = lax.axis_index("gz"), lax.axis_index("gy"), lax.axis_index("gx")
    count = rows * columns
    tile_rows = 2 * rows
    width = columns + 2 * RADIUS
    height = tile_rows + 2 * RADIUS
    per_section = size_y * size_x
    lane = lax.broadcasted_iota(jnp.int32, (1, LANES), 1).astype(jnp.float32)
    line = jnp.floor((lane + 0.5) * (1.0 / width))
    across = lane - line * width
    node_y = line.astype(jnp.int32) - RADIUS + at_y * tile_rows
    node_x = across.astype(jnp.int32) - RADIUS + at_x * columns
    inside = (node_y >= 0) & (node_y < tile_rows * size_y) & (node_x >= 0)
    inside = inside & (node_x < columns * size_x) & (line < height)

    def parts(value, size):
        whole = jnp.floor((value.astype(jnp.float32) + 0.5) * (1.0 / size)).astype(jnp.int32)
        return whole, value - whole * size

    tile_y, in_y = parts(node_y, tile_rows)
    tile_x, in_x = parts(node_x, columns)
    side, in_half = parts(in_y, rows)
    tile = jnp.where(inside, tile_y * size_x + tile_x, -1)
    flow_spot = in_half * columns + in_x
    spots = jnp.concatenate([flow_spot, flow_spot + count, 2 * count + in_y * columns + in_x], 1)
    picked = lax.broadcasted_iota(jnp.int32, (LANES, 3 * LANES), 0) == spots
    picker = picked.astype(jnp.float32).astype(jnp.bfloat16)
    rest = got_ref[...]
    spread = jnp.zeros((rest.shape[0], 3 * LANES), jnp.float32)
    for _ in range(3):
        piece = rest.astype(jnp.bfloat16)
        rest = rest - piece.astype(jnp.float32)
        spread = spread + dot(piece, picker)
    source = lax.broadcasted_iota(jnp.int32, (2 * per_section, LANES), 0)
    chosen = source == side * per_section + tile
    chosen = chosen & (tile >= 0)
    flow_y, flow_x = (
        jnp.sum(jnp.where(chosen, spread[:, axis * LANES : (axis + 1) * LANES], 0.0), 0, keepdims=True)
        for axis in range(2)
    )
    chosen = source[:per_section] == tile
    mask_0, mask_1 = (
        jnp.sum(jnp.where(chosen, spread[start : start + per_section, 2 * LANES :], 0.0), 0, keepdims=True)
        for start in (0, per_section)
    )
    flows = jnp.concatenate([flow_y, flow_x], 0)
    weight = mask_0 * mask_1
    kept = inside.astype(jnp.float32)
    sign = jnp.where(lax.broadcasted_iota(jnp.int32, (4, LANES), 0) < 2, 1.0, -1.0)
    weight = weight * sign
    offsets = jnp.zeros((4, LANES), jnp.float32)
    for step in range(RELAX):
        lower, upper = offsets[:2], offsets[2:]
        pull = upper - lower - flows
        forces = weight * jnp.concatenate([pull, pull], 0)
        if step:
            left = jnp.where(across < 0.5, 0.0, pltpu.roll(offsets, 1, 1))
            right = jnp.where(across > width - 1.5, 0.0, pltpu.roll(offsets, LANES - 1, 1))
            laplace = pltpu.roll(offsets, width, 1) + pltpu.roll(offsets, LANES - width, 1)
            forces = STIFFNESS * (laplace + left + right - 4.0 * offsets) + forces
        offsets = (offsets + STEP_SIZE * forces) * kept
    first = half == 0
    result = jnp.where(first, offsets[:2], offsets[2:])
    flows = jnp.where(first, flows, 0.0)
    for row in range(tile_rows):
        start = (RADIUS + row) * width + RADIUS
        for axis in range(2):
            offsets_ref[axis, 0, pl.ds(row, 1)] = result[axis : axis + 1, start : start + columns]
            flow_ref[axis, 0, pl.ds(row, 1)] = flows[axis : axis + 1, start : start + columns]
    flow_ref[2:] = jnp.zeros((flow_ref.shape[0] - 2, *flow_ref.shape[1:]), jnp.float32)


def vmem(count):
    return [pl.BlockSpec(memory_space=pltpu.VMEM)] * count


def pair_body(images, tissue_mask):
    sections, size_y, size_x = (lax.axis_size(name) for name in ("gz", "gy", "gx"))
    count_y = images.shape[1] // STRIDE
    count_x = images.shape[2] // STRIDE
    rows = count_y // 2
    half = lax.axis_index("gz")
    is_odd = lax.axis_index("gx") % 2 == 1
    other = lax.ppermute(images, "gz", [(0, 1), (1, 0)])
    both = jnp.concatenate([images, other], 0)
    edge = jnp.where(half == 1, both[:, PATCH - HALO :], both[:, :HALO])
    diagonal = []
    for tile in range(1, size_y):
        diagonal += [(size_y + tile - 1, tile), (tile, size_y + tile - 1)]
    beyond = lax.ppermute(edge, ("gz", "gy"), diagonal)
    tall = jnp.concatenate([both, beyond[::-1]], 1)
    low_side = tall[:, :, :LANES]
    high_side = jnp.concatenate([tall[:, :, LANES:], tall[:, :, PATCH - LANES : LANES]], 2)
    swaps = [
        [pair for left in range(offset, size_x - 1, 2) for pair in ((left, left + 1), (left + 1, left))]
        for offset in range(2)
    ]
    first = lax.ppermute(jnp.where(is_odd, low_side, high_side), "gx", swaps[0])
    second = lax.ppermute(jnp.where(is_odd, high_side, low_side), "gx", swaps[1])
    devices = sections * size_y * size_x
    tables = [jnp.asarray(table) for table in (column_table(), *row_tables(), *inverse_tables())]

    def flows(late, beside, before, lines):
        patches = count_x
        held = PATCH + HALO
        return pl.pallas_call(
            functools.partial(flow_kernel, count_x, late),
            out_shape=jax.ShapeDtypeStruct((lines, LANES), jnp.float32),
            in_specs=vmem(10),
            out_specs=vmem(1)[0],
            scratch_shapes=[
                pltpu.VMEM((patches * held, PATCH), jnp.bfloat16),
                pltpu.VMEM((patches * held, 2 * LANES), jnp.float32),
                pltpu.VMEM((patches * PATCH, 2 * LANES), jnp.bfloat16),
                pltpu.VMEM((patches * PATCH, 2 * LANES), jnp.bfloat16),
                pltpu.VMEM((2, patches, PATCH), jnp.float32),
            ],
            compiler_params=pltpu.CompilerParams(vmem_limit_bytes=16 * 2**20),
            cost_estimate=pl.CostEstimate(
                flops=patches * 2 * 2400 * 256 * 256, bytes_accessed=2**21, transcendentals=0
            ),
            name="flows",
        )(images, other, beyond, beside, before, *tables)

    lines = flows(True, second, flows(False, first, tissue_mask, 1), devices)
    got = lax.all_to_all(lines, ("gz", "gy", "gx"), 0, 0, tiled=True)
    return pl.pallas_call(
        functools.partial(relax_kernel, rows, count_x),
        out_shape=(
            jax.ShapeDtypeStruct((4, 1, count_y, count_x), jnp.float32),
            jax.ShapeDtypeStruct((2, 1, count_y, count_x), jnp.float32),
        ),
        in_specs=vmem(1),
        out_specs=tuple(vmem(2)),
        compiler_params=pltpu.CompilerParams(vmem_limit_bytes=4 * 2**20),
        name="relax",
    )(got)


def body(images, tissue_mask):
    paired = lax.axis_size("gz") == 2 and images.shape == (1, PATCH, PATCH)
    return (pair_body if paired else general_body)(images, tissue_mask)


def solution(mesh):
    placed = (P("gz", "gy", "gx"), P("gz", "gy", "gx"))
    return jax.shard_map(
        body,
        mesh=mesh,
        in_specs=placed,
        out_specs=(P(None, "gz", "gy", "gx"), P(None, "gz", "gy", "gx")),
        check_vma=False,
    )
```

```python
import functools
import math

import jax
import jax.numpy as jnp
import numpy as np
from jax import lax
from jax.experimental import pallas as pl
from jax.experimental.pallas import tpu as pltpu
from jax.sharding import PartitionSpec as P

PATCH = 160
STRIDE = 40
RELAX = 4


EPSILON = 1e-06
STIFFNESS = 0.5
STEP_SIZE = 0.2


def shifted(value, axis, steps):
    count = lax.axis_size(axis)
    initial, last = (max(0, -steps), min(count, count - steps))
    return lax.ppermute(value, axis, [(source, source + steps) for source in range(initial, last)])


def padded_2(x, sides, width):
    for axis, dim in sides:
        size, length = (lax.axis_size(axis), x.shape[dim])
        up = [(i, (i + 1) % size) for i in range(size - 1)]
        down = [(j, i) for i, j in up]
        last = lax.slice_in_dim(x, length - width, length, axis=dim)
        initial = lax.slice_in_dim(x, 0, width, axis=dim)
        before = lax.ppermute(last, axis, up)
        after = lax.ppermute(initial, axis, down)
        x = jnp.concatenate([before, x, after], axis=dim)
    return x


def windows(section):
    repeats = PATCH // STRIDE
    count_y = section.shape[0] // STRIDE - repeats + 1
    count_x = section.shape[1] // STRIDE - repeats + 1
    blocks = section.reshape(section.shape[0] // STRIDE, STRIDE, section.shape[1] // STRIDE, STRIDE)
    pieces = []
    for first in range(repeats):
        row_pieces = [
            blocks[first : first + count_y, :, second : second + count_x, :]
            for second in range(repeats)
        ]
        pieces.append(jnp.stack(row_pieces, 0))
    stacked = jnp.stack(pieces, 0)
    stacked = jnp.transpose(stacked, (2, 4, 0, 3, 1, 5))
    return stacked.reshape(count_y * count_x, PATCH, PATCH)


def tables():
    indices = jnp.arange(PATCH, dtype=jnp.int32)
    phases = indices[:, None] * indices[None, :] % PATCH
    angles = phases.astype(jnp.float32) * (2.0 * math.pi / PATCH)
    cosine_table = jnp.cos(angles)
    sine_table = jnp.sin(angles)
    left_table = jnp.concatenate([cosine_table, sine_table], 0)
    right_table = jnp.concatenate([cosine_table, sine_table], 1)
    return (left_table, right_table)


def spectrum(section, left_table, right_table):
    patches = windows(section)
    halfway = jnp.einsum("pnm,mk->pnk", patches, right_table, precision=lax.Precision.HIGHEST)
    products = jnp.einsum("kn,pnm->pkm", left_table, halfway, precision=lax.Precision.HIGHEST)
    cos_a = products[:, :PATCH, :PATCH]
    cos_b = products[:, :PATCH, PATCH:]
    sin_a = products[:, PATCH:, :PATCH]
    sin_b = products[:, PATCH:, PATCH:]
    return (cos_a - sin_b, -(cos_b + sin_a))


def flow_between(own_re, own_im, next_re, next_im, left_table, count_y, count_x):
    cross_re = next_re * own_re + next_im * own_im
    cross_im = next_im * own_re - next_re * own_im
    stacked = jnp.concatenate([cross_re, cross_im], 2)
    products = jnp.einsum("kn,pnm->pkm", left_table, stacked, precision=lax.Precision.HIGHEST)
    mixed_re = products[:, :PATCH, :PATCH] - products[:, PATCH:, PATCH:]
    mixed_im = products[:, :PATCH, PATCH:] + products[:, PATCH:, :PATCH]
    joined = jnp.concatenate([mixed_re, -mixed_im], 2)
    correl = jnp.einsum("pnm,mk->pnk", joined, left_table, precision=lax.Precision.HIGHEST) / (
        PATCH * PATCH
    )
    squared = correl * correl
    weights = squared * squared
    totals = jnp.sum(weights, axis=(1, 2)) + EPSILON
    shifts = ((jnp.arange(PATCH, dtype=jnp.int32) + PATCH // 2) % PATCH - PATCH // 2).astype(
        jnp.float32
    )
    flow_y = jnp.sum(weights * shifts[None, :, None], axis=(1, 2)) / totals
    flow_x = jnp.sum(weights * shifts[None, None, :], axis=(1, 2)) / totals
    return jnp.stack([flow_y, flow_x], 0).reshape(2, count_y, count_x)


def laplacian(widened, offsets):
    return (
        widened[:, :, :-2, 1:-1]
        + widened[:, :, 2:, 1:-1]
        + widened[:, :, 1:-1, :-2]
        + widened[:, :, 1:-1, 2:]
        - 4.0 * offsets
    )


def remote_neighbours(offsets):
    up_one = shifted(offsets, "gz", -1)
    up_two = shifted(offsets, "gz", -2)
    down_one = shifted(offsets, "gz", 1)
    down_two = shifted(offsets, "gz", 2)
    return (up_one, up_two, down_one, down_two)


def mesh_step(offsets, laplace, coeffs):
    up_one, up_two, down_one, down_two = remote_neighbours(offsets)
    forces = STIFFNESS * laplace
    forces = forces + coeffs[2:3] * (up_one - offsets - coeffs[0:2])
    forces = forces + coeffs[5:6] * (up_two - offsets - coeffs[3:5])
    forces = forces - coeffs[8:9] * (offsets - down_one - coeffs[6:8])
    forces = forces - coeffs[11:12] * (offsets - down_two - coeffs[9:11])
    return offsets + STEP_SIZE * forces


def general_body(images, tissue_mask):
    margin = (PATCH - STRIDE) // 2
    count_y = images.shape[1] // STRIDE
    count_x = images.shape[2] // STRIDE
    padded = padded_2(images, (("gy", 1), ("gx", 2)), margin)
    left_table, right_table = tables()
    own_mask = tissue_mask.astype(jnp.float32)
    own_re, own_im = spectrum(padded[0].astype(jnp.float32), left_table, right_table)
    next_re, next_im, next_mask = shifted((own_re, own_im, own_mask), "gz", -1)
    far_re, far_im, far_mask = shifted((own_re, own_im, own_mask), "gz", -2)
    flow_one = flow_between(own_re, own_im, next_re, next_im, left_table, count_y, count_x)
    flow_two = flow_between(own_re, own_im, far_re, far_im, left_table, count_y, count_x)
    weight_one = own_mask * next_mask
    weight_two = own_mask * far_mask
    low_flow_one, low_weight_one = shifted((flow_one, weight_one), "gz", 1)
    low_flow_two, low_weight_two = shifted((flow_two, weight_two), "gz", 2)
    coeffs = jnp.concatenate(
        [
            flow_one,
            weight_one,
            flow_two,
            weight_two,
            low_flow_one,
            low_weight_one,
            low_flow_two,
            low_weight_two,
        ],
        0,
    )[:, None]
    spread = padded_2(coeffs, (("gy", 2), ("gx", 3)), RELAX)
    global_y = lax.axis_index("gy") * count_y + jnp.arange(-RELAX, count_y + RELAX, dtype=jnp.int32)
    global_x = lax.axis_index("gx") * count_x + jnp.arange(-RELAX, count_x + RELAX, dtype=jnp.int32)
    inside_y = (global_y >= 0) & (global_y < count_y * lax.axis_size("gy"))
    inside_x = (global_x >= 0) & (global_x < count_x * lax.axis_size("gx"))
    inside = (inside_y[:, None] & inside_x[None, :]).astype(jnp.float32)
    offsets = jnp.zeros((2, 1, count_y + 2 * RELAX, count_x + 2 * RELAX), jnp.float32)
    for _ in range(RELAX):
        widened = jnp.pad(offsets, ((0, 0), (0, 0), (1, 1), (1, 1)))
        offsets = mesh_step(offsets, laplacian(widened, offsets), spread) * inside[None, None]
    offsets = offsets[:, :, RELAX : RELAX + count_y, RELAX : RELAX + count_x]
    flow_fields = jnp.concatenate([flow_one, flow_two], 0)[:, None]
    return (flow_fields, offsets)


MARGIN = (PATCH - STRIDE) // 2
HALF = PATCH // 2 + 1
LANES = 128
SUBLANES = 8
BAND = HALF - 1
HALO = -(-MARGIN // 16) * 16
RADIUS = RELAX - 1
WIDE = 2 * LANES
STEP_ROWS = (PATCH - MARGIN, MARGIN - STRIDE)
STEP_HELD = STRIDE + SUBLANES
TOP_CUT = PATCH - HALO
LOW_CUT = HALO - SUBLANES


def split_table(table):
    high = table.astype(jnp.bfloat16)
    low = (table - high.astype(np.float64)).astype(jnp.bfloat16)
    return np.stack([high, low])


def trig(first, second):
    angle = 2.0 * np.pi / PATCH * ((first[:, None] * second[None, :]) % PATCH)
    return np.cos(angle), np.sin(angle)


def column_table():
    cosine, sine = trig(np.arange(PATCH), np.arange(HALF))
    table = np.zeros((PATCH, 2 * LANES))
    table[:, :HALF] = cosine
    table[:, LANES : LANES + HALF] = sine
    return split_table(table)


def stacked(table):
    high, low = split_table(table)
    return np.concatenate([high, low, high], 1)


def frequency_rows(positions):
    cosine, sine = trig(np.arange(HALF), positions)
    return np.concatenate([cosine[:BAND], cosine[BAND:], sine[1:BAND]], 0)


def row_tables():
    whole = stacked(frequency_rows(np.arange(PATCH)))
    changes = []
    for half in range(2):
        first = (STEP_ROWS[half] // SUBLANES) * SUBLANES
        positions = first + np.arange(STEP_HELD)
        used = (positions >= STEP_ROWS[half]) & (positions < STEP_ROWS[half] + STRIDE)
        changes.append(stacked(frequency_rows(positions) * used))
    return whole, np.stack(changes)


def inverse_tables():
    cosine, sine = trig(np.arange(PATCH), np.arange(HALF))
    weight = np.full((HALF,), 2.0 / PATCH)
    weight[0] = weight[-1] = 1.0 / PATCH
    cosine, sine = cosine * weight, sine * weight
    left = np.concatenate([cosine[:, :BAND], cosine[:, BAND:], -sine[:, 1:BAND]], 1)
    right = np.zeros((2 * LANES, PATCH))
    right[:HALF] = cosine.T
    right[LANES : LANES + HALF] = -sine.T
    return stacked(left), split_table(right)


def all_tables():
    column = column_table()
    whole, change = row_tables()
    left, right = inverse_tables()
    blocks = [(column[0], column[1]), (whole,), (left,), (change[0], change[1]), (right[0], right[1])]
    rows = []
    for parts in blocks:
        block = np.zeros((parts[0].shape[0], 2 * WIDE), jnp.bfloat16)
        for at, part in enumerate(parts):
            block[:, at * WIDE : at * WIDE + part.shape[1]] = part
        rows.append(block)
    return np.concatenate(rows, 0)


def dot(left, right):
    return jnp.dot(left, right, preferred_element_type=jnp.float32)


def halves_of(value):
    high = value.astype(jnp.bfloat16)
    return high, (value - high.astype(jnp.float32)).astype(jnp.bfloat16)


def table_first(table, value):
    high, low = halves_of(value)
    return dot(table, jnp.concatenate([high, high, low], 0))


def cross_spectrum(first, second, sign):
    (acc, acs, asc, ass), (bcc, bcs, bsc, bss) = (
        (value[:BAND, :LANES], value[:BAND, LANES:], value[BAND:, :LANES], value[BAND:, LANES:])
        for value in (first, second)
    )
    even_0 = acc * bcc + acs * bcs
    even_1 = asc * bsc + ass * bss
    column_0 = acs * bcc - acc * bcs
    column_1 = ass * bsc - asc * bss
    by_row = sign * (asc * bcc - acc * bsc + ass * bcs - acs * bss)
    both = acc * bss + ass * bcc - asc * bcs - acs * bsc
    top = SUBLANES
    lone = lax.broadcasted_iota(jnp.int32, (top, LANES), 0) == 0

    def with_top(usual, single):
        return jnp.concatenate([jnp.where(lone, single[:top], usual[:top]), usual[top:]], 0)

    even = with_top(even_0 + even_1, even_0)
    by_row = with_top(by_row, even_1)
    by_column = sign * with_top(column_0 + column_1, column_0)
    both = with_top(both, sign * column_1[:top])
    return jnp.concatenate(
        [jnp.concatenate([even, by_column], 1), jnp.concatenate([by_row, both], 1)], 0
    )


def load_kernel(own_ref, table_ref, own_out, table_out, done):
    copies = [
        pltpu.make_async_copy(source, target, done.at[at])
        for at, (source, target) in enumerate([(own_ref, own_out), (table_ref, table_out)])
    ]
    for copy in copies:
        copy.start()
    for copy in copies:
        copy.wait()


def edge_kernel(own_ref, other_ref, out_ref):
    start = pl.multiple_of(jnp.where(lax.axis_index("gz") == 0, PATCH - HALO, 0), HALO // 2)
    out_ref[0] = own_ref[0, pl.ds(start, HALO)]
    out_ref[1] = other_ref[0, pl.ds(start, HALO)]


def pack_kernel(own_ref, other_ref, beyond_ref, first_ref, second_ref):
    wide, narrow = [], []
    for image in range(2):
        tile = own_ref[0] if image == 0 else other_ref[0]
        tall = jnp.concatenate([tile, beyond_ref[image]], 0).astype(jnp.float32)
        wide.append(tall[:, :LANES])
        narrow.append(jnp.concatenate([tall[:, LANES:]] * (LANES // (PATCH - LANES)), 1))
    lane = lax.broadcasted_iota(jnp.int32, wide[0].shape, 1)
    middle = LANES // 2
    extra = PATCH - LANES
    low = jnp.where(lane < middle, wide[0], pltpu.roll(wide[1], middle, 1))
    high = jnp.where(lane < middle, pltpu.roll(wide[0], middle, 1), wide[1])
    high = jnp.where(lane < extra, narrow[0], high)
    high = jnp.where((lane >= middle) & (lane < middle + extra), narrow[1], high)
    odd = lax.rem(lax.axis_index("gx"), 2) == 1
    first_ref[...] = jnp.where(odd, low, high).astype(jnp.bfloat16)
    second_ref[...] = jnp.where(odd, high, low).astype(jnp.bfloat16)


def flow_kernel(columns, late, own_ref, other_ref, beyond_ref, beside_ref, before_ref, table_ref, out_ref,
                pixel_ref, partial_ref, high_ref, low_ref, rows_ref):
    half = lax.axis_index("gz")
    odd = lax.rem(lax.axis_index("gx"), 2)
    side = odd if late else 1 - odd
    held = PATCH + HALO
    lane = lax.broadcasted_iota(jnp.int32, (held, PATCH), 1)
    group = columns // 2
    base = side * group
    beside = beside_ref[...].astype(jnp.float32)
    turned = pltpu.roll(beside, LANES // 2, 1)
    near_lanes = lax.broadcasted_iota(jnp.int32, (held, LANES), 1) < LANES // 2
    for image in range(2):
        tile = own_ref[0] if image == 0 else other_ref[0]
        mine = jnp.concatenate([tile, beyond_ref[image]], 0).astype(jnp.float32)
        here, there = (beside, turned) if image == 0 else (turned, beside)
        halo = jnp.where(near_lanes, here, there)
        halo = jnp.concatenate([halo, here[:, : PATCH - LANES]], 1)
        for column in range(group):
            start = (base + column) * STRIDE - MARGIN
            low_lane = jnp.where(side == 0, 0, start)
            high_lane = jnp.where(side == 0, start + PATCH, PATCH)
            inside = (lane >= low_lane) & (lane < high_lane)
            spot = (2 * column + image) * held
            pixel_ref[spot : spot + held] = jnp.where(inside, mine, halo).astype(jnp.bfloat16)
    pixels = pixel_ref[...]
    partial_ref[...] = dot(pixels, table_ref[:PATCH, :WIDE]) + dot(pixels, table_ref[:PATCH, WIDE:])
    whole = table_ref[PATCH : 2 * PATCH, : 3 * PATCH]
    left = table_ref[2 * PATCH : 3 * PATCH, : 3 * PATCH]
    changes = (
        table_ref[3 * PATCH : 4 * PATCH, start : start + 3 * STEP_HELD] for start in (0, WIDE)
    )
    step_table = jnp.where(half == 0, *changes)
    right = [table_ref[4 * PATCH :, start : start + PATCH] for start in (0, WIDE)]
    sign = jnp.where(half == 0, 1.0, -1.0).astype(jnp.float32)
    upper = half == 0
    inner = lax.broadcasted_iota(jnp.int32, (SUBLANES, 2 * LANES), 0) < PATCH - MARGIN - TOP_CUT
    for column in range(group):
        spectra = []
        for image in range(2):
            spot = (2 * column + image) * held
            halo_spot = spot + PATCH

            def rows_at(upper_start, lower_start, size):
                start = pl.multiple_of(jnp.where(upper, upper_start, lower_start), SUBLANES)
                return partial_ref[pl.ds(start, size)]

            low_mix = jnp.where(
                inner & (half == 1),
                partial_ref[halo_spot + LOW_CUT : halo_spot + HALO],
                partial_ref[spot + LOW_CUT : spot + HALO],
            )
            top_mix = jnp.where(
                inner | (half == 1),
                partial_ref[spot + TOP_CUT : spot + TOP_CUT + SUBLANES],
                partial_ref[halo_spot : halo_spot + SUBLANES],
            )
            window = jnp.concatenate(
                [
                    rows_at(spot, halo_spot, LOW_CUT),
                    low_mix,
                    partial_ref[spot + HALO : spot + TOP_CUT],
                    top_mix,
                    rows_at(halo_spot + SUBLANES, spot + TOP_CUT + SUBLANES, HALO - SUBLANES),
                ],
                0,
            )
            change = rows_at(spot + TOP_CUT, spot + HALO - STEP_HELD, STEP_HELD)
            change = change - rows_at(halo_spot, halo_spot + HALO - STEP_HELD, STEP_HELD)
            near = table_first(whole, window)
            spectra.append((near, near + table_first(step_table, change)))
        for row in range(2):
            cross = cross_spectrum(spectra[0][row], spectra[1][row], sign)
            high, low = halves_of(table_first(left, cross))
            spot = (row * group + column) * PATCH
            high_ref[spot : spot + PATCH] = high
            low_ref[spot : spot + PATCH] = low
    correl = dot(high_ref[...], right[0]) + dot(high_ref[...], right[1]) + dot(low_ref[...], right[0])
    count = 2 * group
    for patch in range(count):
        squared = correl[patch * PATCH : (patch + 1) * PATCH]
        squared = squared * squared
        weights = squared * squared
        total = weights[:SUBLANES]
        based = jnp.zeros_like(total)
        for piece_at in range(1, PATCH // SUBLANES):
            piece = weights[piece_at * SUBLANES : (piece_at + 1) * SUBLANES]
            shift = piece_at * SUBLANES
            shift = shift - PATCH if shift >= PATCH // 2 else shift
            total = total + piece
            based = based + piece * float(shift)
        step = lax.broadcasted_iota(jnp.int32, (SUBLANES, PATCH), 0).astype(jnp.float32)
        based = based + step * total
        rows_ref[0, pl.ds(patch, 1)] = jnp.sum(total, 0, keepdims=True)
        rows_ref[1, pl.ds(patch, 1)] = jnp.sum(based, 0, keepdims=True)
    totals = rows_ref[0]
    shift = lax.broadcasted_iota(jnp.int32, (count, PATCH), 1)
    shift = jnp.where(shift >= PATCH // 2, shift - PATCH, shift).astype(jnp.float32)
    below = jnp.sum(totals, 1, keepdims=True) + EPSILON
    flow_y = jnp.sum(rows_ref[1], 1, keepdims=True) / below
    flow_x = jnp.sum(totals * shift, 1, keepdims=True) / below
    at = lax.broadcasted_iota(jnp.int32, (count, LANES), 1)
    patch = lax.broadcasted_iota(jnp.int32, (count, LANES), 0)
    second_row = (patch >= group).astype(jnp.int32)
    row = jnp.where(upper, second_row, 1 - second_row)
    spot = patch - group * second_row + columns * row + base
    line = jnp.where(at == spot, flow_y, 0.0) + jnp.where(at == spot + 2 * count, flow_x, 0.0)
    line = jnp.sum(line, 0, keepdims=True)
    if late:
        line = line + before_ref[...]
    else:
        lanes = lax.broadcasted_iota(jnp.int32, (1, LANES), 1)
        mask = before_ref[0].astype(jnp.float32)
        for row in range(mask.shape[0]):
            for column in range(columns):
                spot = 4 * count + row * columns + column
                line = jnp.where(lanes == spot, mask[row : row + 1, column : column + 1], line)
    out_ref[...] = jnp.broadcast_to(line, out_ref.shape)


def relax_kernel(rows, columns, got_ref, flow_ref, offsets_ref):
    size_y, size_x = lax.axis_size("gy"), lax.axis_size("gx")
    half, at_y, at_x = lax.axis_index("gz"), lax.axis_index("gy"), lax.axis_index("gx")
    count = rows * columns
    tile_rows = 2 * rows
    width = columns + 2 * RADIUS
    height = tile_rows + 2 * RADIUS
    per_section = size_y * size_x
    lane = lax.broadcasted_iota(jnp.int32, (1, LANES), 1).astype(jnp.float32)
    line = jnp.floor((lane + 0.5) * (1.0 / width))
    across = lane - line * width
    node_y = line.astype(jnp.int32) - RADIUS + at_y * tile_rows
    node_x = across.astype(jnp.int32) - RADIUS + at_x * columns
    inside = (node_y >= 0) & (node_y < tile_rows * size_y) & (node_x >= 0)
    inside = inside & (node_x < columns * size_x) & (line < height)

    def parts(value, size):
        whole = jnp.floor((value.astype(jnp.float32) + 0.5) * (1.0 / size)).astype(jnp.int32)
        return whole, value - whole * size

    tile_y, in_y = parts(node_y, tile_rows)
    tile_x, in_x = parts(node_x, columns)
    side, in_half = parts(in_y, rows)
    tile = jnp.where(inside, tile_y * size_x + tile_x, -1)
    flow_spot = in_half * columns + in_x
    spots = jnp.concatenate([flow_spot, flow_spot + count, 2 * count + in_y * columns + in_x], 1)
    picked = lax.broadcasted_iota(jnp.int32, (LANES, 3 * LANES), 0) == spots
    picker = picked.astype(jnp.float32).astype(jnp.bfloat16)
    rest = got_ref[...]
    spread = jnp.zeros((rest.shape[0], 3 * LANES), jnp.float32)
    for _ in range(3):
        piece = rest.astype(jnp.bfloat16)
        rest = rest - piece.astype(jnp.float32)
        spread = spread + dot(piece, picker)
    source = lax.broadcasted_iota(jnp.int32, (2 * per_section, LANES), 0)
    chosen = source == side * per_section + tile
    chosen = chosen & (tile >= 0)
    flow_y, flow_x = (
        jnp.sum(jnp.where(chosen, spread[:, axis * LANES : (axis + 1) * LANES], 0.0), 0, keepdims=True)
        for axis in range(2)
    )
    chosen = source[:per_section] == tile
    mask_0, mask_1 = (
        jnp.sum(jnp.where(chosen, spread[start : start + per_section, 2 * LANES :], 0.0), 0, keepdims=True)
        for start in (0, per_section)
    )
    flows = jnp.concatenate([flow_y, flow_x], 0)
    weight = mask_0 * mask_1
    kept = inside.astype(jnp.float32)
    sign = jnp.where(lax.broadcasted_iota(jnp.int32, (4, LANES), 0) < 2, 1.0, -1.0)
    weight = weight * sign
    offsets = jnp.zeros((4, LANES), jnp.float32)
    for step in range(RELAX):
        lower, upper = offsets[:2], offsets[2:]
        pull = upper - lower - flows
        forces = weight * jnp.concatenate([pull, pull], 0)
        if step:
            left = jnp.where(across < 0.5, 0.0, pltpu.roll(offsets, 1, 1))
            right = jnp.where(across > width - 1.5, 0.0, pltpu.roll(offsets, LANES - 1, 1))
            laplace = pltpu.roll(offsets, width, 1) + pltpu.roll(offsets, LANES - width, 1)
            forces = STIFFNESS * (laplace + left + right - 4.0 * offsets) + forces
        offsets = (offsets + STEP_SIZE * forces) * kept
    first = half == 0
    result = jnp.where(first, offsets[:2], offsets[2:])
    flows = jnp.where(first, flows, 0.0)
    for row in range(tile_rows):
        start = (RADIUS + row) * width + RADIUS
        for axis in range(2):
            offsets_ref[axis, 0, pl.ds(row, 1)] = result[axis : axis + 1, start : start + columns]
            flow_ref[axis, 0, pl.ds(row, 1)] = flows[axis : axis + 1, start : start + columns]
    flow_ref[2:] = jnp.zeros((flow_ref.shape[0] - 2, *flow_ref.shape[1:]), jnp.float32)


def vmem(count):
    return [pl.BlockSpec(memory_space=pltpu.VMEM)] * count


def pair_body(images, tissue_mask):
    sections, size_y, size_x = (lax.axis_size(name) for name in ("gz", "gy", "gx"))
    count_y = images.shape[1] // STRIDE
    count_x = images.shape[2] // STRIDE
    rows = count_y // 2
    other = lax.ppermute(images, "gz", [(0, 1), (1, 0)])
    table = jnp.asarray(all_tables())
    own, table = pl.pallas_call(
        load_kernel,
        out_shape=(
            jax.ShapeDtypeStruct(images.shape, images.dtype),
            jax.ShapeDtypeStruct(table.shape, table.dtype),
        ),
        in_specs=[pl.BlockSpec(memory_space=pltpu.HBM)] * 2,
        out_specs=tuple(vmem(2)),
        scratch_shapes=[pltpu.SemaphoreType.DMA((2,))],
        compiler_params=pltpu.CompilerParams(vmem_limit_bytes=4 * 2**20),
        cost_estimate=pl.CostEstimate(flops=0, bytes_accessed=4 * table.size, transcendentals=0),
        name="load",
    )(images, table)
    edge = pl.pallas_call(
        edge_kernel,
        out_shape=jax.ShapeDtypeStruct((2, HALO, PATCH), jnp.bfloat16),
        in_specs=vmem(2),
        out_specs=vmem(1)[0],
        compiler_params=pltpu.CompilerParams(vmem_limit_bytes=4 * 2**20),
        name="edge",
    )(own, other)
    onward = []
    for tile in range(1, size_y):
        onward += [(tile - 1, tile), (size_y + tile, size_y + tile - 1)]
    beyond = lax.ppermute(edge, ("gz", "gy"), onward)
    swaps = [
        [pair for left in range(offset, size_x - 1, 2) for pair in ((left, left + 1), (left + 1, left))]
        for offset in range(2)
    ]
    packed = jax.ShapeDtypeStruct((PATCH + HALO, LANES), jnp.bfloat16)
    sends = pl.pallas_call(
        pack_kernel,
        out_shape=(packed, packed),
        in_specs=vmem(3),
        out_specs=tuple(vmem(2)),
        compiler_params=pltpu.CompilerParams(vmem_limit_bytes=4 * 2**20),
        name="pack",
    )(own, other, beyond)
    first, second = (lax.ppermute(send, "gx", swap) for send, swap in zip(sends, swaps))
    devices = sections * size_y * size_x

    def flows(late, beside, before, lines):
        patches = count_x
        held = PATCH + HALO
        return pl.pallas_call(
            functools.partial(flow_kernel, count_x, late),
            out_shape=jax.ShapeDtypeStruct((lines, LANES), jnp.float32),
            in_specs=vmem(6),
            out_specs=vmem(1)[0],
            scratch_shapes=[
                pltpu.VMEM((patches * held, PATCH), jnp.bfloat16),
                pltpu.VMEM((patches * held, 2 * LANES), jnp.float32),
                pltpu.VMEM((patches * PATCH, 2 * LANES), jnp.bfloat16),
                pltpu.VMEM((patches * PATCH, 2 * LANES), jnp.bfloat16),
                pltpu.VMEM((2, patches, PATCH), jnp.float32),
            ],
            compiler_params=pltpu.CompilerParams(vmem_limit_bytes=16 * 2**20),
            cost_estimate=pl.CostEstimate(
                flops=patches * 2 * 2400 * 256 * 256, bytes_accessed=2**21, transcendentals=0
            ),
            name="flows",
        )(own, other, beyond, beside, before, table)

    lines = flows(True, second, flows(False, first, tissue_mask, 1), devices)
    got = lax.all_to_all(lines, ("gz", "gy", "gx"), 0, 0, tiled=True)
    return pl.pallas_call(
        functools.partial(relax_kernel, rows, count_x),
        out_shape=(
            jax.ShapeDtypeStruct((4, 1, count_y, count_x), jnp.float32),
            jax.ShapeDtypeStruct((2, 1, count_y, count_x), jnp.float32),
        ),
        in_specs=vmem(1),
        out_specs=tuple(vmem(2)),
        compiler_params=pltpu.CompilerParams(vmem_limit_bytes=4 * 2**20),
        name="relax",
    )(got)


def body(images, tissue_mask):
    paired = lax.axis_size("gz") == 2 and images.shape == (1, PATCH, PATCH)
    return (pair_body if paired else general_body)(images, tissue_mask)


def solution(mesh):
    placed = (P("gz", "gy", "gx"), P("gz", "gy", "gx"))
    return jax.shard_map(
        body,
        mesh=mesh,
        in_specs=placed,
        out_specs=(P(None, "gz", "gy", "gx"), P(None, "gz", "gy", "gx")),
        check_vma=False,
    )
```

```python
import functools
import math

import jax
import jax.numpy as jnp
import numpy as np
from jax import lax
from jax.experimental import pallas as pl
from jax.experimental.pallas import tpu as pltpu
from jax.sharding import PartitionSpec as P

PATCH = 160
STRIDE = 40
RELAX = 4


EPSILON = 1e-06
STIFFNESS = 0.5
STEP_SIZE = 0.2


def shifted(value, axis, steps):
    count = lax.axis_size(axis)
    initial, last = (max(0, -steps), min(count, count - steps))
    return lax.ppermute(value, axis, [(source, source + steps) for source in range(initial, last)])


def padded_2(x, sides, width):
    for axis, dim in sides:
        size, length = (lax.axis_size(axis), x.shape[dim])
        up = [(i, (i + 1) % size) for i in range(size - 1)]
        down = [(j, i) for i, j in up]
        last = lax.slice_in_dim(x, length - width, length, axis=dim)
        initial = lax.slice_in_dim(x, 0, width, axis=dim)
        before = lax.ppermute(last, axis, up)
        after = lax.ppermute(initial, axis, down)
        x = jnp.concatenate([before, x, after], axis=dim)
    return x


def windows(section):
    repeats = PATCH // STRIDE
    count_y = section.shape[0] // STRIDE - repeats + 1
    count_x = section.shape[1] // STRIDE - repeats + 1
    blocks = section.reshape(section.shape[0] // STRIDE, STRIDE, section.shape[1] // STRIDE, STRIDE)
    pieces = []
    for first in range(repeats):
        row_pieces = [
            blocks[first : first + count_y, :, second : second + count_x, :]
            for second in range(repeats)
        ]
        pieces.append(jnp.stack(row_pieces, 0))
    stacked = jnp.stack(pieces, 0)
    stacked = jnp.transpose(stacked, (2, 4, 0, 3, 1, 5))
    return stacked.reshape(count_y * count_x, PATCH, PATCH)


def tables():
    indices = jnp.arange(PATCH, dtype=jnp.int32)
    phases = indices[:, None] * indices[None, :] % PATCH
    angles = phases.astype(jnp.float32) * (2.0 * math.pi / PATCH)
    cosine_table = jnp.cos(angles)
    sine_table = jnp.sin(angles)
    left_table = jnp.concatenate([cosine_table, sine_table], 0)
    right_table = jnp.concatenate([cosine_table, sine_table], 1)
    return (left_table, right_table)


def spectrum(section, left_table, right_table):
    patches = windows(section)
    halfway = jnp.einsum("pnm,mk->pnk", patches, right_table, precision=lax.Precision.HIGHEST)
    products = jnp.einsum("kn,pnm->pkm", left_table, halfway, precision=lax.Precision.HIGHEST)
    cos_a = products[:, :PATCH, :PATCH]
    cos_b = products[:, :PATCH, PATCH:]
    sin_a = products[:, PATCH:, :PATCH]
    sin_b = products[:, PATCH:, PATCH:]
    return (cos_a - sin_b, -(cos_b + sin_a))


def flow_between(own_re, own_im, next_re, next_im, left_table, count_y, count_x):
    cross_re = next_re * own_re + next_im * own_im
    cross_im = next_im * own_re - next_re * own_im
    stacked = jnp.concatenate([cross_re, cross_im], 2)
    products = jnp.einsum("kn,pnm->pkm", left_table, stacked, precision=lax.Precision.HIGHEST)
    mixed_re = products[:, :PATCH, :PATCH] - products[:, PATCH:, PATCH:]
    mixed_im = products[:, :PATCH, PATCH:] + products[:, PATCH:, :PATCH]
    joined = jnp.concatenate([mixed_re, -mixed_im], 2)
    correl = jnp.einsum("pnm,mk->pnk", joined, left_table, precision=lax.Precision.HIGHEST) / (
        PATCH * PATCH
    )
    squared = correl * correl
    weights = squared * squared
    totals = jnp.sum(weights, axis=(1, 2)) + EPSILON
    shifts = ((jnp.arange(PATCH, dtype=jnp.int32) + PATCH // 2) % PATCH - PATCH // 2).astype(
        jnp.float32
    )
    flow_y = jnp.sum(weights * shifts[None, :, None], axis=(1, 2)) / totals
    flow_x = jnp.sum(weights * shifts[None, None, :], axis=(1, 2)) / totals
    return jnp.stack([flow_y, flow_x], 0).reshape(2, count_y, count_x)


def laplacian(widened, offsets):
    return (
        widened[:, :, :-2, 1:-1]
        + widened[:, :, 2:, 1:-1]
        + widened[:, :, 1:-1, :-2]
        + widened[:, :, 1:-1, 2:]
        - 4.0 * offsets
    )


def remote_neighbours(offsets):
    up_one = shifted(offsets, "gz", -1)
    up_two = shifted(offsets, "gz", -2)
    down_one = shifted(offsets, "gz", 1)
    down_two = shifted(offsets, "gz", 2)
    return (up_one, up_two, down_one, down_two)


def mesh_step(offsets, laplace, coeffs):
    up_one, up_two, down_one, down_two = remote_neighbours(offsets)
    forces = STIFFNESS * laplace
    forces = forces + coeffs[2:3] * (up_one - offsets - coeffs[0:2])
    forces = forces + coeffs[5:6] * (up_two - offsets - coeffs[3:5])
    forces = forces - coeffs[8:9] * (offsets - down_one - coeffs[6:8])
    forces = forces - coeffs[11:12] * (offsets - down_two - coeffs[9:11])
    return offsets + STEP_SIZE * forces


def general_body(images, tissue_mask):
    margin = (PATCH - STRIDE) // 2
    count_y = images.shape[1] // STRIDE
    count_x = images.shape[2] // STRIDE
    padded = padded_2(images, (("gy", 1), ("gx", 2)), margin)
    left_table, right_table = tables()
    own_mask = tissue_mask.astype(jnp.float32)
    own_re, own_im = spectrum(padded[0].astype(jnp.float32), left_table, right_table)
    next_re, next_im, next_mask = shifted((own_re, own_im, own_mask), "gz", -1)
    far_re, far_im, far_mask = shifted((own_re, own_im, own_mask), "gz", -2)
    flow_one = flow_between(own_re, own_im, next_re, next_im, left_table, count_y, count_x)
    flow_two = flow_between(own_re, own_im, far_re, far_im, left_table, count_y, count_x)
    weight_one = own_mask * next_mask
    weight_two = own_mask * far_mask
    low_flow_one, low_weight_one = shifted((flow_one, weight_one), "gz", 1)
    low_flow_two, low_weight_two = shifted((flow_two, weight_two), "gz", 2)
    coeffs = jnp.concatenate(
        [
            flow_one,
            weight_one,
            flow_two,
            weight_two,
            low_flow_one,
            low_weight_one,
            low_flow_two,
            low_weight_two,
        ],
        0,
    )[:, None]
    spread = padded_2(coeffs, (("gy", 2), ("gx", 3)), RELAX)
    global_y = lax.axis_index("gy") * count_y + jnp.arange(-RELAX, count_y + RELAX, dtype=jnp.int32)
    global_x = lax.axis_index("gx") * count_x + jnp.arange(-RELAX, count_x + RELAX, dtype=jnp.int32)
    inside_y = (global_y >= 0) & (global_y < count_y * lax.axis_size("gy"))
    inside_x = (global_x >= 0) & (global_x < count_x * lax.axis_size("gx"))
    inside = (inside_y[:, None] & inside_x[None, :]).astype(jnp.float32)
    offsets = jnp.zeros((2, 1, count_y + 2 * RELAX, count_x + 2 * RELAX), jnp.float32)
    for _ in range(RELAX):
        widened = jnp.pad(offsets, ((0, 0), (0, 0), (1, 1), (1, 1)))
        offsets = mesh_step(offsets, laplacian(widened, offsets), spread) * inside[None, None]
    offsets = offsets[:, :, RELAX : RELAX + count_y, RELAX : RELAX + count_x]
    flow_fields = jnp.concatenate([flow_one, flow_two], 0)[:, None]
    return (flow_fields, offsets)


MARGIN = (PATCH - STRIDE) // 2
HALF = PATCH // 2 + 1
LANES = 128
SUBLANES = 8
BAND = HALF - 1
HALO = -(-MARGIN // 16) * 16
RADIUS = RELAX - 1
WIDE = 2 * LANES
STEP_ROWS = (PATCH - MARGIN, MARGIN - STRIDE)
STEP_HELD = STRIDE + SUBLANES
TOP_CUT = PATCH - HALO
LOW_CUT = HALO - SUBLANES


def split_table(table):
    high = table.astype(jnp.bfloat16)
    low = (table - high.astype(np.float64)).astype(jnp.bfloat16)
    return np.stack([high, low])


def trig(first, second):
    angle = 2.0 * np.pi / PATCH * ((first[:, None] * second[None, :]) % PATCH)
    return np.cos(angle), np.sin(angle)


def column_table():
    cosine, sine = trig(np.arange(PATCH), np.arange(HALF))
    table = np.zeros((PATCH, 2 * LANES))
    table[:, :HALF] = cosine
    table[:, LANES : LANES + HALF] = sine
    return split_table(table)


def stacked(table):
    high, low = split_table(table)
    return np.concatenate([high, low, high], 1)


def frequency_rows(positions):
    cosine, sine = trig(np.arange(HALF), positions)
    return np.concatenate([cosine[:BAND], cosine[BAND:], sine[1:BAND]], 0)


def row_tables():
    whole = stacked(frequency_rows(np.arange(PATCH)))
    changes = []
    for half in range(2):
        first = (STEP_ROWS[half] // SUBLANES) * SUBLANES
        positions = first + np.arange(STEP_HELD)
        used = (positions >= STEP_ROWS[half]) & (positions < STEP_ROWS[half] + STRIDE)
        changes.append(stacked(frequency_rows(positions) * used))
    return whole, np.stack(changes)


def inverse_tables():
    cosine, sine = trig(np.arange(PATCH), np.arange(HALF))
    weight = np.full((HALF,), 2.0 / PATCH)
    weight[0] = weight[-1] = 1.0 / PATCH
    cosine, sine = cosine * weight, sine * weight
    left = np.concatenate([cosine[:, :BAND], cosine[:, BAND:], -sine[:, 1:BAND]], 1)
    right = np.zeros((2 * LANES, PATCH))
    right[:HALF] = cosine.T
    right[LANES : LANES + HALF] = -sine.T
    return stacked(left), split_table(right)


def all_tables():
    column = column_table()
    whole, change = row_tables()
    left, right = inverse_tables()
    blocks = [(column[0], column[1]), (whole,), (left,), (change[0], change[1]), (right[0], right[1])]
    rows = []
    for parts in blocks:
        block = np.zeros((parts[0].shape[0], 2 * WIDE), jnp.bfloat16)
        for at, part in enumerate(parts):
            block[:, at * WIDE : at * WIDE + part.shape[1]] = part
        rows.append(block)
    return np.concatenate(rows, 0)


def dot(left, right):
    return jnp.dot(left, right, preferred_element_type=jnp.float32)


def halves_of(value):
    high = value.astype(jnp.bfloat16)
    return high, (value - high.astype(jnp.float32)).astype(jnp.bfloat16)


def table_first(table, value):
    high, low = halves_of(value)
    return dot(table, jnp.concatenate([high, high, low], 0))


def cross_spectrum(first, second):
    (acc, acs, asc, ass), (bcc, bcs, bsc, bss) = (
        (value[:BAND, :LANES], value[:BAND, LANES:], value[BAND:, :LANES], value[BAND:, LANES:])
        for value in (first, second)
    )
    even_0 = acc * bcc + acs * bcs
    even_1 = asc * bsc + ass * bss
    column_0 = acs * bcc - acc * bcs
    column_1 = ass * bsc - asc * bss
    by_row = asc * bcc - acc * bsc + ass * bcs - acs * bss
    both = acc * bss + ass * bcc - asc * bcs - acs * bsc
    top = SUBLANES
    lone = lax.broadcasted_iota(jnp.int32, (top, LANES), 0) == 0

    def with_top(usual, single):
        return jnp.concatenate([jnp.where(lone, single[:top], usual[:top]), usual[top:]], 0)

    even = with_top(even_0 + even_1, even_0)
    by_row = with_top(by_row, even_1)
    by_column = with_top(column_0 + column_1, column_0)
    both = with_top(both, column_1)
    return jnp.concatenate(
        [jnp.concatenate([even, by_column], 1), jnp.concatenate([by_row, both], 1)], 0
    )


def load_kernel(own_ref, table_ref, own_out, table_out, done):
    copies = [
        pltpu.make_async_copy(source, target, done.at[at])
        for at, (source, target) in enumerate([(own_ref, own_out), (table_ref, table_out)])
    ]
    for copy in copies:
        copy.start()
    for copy in copies:
        copy.wait()


def edge_kernel(own_ref, other_ref, out_ref):
    start = pl.multiple_of(jnp.where(lax.axis_index("gz") == 0, PATCH - HALO, 0), HALO // 2)
    out_ref[0] = own_ref[0, pl.ds(start, HALO)]
    out_ref[1] = other_ref[0, pl.ds(start, HALO)]


def pack_kernel(own_ref, other_ref, beyond_ref, first_ref, second_ref):
    wide, narrow = [], []
    for image in range(2):
        tile = own_ref[0] if image == 0 else other_ref[0]
        tall = jnp.concatenate([tile, beyond_ref[image]], 0).astype(jnp.float32)
        wide.append(tall[:, :LANES])
        narrow.append(jnp.concatenate([tall[:, LANES:]] * (LANES // (PATCH - LANES)), 1))
    lane = lax.broadcasted_iota(jnp.int32, wide[0].shape, 1)
    middle = LANES // 2
    extra = PATCH - LANES
    low = jnp.where(lane < middle, wide[0], pltpu.roll(wide[1], middle, 1))
    high = jnp.where(lane < middle, pltpu.roll(wide[0], middle, 1), wide[1])
    high = jnp.where(lane < extra, narrow[0], high)
    high = jnp.where((lane >= middle) & (lane < middle + extra), narrow[1], high)
    odd = lax.rem(lax.axis_index("gx"), 2) == 1
    first_ref[...] = jnp.where(odd, low, high).astype(jnp.bfloat16)
    second_ref[...] = jnp.where(odd, high, low).astype(jnp.bfloat16)


def flow_kernel(columns, late, own_ref, other_ref, beyond_ref, beside_ref, before_ref, table_ref, out_ref,
                pixel_ref, partial_ref, high_ref, low_ref, rows_ref):
    half = lax.axis_index("gz")
    odd = lax.rem(lax.axis_index("gx"), 2)
    side = odd if late else 1 - odd
    held = PATCH + HALO
    group = columns // 2
    base = side * group
    beside = beside_ref[...].astype(jnp.float32)
    turned = pltpu.roll(beside, LANES // 2, 1).astype(jnp.bfloat16)
    beside = beside_ref[...]
    lane = lax.broadcasted_iota(jnp.int32, (held, PATCH), 1).astype(jnp.float32).astype(jnp.bfloat16)
    near_lanes = lane[:, :LANES] < LANES // 2
    for image in range(2):
        tile = own_ref[0] if image == 0 else other_ref[0]
        mine = jnp.concatenate([tile, beyond_ref[image]], 0)
        here, there = (beside, turned) if image == 0 else (turned, beside)
        halo = jnp.where(near_lanes, here, there)
        halo = jnp.concatenate([halo, here[:, : PATCH - LANES]], 1)
        for column in range(group):
            start = (base + column) * STRIDE - MARGIN
            low_lane = jnp.where(side == 0, 0, start).astype(jnp.float32).astype(jnp.bfloat16)
            high_lane = jnp.where(side == 0, start + PATCH, PATCH).astype(jnp.float32).astype(jnp.bfloat16)
            inside = (lane >= low_lane) & (lane < high_lane)
            section = half if image == 0 else 1 - half
            spot = pl.multiple_of((2 * column + section) * held, HALO // 2)
            pixel_ref[pl.ds(spot, held)] = jnp.where(inside, mine, halo)
    for spot in range(0, pixel_ref.shape[0], held):
        pixels = pixel_ref[spot : spot + held]
        partial_ref[spot : spot + held] = dot(pixels, table_ref[:PATCH, :WIDE]) + dot(
            pixels, table_ref[:PATCH, WIDE:]
        )
    whole = table_ref[PATCH : 2 * PATCH, : 3 * PATCH]
    left = table_ref[2 * PATCH : 3 * PATCH, : 3 * PATCH]
    changes = (
        table_ref[3 * PATCH : 4 * PATCH, start : start + 3 * STEP_HELD] for start in (0, WIDE)
    )
    step_table = jnp.where(half == 0, *changes)
    right = [table_ref[4 * PATCH :, start : start + PATCH] for start in (0, WIDE)]
    upper = half == 0
    inner = lax.broadcasted_iota(jnp.int32, (SUBLANES, 2 * LANES), 0) < PATCH - MARGIN - TOP_CUT
    every = []
    for column in range(group):
        spectra = []
        every.append(spectra)
        for image in range(2):
            spot = (2 * column + image) * held
            halo_spot = spot + PATCH

            def rows_at(upper_start, lower_start, size):
                start = pl.multiple_of(jnp.where(upper, upper_start, lower_start), SUBLANES)
                return partial_ref[pl.ds(start, size)]

            low_mix = jnp.where(
                inner & (half == 1),
                partial_ref[halo_spot + LOW_CUT : halo_spot + HALO],
                partial_ref[spot + LOW_CUT : spot + HALO],
            )
            top_mix = jnp.where(
                inner | (half == 1),
                partial_ref[spot + TOP_CUT : spot + TOP_CUT + SUBLANES],
                partial_ref[halo_spot : halo_spot + SUBLANES],
            )
            window = jnp.concatenate(
                [
                    rows_at(spot, halo_spot, LOW_CUT),
                    low_mix,
                    partial_ref[spot + HALO : spot + TOP_CUT],
                    top_mix,
                    rows_at(halo_spot + SUBLANES, spot + TOP_CUT + SUBLANES, HALO - SUBLANES),
                ],
                0,
            )
            change = rows_at(spot + TOP_CUT, spot + HALO - STEP_HELD, STEP_HELD)
            change = change - rows_at(halo_spot, halo_spot + HALO - STEP_HELD, STEP_HELD)
            near = table_first(whole, window)
            spectra.append((near, near + table_first(step_table, change)))
    for column, spectra in enumerate(every):
        for row in range(2):
            cross = cross_spectrum(spectra[0][row], spectra[1][row])
            high, low = halves_of(table_first(left, cross))
            spot = (row * group + column) * PATCH
            high_ref[spot : spot + PATCH] = high
            low_ref[spot : spot + PATCH] = low
    count = 2 * group
    for patch in range(count):
        if patch % group == 0:
            block = slice(patch * PATCH, (patch + group) * PATCH)
            correl = dot(high_ref[block], right[0]) + dot(high_ref[block], right[1])
            correl = correl + dot(low_ref[block], right[0])
        squared = correl[patch % group * PATCH : (patch % group + 1) * PATCH]
        squared = squared * squared
        weights = squared * squared
        pieces = [weights[at : at + SUBLANES] for at in range(0, PATCH, SUBLANES)]
        middle = len(pieces) // 2
        above = pieces[middle - 1]
        ranks = above
        for piece in pieces[middle - 2 : 0 : -1]:
            above = above + piece
            ranks = ranks + above
        below = pieces[middle]
        depths = below
        for piece in pieces[middle + 1 :]:
            below = below + piece
            depths = depths + below
        total = pieces[0] + above + below
        based = float(SUBLANES) * (ranks - depths)
        step = lax.broadcasted_iota(jnp.int32, (SUBLANES, PATCH), 0).astype(jnp.float32)
        based = based + step * total
        rows_ref[0, pl.ds(patch, 1)] = jnp.sum(total, 0, keepdims=True)
        rows_ref[1, pl.ds(patch, 1)] = jnp.sum(based, 0, keepdims=True)
    totals = rows_ref[0]
    shift = lax.broadcasted_iota(jnp.int32, (count, PATCH), 1)
    shift = jnp.where(shift >= PATCH // 2, shift - PATCH, shift).astype(jnp.float32)
    below = jnp.sum(totals, 1, keepdims=True) + EPSILON
    flow_y = jnp.sum(rows_ref[1], 1, keepdims=True) / below
    flow_x = jnp.sum(totals * shift, 1, keepdims=True) / below
    at = lax.broadcasted_iota(jnp.int32, (count, LANES), 1)
    patch = lax.broadcasted_iota(jnp.int32, (count, LANES), 0)
    second_row = (patch >= group).astype(jnp.int32)
    row = jnp.where(upper, second_row, 1 - second_row)
    spot = patch - group * second_row + columns * row + base
    line = jnp.where(at == spot, flow_y, 0.0) + jnp.where(at == spot + 2 * count, flow_x, 0.0)
    line = jnp.sum(line, 0, keepdims=True)
    if late:
        line = line + before_ref[...]
    else:
        lanes = lax.broadcasted_iota(jnp.int32, (1, LANES), 1)
        mask = before_ref[0].astype(jnp.float32)
        for row in range(mask.shape[0]):
            for column in range(columns):
                spot = 4 * count + row * columns + column
                line = jnp.where(lanes == spot, mask[row : row + 1, column : column + 1], line)
    out_ref[...] = jnp.broadcast_to(line, out_ref.shape)


def relax_kernel(rows, columns, got_ref, flow_ref, offsets_ref):
    size_y, size_x = lax.axis_size("gy"), lax.axis_size("gx")
    half, at_y, at_x = lax.axis_index("gz"), lax.axis_index("gy"), lax.axis_index("gx")
    count = rows * columns
    tile_rows = 2 * rows
    width = columns + 2 * RADIUS
    height = tile_rows + 2 * RADIUS
    per_section = size_y * size_x
    lane = lax.broadcasted_iota(jnp.int32, (1, LANES), 1).astype(jnp.float32)
    line = jnp.floor((lane + 0.5) * (1.0 / width))
    across = lane - line * width
    node_y = line.astype(jnp.int32) - RADIUS + at_y * tile_rows
    node_x = across.astype(jnp.int32) - RADIUS + at_x * columns
    inside = (node_y >= 0) & (node_y < tile_rows * size_y) & (node_x >= 0)
    inside = inside & (node_x < columns * size_x) & (line < height)

    def parts(value, size):
        whole = jnp.floor((value.astype(jnp.float32) + 0.5) * (1.0 / size)).astype(jnp.int32)
        return whole, value - whole * size

    tile_y, in_y = parts(node_y, tile_rows)
    tile_x, in_x = parts(node_x, columns)
    side, in_half = parts(in_y, rows)
    tile = jnp.where(inside, tile_y * size_x + tile_x, -1)
    flow_spot = in_half * columns + in_x
    spots = jnp.concatenate([flow_spot, flow_spot + count, 2 * count + in_y * columns + in_x], 1)
    picked = lax.broadcasted_iota(jnp.int32, (LANES, 3 * LANES), 0) == spots
    picker = picked.astype(jnp.float32).astype(jnp.bfloat16)
    rest = got_ref[...]
    spread = jnp.zeros((rest.shape[0], 3 * LANES), jnp.float32)
    for _ in range(3):
        piece = rest.astype(jnp.bfloat16)
        rest = rest - piece.astype(jnp.float32)
        spread = spread + dot(piece, picker)
    source = lax.broadcasted_iota(jnp.int32, (2 * per_section, LANES), 0)
    chosen = source == side * per_section + tile
    chosen = chosen & (tile >= 0)
    flow_y, flow_x = (
        jnp.sum(jnp.where(chosen, spread[:, axis * LANES : (axis + 1) * LANES], 0.0), 0, keepdims=True)
        for axis in range(2)
    )
    chosen = source[:per_section] == tile
    mask_0, mask_1 = (
        jnp.sum(jnp.where(chosen, spread[start : start + per_section, 2 * LANES :], 0.0), 0, keepdims=True)
        for start in (0, per_section)
    )
    flows = jnp.concatenate([flow_y, flow_x], 0)
    weight = mask_0 * mask_1
    kept = inside.astype(jnp.float32)
    sign = jnp.where(lax.broadcasted_iota(jnp.int32, (4, LANES), 0) < 2, 1.0, -1.0)
    weight = weight * sign
    offsets = jnp.zeros((4, LANES), jnp.float32)
    for step in range(RELAX):
        lower, upper = offsets[:2], offsets[2:]
        pull = upper - lower - flows
        forces = weight * jnp.concatenate([pull, pull], 0)
        if step:
            left = jnp.where(across < 0.5, 0.0, pltpu.roll(offsets, 1, 1))
            right = jnp.where(across > width - 1.5, 0.0, pltpu.roll(offsets, LANES - 1, 1))
            laplace = pltpu.roll(offsets, width, 1) + pltpu.roll(offsets, LANES - width, 1)
            forces = STIFFNESS * (laplace + left + right - 4.0 * offsets) + forces
        offsets = (offsets + STEP_SIZE * forces) * kept
    first = half == 0
    result = jnp.where(first, offsets[:2], offsets[2:])
    flows = jnp.where(first, flows, 0.0)
    for row in range(tile_rows):
        start = (RADIUS + row) * width + RADIUS
        for axis in range(2):
            offsets_ref[axis, 0, pl.ds(row, 1)] = result[axis : axis + 1, start : start + columns]
            flow_ref[axis, 0, pl.ds(row, 1)] = flows[axis : axis + 1, start : start + columns]
    flow_ref[2:] = jnp.zeros((flow_ref.shape[0] - 2, *flow_ref.shape[1:]), jnp.float32)


def vmem(count):
    return [pl.BlockSpec(memory_space=pltpu.VMEM)] * count


def pair_body(images, tissue_mask):
    sections, size_y, size_x = (lax.axis_size(name) for name in ("gz", "gy", "gx"))
    count_y = images.shape[1] // STRIDE
    count_x = images.shape[2] // STRIDE
    rows = count_y // 2
    other = lax.ppermute(images, "gz", [(0, 1), (1, 0)])
    table = jnp.asarray(all_tables())
    own, table = pl.pallas_call(
        load_kernel,
        out_shape=(
            jax.ShapeDtypeStruct(images.shape, images.dtype),
            jax.ShapeDtypeStruct(table.shape, table.dtype),
        ),
        in_specs=[pl.BlockSpec(memory_space=pltpu.HBM)] * 2,
        out_specs=tuple(vmem(2)),
        scratch_shapes=[pltpu.SemaphoreType.DMA((2,))],
        compiler_params=pltpu.CompilerParams(vmem_limit_bytes=4 * 2**20),
        cost_estimate=pl.CostEstimate(flops=0, bytes_accessed=4 * table.size, transcendentals=0),
        name="load",
    )(images, table)
    edge = pl.pallas_call(
        edge_kernel,
        out_shape=jax.ShapeDtypeStruct((2, HALO, PATCH), jnp.bfloat16),
        in_specs=vmem(2),
        out_specs=vmem(1)[0],
        compiler_params=pltpu.CompilerParams(vmem_limit_bytes=4 * 2**20),
        name="edge",
    )(own, other)
    onward = []
    for tile in range(1, size_y):
        onward += [(tile - 1, tile), (size_y + tile, size_y + tile - 1)]
    beyond = lax.ppermute(edge, ("gz", "gy"), onward)
    swaps = [
        [pair for left in range(offset, size_x - 1, 2) for pair in ((left, left + 1), (left + 1, left))]
        for offset in range(2)
    ]
    packed = jax.ShapeDtypeStruct((PATCH + HALO, LANES), jnp.bfloat16)
    sends = pl.pallas_call(
        pack_kernel,
        out_shape=(packed, packed),
        in_specs=vmem(3),
        out_specs=tuple(vmem(2)),
        compiler_params=pltpu.CompilerParams(vmem_limit_bytes=4 * 2**20),
        name="pack",
    )(own, other, beyond)
    first, second = (lax.ppermute(send, "gx", swap) for send, swap in zip(sends, swaps))
    devices = sections * size_y * size_x

    def flows(late, beside, before, lines):
        patches = count_x
        held = PATCH + HALO
        return pl.pallas_call(
            functools.partial(flow_kernel, count_x, late),
            out_shape=jax.ShapeDtypeStruct((lines, LANES), jnp.float32),
            in_specs=vmem(6),
            out_specs=vmem(1)[0],
            scratch_shapes=[
                pltpu.VMEM((patches * held, PATCH), jnp.bfloat16),
                pltpu.VMEM((patches * held, 2 * LANES), jnp.float32),
                pltpu.VMEM((patches * PATCH, 2 * LANES), jnp.bfloat16),
                pltpu.VMEM((patches * PATCH, 2 * LANES), jnp.bfloat16),
                pltpu.VMEM((2, patches, PATCH), jnp.float32),
            ],
            compiler_params=pltpu.CompilerParams(vmem_limit_bytes=16 * 2**20),
            cost_estimate=pl.CostEstimate(
                flops=patches * 2 * 2400 * 256 * 256, bytes_accessed=2**21, transcendentals=0
            ),
            name="flows",
        )(own, other, beyond, beside, before, table)

    lines = flows(True, second, flows(False, first, tissue_mask, 1), devices)
    got = lax.all_to_all(lines, ("gz", "gy", "gx"), 0, 0, tiled=True)
    return pl.pallas_call(
        functools.partial(relax_kernel, rows, count_x),
        out_shape=(
            jax.ShapeDtypeStruct((4, 1, count_y, count_x), jnp.float32),
            jax.ShapeDtypeStruct((2, 1, count_y, count_x), jnp.float32),
        ),
        in_specs=vmem(1),
        out_specs=tuple(vmem(2)),
        compiler_params=pltpu.CompilerParams(vmem_limit_bytes=4 * 2**20),
        name="relax",
    )(got)


def body(images, tissue_mask):
    paired = lax.axis_size("gz") == 2 and images.shape == (1, PATCH, PATCH)
    return (pair_body if paired else general_body)(images, tissue_mask)


def solution(mesh):
    placed = (P("gz", "gy", "gx"), P("gz", "gy", "gx"))
    return jax.shard_map(
        body,
        mesh=mesh,
        in_specs=placed,
        out_specs=(P(None, "gz", "gy", "gx"), P(None, "gz", "gy", "gx")),
        check_vma=False,
    )
```

```python
import functools
import math

import jax
import jax.numpy as jnp
import numpy as np
from jax import lax
from jax.experimental import pallas as pl
from jax.experimental.pallas import tpu as pltpu
from jax.sharding import PartitionSpec as P

PATCH = 160
STRIDE = 40
RELAX = 4


EPSILON = 1e-06
STIFFNESS = 0.5
STEP_SIZE = 0.2


def shifted(value, axis, steps):
    count = lax.axis_size(axis)
    initial, last = (max(0, -steps), min(count, count - steps))
    return lax.ppermute(value, axis, [(source, source + steps) for source in range(initial, last)])


def padded_2(x, sides, width):
    for axis, dim in sides:
        size, length = (lax.axis_size(axis), x.shape[dim])
        up = [(i, (i + 1) % size) for i in range(size - 1)]
        down = [(j, i) for i, j in up]
        last = lax.slice_in_dim(x, length - width, length, axis=dim)
        initial = lax.slice_in_dim(x, 0, width, axis=dim)
        before = lax.ppermute(last, axis, up)
        after = lax.ppermute(initial, axis, down)
        x = jnp.concatenate([before, x, after], axis=dim)
    return x


def windows(section):
    repeats = PATCH // STRIDE
    count_y = section.shape[0] // STRIDE - repeats + 1
    count_x = section.shape[1] // STRIDE - repeats + 1
    blocks = section.reshape(section.shape[0] // STRIDE, STRIDE, section.shape[1] // STRIDE, STRIDE)
    pieces = []
    for first in range(repeats):
        row_pieces = [
            blocks[first : first + count_y, :, second : second + count_x, :]
            for second in range(repeats)
        ]
        pieces.append(jnp.stack(row_pieces, 0))
    stacked = jnp.stack(pieces, 0)
    stacked = jnp.transpose(stacked, (2, 4, 0, 3, 1, 5))
    return stacked.reshape(count_y * count_x, PATCH, PATCH)


def tables():
    indices = jnp.arange(PATCH, dtype=jnp.int32)
    phases = indices[:, None] * indices[None, :] % PATCH
    angles = phases.astype(jnp.float32) * (2.0 * math.pi / PATCH)
    cosine_table = jnp.cos(angles)
    sine_table = jnp.sin(angles)
    left_table = jnp.concatenate([cosine_table, sine_table], 0)
    right_table = jnp.concatenate([cosine_table, sine_table], 1)
    return (left_table, right_table)


def spectrum(section, left_table, right_table):
    patches = windows(section)
    halfway = jnp.einsum("pnm,mk->pnk", patches, right_table, precision=lax.Precision.HIGHEST)
    products = jnp.einsum("kn,pnm->pkm", left_table, halfway, precision=lax.Precision.HIGHEST)
    cos_a = products[:, :PATCH, :PATCH]
    cos_b = products[:, :PATCH, PATCH:]
    sin_a = products[:, PATCH:, :PATCH]
    sin_b = products[:, PATCH:, PATCH:]
    return (cos_a - sin_b, -(cos_b + sin_a))


def flow_between(own_re, own_im, next_re, next_im, left_table, count_y, count_x):
    cross_re = next_re * own_re + next_im * own_im
    cross_im = next_im * own_re - next_re * own_im
    stacked = jnp.concatenate([cross_re, cross_im], 2)
    products = jnp.einsum("kn,pnm->pkm", left_table, stacked, precision=lax.Precision.HIGHEST)
    mixed_re = products[:, :PATCH, :PATCH] - products[:, PATCH:, PATCH:]
    mixed_im = products[:, :PATCH, PATCH:] + products[:, PATCH:, :PATCH]
    joined = jnp.concatenate([mixed_re, -mixed_im], 2)
    correl = jnp.einsum("pnm,mk->pnk", joined, left_table, precision=lax.Precision.HIGHEST) / (
        PATCH * PATCH
    )
    squared = correl * correl
    weights = squared * squared
    totals = jnp.sum(weights, axis=(1, 2)) + EPSILON
    shifts = ((jnp.arange(PATCH, dtype=jnp.int32) + PATCH // 2) % PATCH - PATCH // 2).astype(
        jnp.float32
    )
    flow_y = jnp.sum(weights * shifts[None, :, None], axis=(1, 2)) / totals
    flow_x = jnp.sum(weights * shifts[None, None, :], axis=(1, 2)) / totals
    return jnp.stack([flow_y, flow_x], 0).reshape(2, count_y, count_x)


def laplacian(widened, offsets):
    return (
        widened[:, :, :-2, 1:-1]
        + widened[:, :, 2:, 1:-1]
        + widened[:, :, 1:-1, :-2]
        + widened[:, :, 1:-1, 2:]
        - 4.0 * offsets
    )


def remote_neighbours(offsets):
    up_one = shifted(offsets, "gz", -1)
    up_two = shifted(offsets, "gz", -2)
    down_one = shifted(offsets, "gz", 1)
    down_two = shifted(offsets, "gz", 2)
    return (up_one, up_two, down_one, down_two)


def mesh_step(offsets, laplace, coeffs):
    up_one, up_two, down_one, down_two = remote_neighbours(offsets)
    forces = STIFFNESS * laplace
    forces = forces + coeffs[2:3] * (up_one - offsets - coeffs[0:2])
    forces = forces + coeffs[5:6] * (up_two - offsets - coeffs[3:5])
    forces = forces - coeffs[8:9] * (offsets - down_one - coeffs[6:8])
    forces = forces - coeffs[11:12] * (offsets - down_two - coeffs[9:11])
    return offsets + STEP_SIZE * forces


def general_body(images, tissue_mask):
    margin = (PATCH - STRIDE) // 2
    count_y = images.shape[1] // STRIDE
    count_x = images.shape[2] // STRIDE
    padded = padded_2(images, (("gy", 1), ("gx", 2)), margin)
    left_table, right_table = tables()
    own_mask = tissue_mask.astype(jnp.float32)
    own_re, own_im = spectrum(padded[0].astype(jnp.float32), left_table, right_table)
    next_re, next_im, next_mask = shifted((own_re, own_im, own_mask), "gz", -1)
    far_re, far_im, far_mask = shifted((own_re, own_im, own_mask), "gz", -2)
    flow_one = flow_between(own_re, own_im, next_re, next_im, left_table, count_y, count_x)
    flow_two = flow_between(own_re, own_im, far_re, far_im, left_table, count_y, count_x)
    weight_one = own_mask * next_mask
    weight_two = own_mask * far_mask
    low_flow_one, low_weight_one = shifted((flow_one, weight_one), "gz", 1)
    low_flow_two, low_weight_two = shifted((flow_two, weight_two), "gz", 2)
    coeffs = jnp.concatenate(
        [
            flow_one,
            weight_one,
            flow_two,
            weight_two,
            low_flow_one,
            low_weight_one,
            low_flow_two,
            low_weight_two,
        ],
        0,
    )[:, None]
    spread = padded_2(coeffs, (("gy", 2), ("gx", 3)), RELAX)
    global_y = lax.axis_index("gy") * count_y + jnp.arange(-RELAX, count_y + RELAX, dtype=jnp.int32)
    global_x = lax.axis_index("gx") * count_x + jnp.arange(-RELAX, count_x + RELAX, dtype=jnp.int32)
    inside_y = (global_y >= 0) & (global_y < count_y * lax.axis_size("gy"))
    inside_x = (global_x >= 0) & (global_x < count_x * lax.axis_size("gx"))
    inside = (inside_y[:, None] & inside_x[None, :]).astype(jnp.float32)
    offsets = jnp.zeros((2, 1, count_y + 2 * RELAX, count_x + 2 * RELAX), jnp.float32)
    for _ in range(RELAX):
        widened = jnp.pad(offsets, ((0, 0), (0, 0), (1, 1), (1, 1)))
        offsets = mesh_step(offsets, laplacian(widened, offsets), spread) * inside[None, None]
    offsets = offsets[:, :, RELAX : RELAX + count_y, RELAX : RELAX + count_x]
    flow_fields = jnp.concatenate([flow_one, flow_two], 0)[:, None]
    return (flow_fields, offsets)


MARGIN = (PATCH - STRIDE) // 2
HALF = PATCH // 2 + 1
LANES = 128
SUBLANES = 8
BAND = HALF - 1
HALO = -(-MARGIN // 16) * 16
RADIUS = RELAX - 1
WIDE = 2 * LANES
HELD = PATCH + HALO
SIDE = LANES // 2
HALO_AT = PATCH
ROWS_AT = HALO_AT + 2 * 3 * SIDE
LEFT_AT = ROWS_AT + 2 * 2 * PATCH
RIGHT_AT = LEFT_AT + PATCH


def split_table(table):
    high = table.astype(jnp.bfloat16)
    low = (table - high.astype(np.float64)).astype(jnp.bfloat16)
    return np.stack([high, low])


def trig(first, second):
    angle = 2.0 * np.pi / PATCH * ((first[:, None] * second[None, :]) % PATCH)
    return np.cos(angle), np.sin(angle)


def column_tables():
    cosine, sine = trig(np.arange(PATCH), np.arange(HALF))
    table = np.zeros((PATCH, WIDE))
    table[:, :HALF] = cosine
    table[:, LANES : LANES + HALF] = sine
    spot = np.arange(SIDE)
    before = np.where(spot < PATCH - LANES, LANES + spot, SIDE + spot)
    outer = []
    for window in range(PATCH // STRIDE):
        start = window * STRIDE - MARGIN
        column = before if start < 0 else spot
        used = column >= start + PATCH if start < 0 else column < start
        high, low = split_table(table[column] * used[:, None])
        outer.append(np.concatenate([high, high, low], 0))
    return split_table(table), outer


def stacked(table):
    high, low = split_table(table)
    return np.concatenate([high, low, high], 1)


def frequency_rows(positions):
    cosine, sine = trig(np.arange(HALF), positions)
    return np.concatenate([cosine[:BAND], cosine[BAND:], sine[1:BAND]], 0)


def row_tables():
    tables = []
    for half in range(2):
        first = PATCH - HALO if half == 0 else 0
        position = np.concatenate([np.arange(PATCH), first + np.arange(HALO)])
        image_row = position + np.where(np.arange(HELD) < PATCH, 0, -PATCH if half == 0 else PATCH)
        rows = frequency_rows(position)
        windows = []
        for window in (2 * half, 2 * half + 1):
            start = window * STRIDE - MARGIN
            windows.append(rows * ((image_row >= start) & (image_row < start + PATCH)))
        tables.append(split_table(np.concatenate(windows, 0)))
    return tables


def inverse_tables():
    cosine, sine = trig(np.arange(PATCH), np.arange(HALF))
    weight = np.full((HALF,), 2.0 / PATCH)
    weight[0] = weight[-1] = 1.0 / PATCH
    cosine, sine = cosine * weight, sine * weight
    left = np.concatenate([cosine[:, :BAND], cosine[:, BAND:], -sine[:, 1:BAND]], 1)
    right = np.zeros((2 * LANES, PATCH))
    right[:HALF] = cosine.T
    right[LANES : LANES + HALF] = -sine.T
    return stacked(left), split_table(right)


def all_tables():
    mine, outer = column_tables()
    left, right = inverse_tables()
    blocks = [mine, outer[:2], outer[2:], *row_tables(), (left,), right]
    rows = []
    for parts in blocks:
        block = np.zeros((parts[0].shape[0], 2 * WIDE), jnp.bfloat16)
        for at, part in enumerate(parts):
            block[:, at * WIDE : at * WIDE + part.shape[1]] = part
        rows.append(block)
    return np.concatenate(rows, 0)


def dot(left, right):
    return jnp.dot(left, right, preferred_element_type=jnp.float32)


def halves_of(value):
    high = value.astype(jnp.bfloat16)
    return high, (value - high.astype(jnp.float32)).astype(jnp.bfloat16)


def table_first(table, value):
    high, low = halves_of(value)
    return dot(table, jnp.concatenate([high, high, low], 0))


def cross_spectrum(first, second):
    (acc, acs, asc, ass), (bcc, bcs, bsc, bss) = (
        (value[:BAND, :LANES], value[:BAND, LANES:], value[BAND:, :LANES], value[BAND:, LANES:])
        for value in (first, second)
    )
    even_0 = acc * bcc + acs * bcs
    even_1 = asc * bsc + ass * bss
    column_0 = acs * bcc - acc * bcs
    column_1 = ass * bsc - asc * bss
    by_row = asc * bcc - acc * bsc + ass * bcs - acs * bss
    both = acc * bss + ass * bcc - asc * bcs - acs * bsc
    top = SUBLANES
    lone = lax.broadcasted_iota(jnp.int32, (top, LANES), 0) == 0

    def with_top(usual, single):
        return jnp.concatenate([jnp.where(lone, single[:top], usual[:top]), usual[top:]], 0)

    even = with_top(even_0 + even_1, even_0)
    by_row = with_top(by_row, even_1)
    by_column = with_top(column_0 + column_1, column_0)
    both = with_top(both, column_1)
    return jnp.concatenate(
        [jnp.concatenate([even, by_column], 1), jnp.concatenate([by_row, both], 1)], 0
    )


def load_kernel(own_ref, table_ref, own_out, table_out, done):
    copies = [
        pltpu.make_async_copy(source, target, done.at[at])
        for at, (source, target) in enumerate([(own_ref, own_out), (table_ref, table_out)])
    ]
    for copy in copies:
        copy.start()
    for copy in copies:
        copy.wait()


def edge_kernel(own_ref, other_ref, out_ref):
    start = pl.multiple_of(jnp.where(lax.axis_index("gz") == 0, PATCH - HALO, 0), HALO // 2)
    out_ref[0] = own_ref[0, pl.ds(start, HALO)]
    out_ref[1] = other_ref[0, pl.ds(start, HALO)]


def pack_kernel(own_ref, other_ref, beyond_ref, first_ref, second_ref):
    wide, narrow = [], []
    for image in range(2):
        tile = own_ref[0] if image == 0 else other_ref[0]
        tall = jnp.concatenate([tile, beyond_ref[image]], 0).astype(jnp.float32)
        wide.append(tall[:, :LANES])
        narrow.append(jnp.concatenate([tall[:, LANES:]] * (LANES // (PATCH - LANES)), 1))
    lane = lax.broadcasted_iota(jnp.int32, wide[0].shape, 1)
    middle = LANES // 2
    extra = PATCH - LANES
    low = jnp.where(lane < middle, wide[0], pltpu.roll(wide[1], middle, 1))
    high = jnp.where(lane < middle, pltpu.roll(wide[0], middle, 1), wide[1])
    high = jnp.where(lane < extra, narrow[0], high)
    high = jnp.where((lane >= middle) & (lane < middle + extra), narrow[1], high)
    odd = lax.rem(lax.axis_index("gx"), 2) == 1
    first_ref[...] = jnp.where(odd, low, high).astype(jnp.bfloat16)
    second_ref[...] = jnp.where(odd, high, low).astype(jnp.bfloat16)


def to_row_frequencies(table_ref, half, pixels):
    start = pl.multiple_of(ROWS_AT + half * (2 * PATCH), PATCH)
    high = table_ref[pl.ds(start, 2 * PATCH), :HELD]
    low = table_ref[pl.ds(start, 2 * PATCH), WIDE : WIDE + HELD]
    return dot(high, pixels) + dot(low, pixels)


def finish(columns, side, own_spectra, own_side, beside_ref, table_ref, high_ref, low_ref, rows_ref):
    half = lax.axis_index("gz")
    group = columns // 2
    beside = to_row_frequencies(table_ref, half, beside_ref[...]) - own_side
    lane = lax.broadcasted_iota(jnp.int32, beside.shape, 1)
    parts = []
    for value in (beside, pltpu.roll(beside, SIDE, 1)):
        high = value.astype(jnp.bfloat16).astype(jnp.float32)
        parts.append((high, value - high))
    factors = []
    for image in range(2):
        high = parts[image][0]
        both = jnp.where(lane < SIDE, high, parts[1 - image][1])
        factors.append(jnp.concatenate([both, high[:, :SIDE]], 1).astype(jnp.bfloat16))
    upper = half == 0
    start = pl.multiple_of(HALO_AT + side * (3 * SIDE), SIDE)
    spectra = []
    for column in range(group):
        table = table_ref[pl.ds(start, 3 * SIDE), column * WIDE : (column + 1) * WIDE]
        for section in range(2):
            factor = jnp.where(upper, factors[section], factors[1 - section])
            spot = slice(section * 2 * PATCH, (section + 1) * 2 * PATCH)
            spectra.append(own_spectra[spot] + dot(factor, table))
    left = table_ref[LEFT_AT:RIGHT_AT, : 3 * PATCH]
    right = [table_ref[RIGHT_AT:, start : start + PATCH] for start in (0, WIDE)]
    count = 2 * group
    for patch in range(count):
        row, column = patch % 2, patch // 2
        start = row * PATCH
        cross = cross_spectrum(
            *(value[start : start + PATCH] for value in spectra[2 * column : 2 * column + 2])
        )
        high, low = halves_of(table_first(left, cross))
        high_ref[patch * PATCH : (patch + 1) * PATCH] = high
        low_ref[patch * PATCH : (patch + 1) * PATCH] = low
    for patch in range(count):
        if patch % 2 == 0:
            block = slice(patch * PATCH, (patch + 2) * PATCH)
            correl = dot(high_ref[block], right[0]) + dot(high_ref[block], right[1])
            correl = correl + dot(low_ref[block], right[0])
        squared = correl[patch % 2 * PATCH : (patch % 2 + 1) * PATCH]
        squared = squared * squared
        weights = squared * squared
        pieces = [weights[at : at + SUBLANES] for at in range(0, PATCH, SUBLANES)]
        middle = len(pieces) // 2
        above = pieces[middle - 1]
        ranks = above
        for piece in pieces[middle - 2 : 0 : -1]:
            above = above + piece
            ranks = ranks + above
        below = pieces[middle]
        depths = below
        for piece in pieces[middle + 1 :]:
            below = below + piece
            depths = depths + below
        total = pieces[0] + above + below
        based = float(SUBLANES) * (ranks - depths)
        step = lax.broadcasted_iota(jnp.int32, (SUBLANES, PATCH), 0).astype(jnp.float32)
        based = based + step * total
        rows_ref[0, pl.ds(patch, 1)] = jnp.sum(total, 0, keepdims=True)
        rows_ref[1, pl.ds(patch, 1)] = jnp.sum(based, 0, keepdims=True)
    totals = rows_ref[0]
    shift = lax.broadcasted_iota(jnp.int32, (count, PATCH), 1)
    shift = jnp.where(shift >= PATCH // 2, shift - PATCH, shift).astype(jnp.float32)
    below = jnp.sum(totals, 1, keepdims=True) + EPSILON
    flow_y = jnp.sum(rows_ref[1], 1, keepdims=True) / below
    flow_x = jnp.sum(totals * shift, 1, keepdims=True) / below
    at = lax.broadcasted_iota(jnp.int32, (count, LANES), 1)
    patch = lax.broadcasted_iota(jnp.int32, (count, LANES), 0)
    spot = (patch >> 1) + columns * (patch & 1) + side * group
    line = jnp.where(at == spot, flow_y, 0.0) + jnp.where(at == spot + 2 * count, flow_x, 0.0)
    return jnp.sum(line, 0, keepdims=True)


def early_kernel(columns, own_ref, other_ref, beyond_ref, early_side_ref, late_side_ref, beside_ref,
                 mask_ref, table_ref, line_ref, own_spectra_ref, own_side_ref, high_rows_ref,
                 low_rows_ref, high_ref, low_ref, rows_ref):
    half = lax.axis_index("gz")
    side = 1 - lax.rem(lax.axis_index("gx"), 2)
    images = [
        jnp.concatenate([tile, beyond_ref[image]], 0)
        for image, tile in enumerate((own_ref[0], other_ref[0]))
    ]
    upper = half == 0
    one, two = (table_ref[:PATCH, at : at + WIDE] for at in (0, WIDE))
    for section in range(2):
        pixels = jnp.where(upper, images[section], images[1 - section])
        spot = slice(section * 2 * PATCH, (section + 1) * 2 * PATCH)
        high_rows_ref[spot], low_rows_ref[spot] = halves_of(
            to_row_frequencies(table_ref, half, pixels)
        )
        high, low = high_rows_ref[spot], low_rows_ref[spot]
        own_spectra_ref[spot] = dot(high, one) + dot(high, two) + dot(low, one)
    own_side_ref[...] = to_row_frequencies(table_ref, half, late_side_ref[...])
    own_side = to_row_frequencies(table_ref, half, early_side_ref[...])
    line = finish(
        columns, side, own_spectra_ref, own_side, beside_ref, table_ref, high_ref, low_ref, rows_ref
    )
    lanes = lax.broadcasted_iota(jnp.int32, (1, LANES), 1)
    mask = mask_ref[0].astype(jnp.float32)
    for row in range(mask.shape[0]):
        for column in range(columns):
            spot = 4 * columns + row * columns + column
            line = jnp.where(lanes == spot, mask[row : row + 1, column : column + 1], line)
    line_ref[...] = line


def late_kernel(columns, line_ref, own_spectra_ref, own_side_ref, beside_ref, table_ref, out_ref,
                high_ref, low_ref, rows_ref):
    side = lax.rem(lax.axis_index("gx"), 2)
    line = finish(
        columns, side, own_spectra_ref, own_side_ref[...], beside_ref, table_ref, high_ref, low_ref, rows_ref
    )
    out_ref[...] = jnp.broadcast_to(line_ref[...] + line, out_ref.shape)


def relax_kernel(rows, columns, got_ref, flow_ref, offsets_ref):
    size_y, size_x = lax.axis_size("gy"), lax.axis_size("gx")
    half, at_y, at_x = lax.axis_index("gz"), lax.axis_index("gy"), lax.axis_index("gx")
    count = rows * columns
    tile_rows = 2 * rows
    width = columns + 2 * RADIUS
    height = tile_rows + 2 * RADIUS
    per_section = size_y * size_x
    lane = lax.broadcasted_iota(jnp.int32, (1, LANES), 1).astype(jnp.float32)
    line = jnp.floor((lane + 0.5) * (1.0 / width))
    across = lane - line * width
    node_y = line.astype(jnp.int32) - RADIUS + at_y * tile_rows
    node_x = across.astype(jnp.int32) - RADIUS + at_x * columns
    inside = (node_y >= 0) & (node_y < tile_rows * size_y) & (node_x >= 0)
    inside = inside & (node_x < columns * size_x) & (line < height)

    def parts(value, size):
        whole = jnp.floor((value.astype(jnp.float32) + 0.5) * (1.0 / size)).astype(jnp.int32)
        return whole, value - whole * size

    tile_y, in_y = parts(node_y, tile_rows)
    tile_x, in_x = parts(node_x, columns)
    side, in_half = parts(in_y, rows)
    tile = jnp.where(inside, tile_y * size_x + tile_x, -1)
    flow_spot = in_half * columns + in_x
    spots = jnp.concatenate([flow_spot, flow_spot + count, 2 * count + in_y * columns + in_x], 1)
    picked = lax.broadcasted_iota(jnp.int32, (LANES, 3 * LANES), 0) == spots
    picker = picked.astype(jnp.float32).astype(jnp.bfloat16)
    rest = got_ref[...]
    spread = jnp.zeros((rest.shape[0], 3 * LANES), jnp.float32)
    for _ in range(3):
        piece = rest.astype(jnp.bfloat16)
        rest = rest - piece.astype(jnp.float32)
        spread = spread + dot(piece, picker)
    source = lax.broadcasted_iota(jnp.int32, (2 * per_section, LANES), 0)
    chosen = source == side * per_section + tile
    chosen = chosen & (tile >= 0)
    flow_y, flow_x = (
        jnp.sum(jnp.where(chosen, spread[:, axis * LANES : (axis + 1) * LANES], 0.0), 0, keepdims=True)
        for axis in range(2)
    )
    chosen = source[:per_section] == tile
    mask_0, mask_1 = (
        jnp.sum(jnp.where(chosen, spread[start : start + per_section, 2 * LANES :], 0.0), 0, keepdims=True)
        for start in (0, per_section)
    )
    flows = jnp.concatenate([flow_y, flow_x], 0)
    weight = mask_0 * mask_1
    kept = inside.astype(jnp.float32)
    sign = jnp.where(lax.broadcasted_iota(jnp.int32, (4, LANES), 0) < 2, 1.0, -1.0)
    weight = weight * sign
    offsets = jnp.zeros((4, LANES), jnp.float32)
    for step in range(RELAX):
        lower, upper = offsets[:2], offsets[2:]
        pull = upper - lower - flows
        forces = weight * jnp.concatenate([pull, pull], 0)
        if step:
            left = jnp.where(across < 0.5, 0.0, pltpu.roll(offsets, 1, 1))
            right = jnp.where(across > width - 1.5, 0.0, pltpu.roll(offsets, LANES - 1, 1))
            laplace = pltpu.roll(offsets, width, 1) + pltpu.roll(offsets, LANES - width, 1)
            forces = STIFFNESS * (laplace + left + right - 4.0 * offsets) + forces
        offsets = (offsets + STEP_SIZE * forces) * kept
    first = half == 0
    result = jnp.where(first, offsets[:2], offsets[2:])
    flows = jnp.where(first, flows, 0.0)
    for row in range(tile_rows):
        start = (RADIUS + row) * width + RADIUS
        for axis in range(2):
            offsets_ref[axis, 0, pl.ds(row, 1)] = result[axis : axis + 1, start : start + columns]
            flow_ref[axis, 0, pl.ds(row, 1)] = flows[axis : axis + 1, start : start + columns]
    flow_ref[2:] = jnp.zeros((flow_ref.shape[0] - 2, *flow_ref.shape[1:]), jnp.float32)


def vmem(count):
    return [pl.BlockSpec(memory_space=pltpu.VMEM)] * count


def pair_body(images, tissue_mask):
    sections, size_y, size_x = (lax.axis_size(name) for name in ("gz", "gy", "gx"))
    count_y = images.shape[1] // STRIDE
    count_x = images.shape[2] // STRIDE
    rows = count_y // 2
    other = lax.ppermute(images, "gz", [(0, 1), (1, 0)])
    table = jnp.asarray(all_tables())
    own, table = pl.pallas_call(
        load_kernel,
        out_shape=(
            jax.ShapeDtypeStruct(images.shape, images.dtype),
            jax.ShapeDtypeStruct(table.shape, table.dtype),
        ),
        in_specs=[pl.BlockSpec(memory_space=pltpu.HBM)] * 2,
        out_specs=tuple(vmem(2)),
        scratch_shapes=[pltpu.SemaphoreType.DMA((2,))],
        compiler_params=pltpu.CompilerParams(vmem_limit_bytes=4 * 2**20),
        cost_estimate=pl.CostEstimate(flops=0, bytes_accessed=4 * table.size, transcendentals=0),
        name="load",
    )(images, table)
    edge = pl.pallas_call(
        edge_kernel,
        out_shape=jax.ShapeDtypeStruct((2, HALO, PATCH), jnp.bfloat16),
        in_specs=vmem(2),
        out_specs=vmem(1)[0],
        compiler_params=pltpu.CompilerParams(vmem_limit_bytes=4 * 2**20),
        name="edge",
    )(own, other)
    onward = []
    for tile in range(1, size_y):
        onward += [(tile - 1, tile), (size_y + tile, size_y + tile - 1)]
    beyond = lax.ppermute(edge, ("gz", "gy"), onward)
    swaps = [
        [pair for left in range(offset, size_x - 1, 2) for pair in ((left, left + 1), (left + 1, left))]
        for offset in range(2)
    ]
    packed = jax.ShapeDtypeStruct((PATCH + HALO, LANES), jnp.bfloat16)
    sends = pl.pallas_call(
        pack_kernel,
        out_shape=(packed, packed),
        in_specs=vmem(3),
        out_specs=tuple(vmem(2)),
        compiler_params=pltpu.CompilerParams(vmem_limit_bytes=4 * 2**20),
        name="pack",
    )(own, other, beyond)
    first, second = (lax.ppermute(send, "gx", swap) for send, swap in zip(sends, swaps))
    devices = sections * size_y * size_x

    patches = rows * count_x // 2
    common = [
        pltpu.VMEM((patches * PATCH, WIDE), jnp.bfloat16),
        pltpu.VMEM((patches * PATCH, WIDE), jnp.bfloat16),
        pltpu.VMEM((2, patches, PATCH), jnp.float32),
    ]
    params = pltpu.CompilerParams(vmem_limit_bytes=16 * 2**20)
    line, own_spectra, own_side = pl.pallas_call(
        functools.partial(early_kernel, count_x),
        out_shape=(
            jax.ShapeDtypeStruct((1, LANES), jnp.float32),
            jax.ShapeDtypeStruct((4 * PATCH, WIDE), jnp.float32),
            jax.ShapeDtypeStruct((2 * PATCH, LANES), jnp.float32),
        ),
        in_specs=vmem(8),
        out_specs=tuple(vmem(3)),
        scratch_shapes=[pltpu.VMEM((4 * PATCH, PATCH), jnp.bfloat16)] * 2 + common,
        compiler_params=params,
        cost_estimate=pl.CostEstimate(flops=2 * 10**9, bytes_accessed=2**21, transcendentals=0),
        name="early",
    )(own, other, beyond, sends[1], sends[0], first, tissue_mask, table)
    lines = pl.pallas_call(
        functools.partial(late_kernel, count_x),
        out_shape=jax.ShapeDtypeStruct((devices, LANES), jnp.float32),
        in_specs=vmem(5),
        out_specs=vmem(1)[0],
        scratch_shapes=common,
        compiler_params=params,
        cost_estimate=pl.CostEstimate(flops=10**9, bytes_accessed=2**21, transcendentals=0),
        name="late",
    )(line, own_spectra, own_side, second, table)
    got = lax.all_to_all(lines, ("gz", "gy", "gx"), 0, 0, tiled=True)
    return pl.pallas_call(
        functools.partial(relax_kernel, rows, count_x),
        out_shape=(
            jax.ShapeDtypeStruct((4, 1, count_y, count_x), jnp.float32),
            jax.ShapeDtypeStruct((2, 1, count_y, count_x), jnp.float32),
        ),
        in_specs=vmem(1),
        out_specs=tuple(vmem(2)),
        compiler_params=pltpu.CompilerParams(vmem_limit_bytes=4 * 2**20),
        name="relax",
    )(got)


def body(images, tissue_mask):
    paired = lax.axis_size("gz") == 2 and images.shape == (1, PATCH, PATCH)
    return (pair_body if paired else general_body)(images, tissue_mask)


def solution(mesh):
    placed = (P("gz", "gy", "gx"), P("gz", "gy", "gx"))
    return jax.shard_map(
        body,
        mesh=mesh,
        in_specs=placed,
        out_specs=(P(None, "gz", "gy", "gx"), P(None, "gz", "gy", "gx")),
        check_vma=False,
    )
```

```python
import functools
import math

import jax
import jax.numpy as jnp
import numpy as np
from jax import lax
from jax.experimental import pallas as pl
from jax.experimental.pallas import tpu as pltpu
from jax.sharding import PartitionSpec as P

PATCH = 160
STRIDE = 40
RELAX = 4


EPSILON = 1e-06
STIFFNESS = 0.5
STEP_SIZE = 0.2


def shifted(value, axis, steps):
    count = lax.axis_size(axis)
    initial, last = (max(0, -steps), min(count, count - steps))
    return lax.ppermute(value, axis, [(source, source + steps) for source in range(initial, last)])


def padded_2(x, sides, width):
    for axis, dim in sides:
        size, length = (lax.axis_size(axis), x.shape[dim])
        up = [(i, (i + 1) % size) for i in range(size - 1)]
        down = [(j, i) for i, j in up]
        last = lax.slice_in_dim(x, length - width, length, axis=dim)
        initial = lax.slice_in_dim(x, 0, width, axis=dim)
        before = lax.ppermute(last, axis, up)
        after = lax.ppermute(initial, axis, down)
        x = jnp.concatenate([before, x, after], axis=dim)
    return x


def windows(section):
    repeats = PATCH // STRIDE
    count_y = section.shape[0] // STRIDE - repeats + 1
    count_x = section.shape[1] // STRIDE - repeats + 1
    blocks = section.reshape(section.shape[0] // STRIDE, STRIDE, section.shape[1] // STRIDE, STRIDE)
    pieces = []
    for first in range(repeats):
        row_pieces = [
            blocks[first : first + count_y, :, second : second + count_x, :]
            for second in range(repeats)
        ]
        pieces.append(jnp.stack(row_pieces, 0))
    stacked = jnp.stack(pieces, 0)
    stacked = jnp.transpose(stacked, (2, 4, 0, 3, 1, 5))
    return stacked.reshape(count_y * count_x, PATCH, PATCH)


def tables():
    indices = jnp.arange(PATCH, dtype=jnp.int32)
    phases = indices[:, None] * indices[None, :] % PATCH
    angles = phases.astype(jnp.float32) * (2.0 * math.pi / PATCH)
    cosine_table = jnp.cos(angles)
    sine_table = jnp.sin(angles)
    left_table = jnp.concatenate([cosine_table, sine_table], 0)
    right_table = jnp.concatenate([cosine_table, sine_table], 1)
    return (left_table, right_table)


def spectrum(section, left_table, right_table):
    patches = windows(section)
    halfway = jnp.einsum("pnm,mk->pnk", patches, right_table, precision=lax.Precision.HIGHEST)
    products = jnp.einsum("kn,pnm->pkm", left_table, halfway, precision=lax.Precision.HIGHEST)
    cos_a = products[:, :PATCH, :PATCH]
    cos_b = products[:, :PATCH, PATCH:]
    sin_a = products[:, PATCH:, :PATCH]
    sin_b = products[:, PATCH:, PATCH:]
    return (cos_a - sin_b, -(cos_b + sin_a))


def flow_between(own_re, own_im, next_re, next_im, left_table, count_y, count_x):
    cross_re = next_re * own_re + next_im * own_im
    cross_im = next_im * own_re - next_re * own_im
    stacked = jnp.concatenate([cross_re, cross_im], 2)
    products = jnp.einsum("kn,pnm->pkm", left_table, stacked, precision=lax.Precision.HIGHEST)
    mixed_re = products[:, :PATCH, :PATCH] - products[:, PATCH:, PATCH:]
    mixed_im = products[:, :PATCH, PATCH:] + products[:, PATCH:, :PATCH]
    joined = jnp.concatenate([mixed_re, -mixed_im], 2)
    correl = jnp.einsum("pnm,mk->pnk", joined, left_table, precision=lax.Precision.HIGHEST) / (
        PATCH * PATCH
    )
    squared = correl * correl
    weights = squared * squared
    totals = jnp.sum(weights, axis=(1, 2)) + EPSILON
    shifts = ((jnp.arange(PATCH, dtype=jnp.int32) + PATCH // 2) % PATCH - PATCH // 2).astype(
        jnp.float32
    )
    flow_y = jnp.sum(weights * shifts[None, :, None], axis=(1, 2)) / totals
    flow_x = jnp.sum(weights * shifts[None, None, :], axis=(1, 2)) / totals
    return jnp.stack([flow_y, flow_x], 0).reshape(2, count_y, count_x)


def laplacian(widened, offsets):
    return (
        widened[:, :, :-2, 1:-1]
        + widened[:, :, 2:, 1:-1]
        + widened[:, :, 1:-1, :-2]
        + widened[:, :, 1:-1, 2:]
        - 4.0 * offsets
    )


def remote_neighbours(offsets):
    up_one = shifted(offsets, "gz", -1)
    up_two = shifted(offsets, "gz", -2)
    down_one = shifted(offsets, "gz", 1)
    down_two = shifted(offsets, "gz", 2)
    return (up_one, up_two, down_one, down_two)


def mesh_step(offsets, laplace, coeffs):
    up_one, up_two, down_one, down_two = remote_neighbours(offsets)
    forces = STIFFNESS * laplace
    forces = forces + coeffs[2:3] * (up_one - offsets - coeffs[0:2])
    forces = forces + coeffs[5:6] * (up_two - offsets - coeffs[3:5])
    forces = forces - coeffs[8:9] * (offsets - down_one - coeffs[6:8])
    forces = forces - coeffs[11:12] * (offsets - down_two - coeffs[9:11])
    return offsets + STEP_SIZE * forces


def general_body(images, tissue_mask):
    margin = (PATCH - STRIDE) // 2
    count_y = images.shape[1] // STRIDE
    count_x = images.shape[2] // STRIDE
    padded = padded_2(images, (("gy", 1), ("gx", 2)), margin)
    left_table, right_table = tables()
    own_mask = tissue_mask.astype(jnp.float32)
    own_re, own_im = spectrum(padded[0].astype(jnp.float32), left_table, right_table)
    next_re, next_im, next_mask = shifted((own_re, own_im, own_mask), "gz", -1)
    far_re, far_im, far_mask = shifted((own_re, own_im, own_mask), "gz", -2)
    flow_one = flow_between(own_re, own_im, next_re, next_im, left_table, count_y, count_x)
    flow_two = flow_between(own_re, own_im, far_re, far_im, left_table, count_y, count_x)
    weight_one = own_mask * next_mask
    weight_two = own_mask * far_mask
    low_flow_one, low_weight_one = shifted((flow_one, weight_one), "gz", 1)
    low_flow_two, low_weight_two = shifted((flow_two, weight_two), "gz", 2)
    coeffs = jnp.concatenate(
        [
            flow_one,
            weight_one,
            flow_two,
            weight_two,
            low_flow_one,
            low_weight_one,
            low_flow_two,
            low_weight_two,
        ],
        0,
    )[:, None]
    spread = padded_2(coeffs, (("gy", 2), ("gx", 3)), RELAX)
    global_y = lax.axis_index("gy") * count_y + jnp.arange(-RELAX, count_y + RELAX, dtype=jnp.int32)
    global_x = lax.axis_index("gx") * count_x + jnp.arange(-RELAX, count_x + RELAX, dtype=jnp.int32)
    inside_y = (global_y >= 0) & (global_y < count_y * lax.axis_size("gy"))
    inside_x = (global_x >= 0) & (global_x < count_x * lax.axis_size("gx"))
    inside = (inside_y[:, None] & inside_x[None, :]).astype(jnp.float32)
    offsets = jnp.zeros((2, 1, count_y + 2 * RELAX, count_x + 2 * RELAX), jnp.float32)
    for _ in range(RELAX):
        widened = jnp.pad(offsets, ((0, 0), (0, 0), (1, 1), (1, 1)))
        offsets = mesh_step(offsets, laplacian(widened, offsets), spread) * inside[None, None]
    offsets = offsets[:, :, RELAX : RELAX + count_y, RELAX : RELAX + count_x]
    flow_fields = jnp.concatenate([flow_one, flow_two], 0)[:, None]
    return (flow_fields, offsets)


MARGIN = (PATCH - STRIDE) // 2
HALF = PATCH // 2 + 1
LANES = 128
SUBLANES = 8
BAND = HALF - 1
HALO = -(-MARGIN // 16) * 16
RADIUS = RELAX - 1
WIDE = 2 * LANES
HELD = PATCH + HALO
SIDE = LANES // 2
HALO_AT = PATCH
ROWS_AT = HALO_AT + 2 * 3 * SIDE
LEFT_AT = ROWS_AT + 2 * 2 * PATCH
RIGHT_AT = LEFT_AT + PATCH


def split_table(table):
    high = table.astype(jnp.bfloat16)
    low = (table - high.astype(np.float64)).astype(jnp.bfloat16)
    return np.stack([high, low])


def trig(first, second):
    angle = 2.0 * np.pi / PATCH * ((first[:, None] * second[None, :]) % PATCH)
    return np.cos(angle), np.sin(angle)


def column_tables():
    cosine, sine = trig(np.arange(PATCH), np.arange(HALF))
    table = np.zeros((PATCH, WIDE))
    table[:, :HALF] = cosine
    table[:, LANES : LANES + HALF] = sine
    spot = np.arange(SIDE)
    before = np.where(spot < PATCH - LANES, LANES + spot, SIDE + spot)
    outer = []
    for window in range(PATCH // STRIDE):
        start = window * STRIDE - MARGIN
        column = before if start < 0 else spot
        used = column >= start + PATCH if start < 0 else column < start
        high, low = split_table(table[column] * used[:, None])
        outer.append(np.concatenate([high, high, low], 0))
    return split_table(table), outer


def stacked(table):
    high, low = split_table(table)
    return np.concatenate([high, low, high], 1)


def frequency_rows(positions):
    cosine, sine = trig(np.arange(HALF), positions)
    return np.concatenate([cosine[:BAND], cosine[BAND:], sine[1:BAND]], 0)


def row_tables():
    tables = []
    for half in range(2):
        first = PATCH - HALO if half == 0 else 0
        position = np.concatenate([np.arange(PATCH), first + np.arange(HALO)])
        image_row = position + np.where(np.arange(HELD) < PATCH, 0, -PATCH if half == 0 else PATCH)
        rows = frequency_rows(position)
        windows = []
        for window in (2 * half, 2 * half + 1):
            start = window * STRIDE - MARGIN
            windows.append(rows * ((image_row >= start) & (image_row < start + PATCH)))
        tables.append(split_table(np.concatenate(windows, 0)))
    return tables


def inverse_tables():
    cosine, sine = trig(np.arange(PATCH), np.arange(HALF))
    weight = np.full((HALF,), 2.0 / PATCH)
    weight[0] = weight[-1] = 1.0 / PATCH
    cosine, sine = cosine * weight, sine * weight
    left = np.concatenate([cosine[:, :BAND], cosine[:, BAND:], -sine[:, 1:BAND]], 1)
    right = np.zeros((2 * LANES, PATCH))
    right[:HALF] = cosine.T
    right[LANES : LANES + HALF] = -sine.T
    return stacked(left), split_table(right)


def all_tables():
    mine, outer = column_tables()
    left, right = inverse_tables()
    blocks = [mine, outer[:2], outer[2:], *row_tables(), (left,), right]
    rows = []
    for parts in blocks:
        block = np.zeros((parts[0].shape[0], 2 * WIDE), jnp.bfloat16)
        for at, part in enumerate(parts):
            block[:, at * WIDE : at * WIDE + part.shape[1]] = part
        rows.append(block)
    return np.concatenate(rows, 0)


def dot(left, right):
    return jnp.dot(left, right, preferred_element_type=jnp.float32)


def halves_of(value):
    high = value.astype(jnp.bfloat16)
    return high, (value - high.astype(jnp.float32)).astype(jnp.bfloat16)


def table_first(table, value):
    high, low = halves_of(value)
    return dot(table, jnp.concatenate([high, high, low], 0))


def cross_spectrum(first, second):
    (acc, acs, asc, ass), (bcc, bcs, bsc, bss) = (
        (value[:BAND, :LANES], value[:BAND, LANES:], value[BAND:, :LANES], value[BAND:, LANES:])
        for value in (first, second)
    )
    even_0 = acc * bcc + acs * bcs
    even_1 = asc * bsc + ass * bss
    column_0 = acs * bcc - acc * bcs
    column_1 = ass * bsc - asc * bss
    by_row = asc * bcc - acc * bsc + ass * bcs - acs * bss
    both = acc * bss + ass * bcc - asc * bcs - acs * bsc
    top = SUBLANES
    lone = lax.broadcasted_iota(jnp.int32, (top, LANES), 0) == 0

    def with_top(usual, single):
        return jnp.concatenate([jnp.where(lone, single[:top], usual[:top]), usual[top:]], 0)

    even = with_top(even_0 + even_1, even_0)
    by_row = with_top(by_row, even_1)
    by_column = with_top(column_0 + column_1, column_0)
    both = with_top(both, column_1)
    return jnp.concatenate(
        [jnp.concatenate([even, by_column], 1), jnp.concatenate([by_row, both], 1)], 0
    )


def load_kernel(own_ref, table_ref, own_out, table_out, done):
    copies = [
        pltpu.make_async_copy(source, target, done.at[at])
        for at, (source, target) in enumerate([(own_ref, own_out), (table_ref, table_out)])
    ]
    for copy in copies:
        copy.start()
    for copy in copies:
        copy.wait()


def repeated(tail):
    return jnp.concatenate([tail] * (LANES // (PATCH - LANES)), 1)


def edge_kernel(own_ref, other_ref, out_ref):
    start = pl.multiple_of(jnp.where(lax.axis_index("gz") == 0, PATCH - HALO, 0), HALO // 2)
    rows = [ref[0, pl.ds(start, HALO)].astype(jnp.float32) for ref in (own_ref, other_ref)]
    lane = lax.broadcasted_iota(jnp.int32, (HALO, LANES), 1)
    tails = [repeated(value[:, LANES:]) for value in rows]
    tail = jnp.where(lane < PATCH - LANES, *tails)
    parts = [rows[0][:, :LANES], rows[1][:, :LANES], tail]
    out_ref[...] = jnp.concatenate(parts, 1).astype(jnp.bfloat16)


def edge_rows(beyond_ref):
    tail = beyond_ref[:, 2 * LANES :].astype(jnp.float32)
    turned = pltpu.roll(tail, LANES - (PATCH - LANES), 1)
    return [
        jnp.concatenate(
            [
                beyond_ref[:, image * LANES : (image + 1) * LANES],
                value[:, : PATCH - LANES].astype(jnp.bfloat16),
            ],
            1,
        )
        for image, value in enumerate((tail, turned))
    ]


def side_columns(tiles):
    tiles = [tile.astype(jnp.float32) for tile in tiles]
    wide = [tile[:, :LANES] for tile in tiles]
    narrow = [repeated(tile[:, LANES:]) for tile in tiles]
    lane = lax.broadcasted_iota(jnp.int32, wide[0].shape, 1)
    extra = PATCH - LANES
    low = jnp.where(lane < SIDE, wide[0], pltpu.roll(wide[1], SIDE, 1))
    high = jnp.where(lane < SIDE, pltpu.roll(wide[0], SIDE, 1), wide[1])
    high = jnp.where(lane < extra, narrow[0], high)
    high = jnp.where((lane >= SIDE) & (lane < SIDE + extra), narrow[1], high)
    odd = lax.rem(lax.axis_index("gx"), 2) == 1
    return [jnp.where(odd, *pair).astype(jnp.bfloat16) for pair in ((low, high), (high, low))]


def pack_kernel(own_ref, other_ref, first_ref, second_ref):
    first_ref[:PATCH], second_ref[:PATCH] = side_columns([own_ref[0], other_ref[0]])


def pack_edge_kernel(beyond_ref, first_in, second_in, first_ref, second_ref):
    del first_in, second_in
    first_ref[PATCH:], second_ref[PATCH:] = side_columns(edge_rows(beyond_ref))


def to_row_frequencies(table_ref, half, pixels):
    start = pl.multiple_of(ROWS_AT + half * (2 * PATCH), PATCH)
    high = table_ref[pl.ds(start, 2 * PATCH), :HELD]
    low = table_ref[pl.ds(start, 2 * PATCH), WIDE : WIDE + HELD]
    return dot(high, pixels) + dot(low, pixels)


def finish(columns, side, own_spectra, own_side, beside_ref, table_ref, high_ref, low_ref, rows_ref):
    half = lax.axis_index("gz")
    group = columns // 2
    beside = to_row_frequencies(table_ref, half, beside_ref[...]) - own_side
    lane = lax.broadcasted_iota(jnp.int32, beside.shape, 1)
    parts = []
    for value in (beside, pltpu.roll(beside, SIDE, 1)):
        high = value.astype(jnp.bfloat16).astype(jnp.float32)
        parts.append((high, value - high))
    factors = []
    for image in range(2):
        high = parts[image][0]
        both = jnp.where(lane < SIDE, high, parts[1 - image][1])
        factors.append(jnp.concatenate([both, high[:, :SIDE]], 1).astype(jnp.bfloat16))
    upper = half == 0
    start = pl.multiple_of(HALO_AT + side * (3 * SIDE), SIDE)
    spectra = []
    for column in range(group):
        table = table_ref[pl.ds(start, 3 * SIDE), column * WIDE : (column + 1) * WIDE]
        for section in range(2):
            factor = jnp.where(upper, factors[section], factors[1 - section])
            spot = slice(section * 2 * PATCH, (section + 1) * 2 * PATCH)
            spectra.append(own_spectra[spot] + dot(factor, table))
    left = table_ref[LEFT_AT:RIGHT_AT, : 3 * PATCH]
    right = [table_ref[RIGHT_AT:, start : start + PATCH] for start in (0, WIDE)]
    count = 2 * group
    for patch in range(count):
        row, column = patch % 2, patch // 2
        start = row * PATCH
        cross = cross_spectrum(
            *(value[start : start + PATCH] for value in spectra[2 * column : 2 * column + 2])
        )
        high, low = halves_of(table_first(left, cross))
        high_ref[patch * PATCH : (patch + 1) * PATCH] = high
        low_ref[patch * PATCH : (patch + 1) * PATCH] = low
    for patch in range(count):
        if patch % 2 == 0:
            block = slice(patch * PATCH, (patch + 2) * PATCH)
            correl = dot(high_ref[block], right[0]) + dot(high_ref[block], right[1])
            correl = correl + dot(low_ref[block], right[0])
        squared = correl[patch % 2 * PATCH : (patch % 2 + 1) * PATCH]
        squared = squared * squared
        weights = squared * squared
        pieces = [weights[at : at + SUBLANES] for at in range(0, PATCH, SUBLANES)]
        middle = len(pieces) // 2
        above = pieces[middle - 1]
        ranks = above
        for piece in pieces[middle - 2 : 0 : -1]:
            above = above + piece
            ranks = ranks + above
        below = pieces[middle]
        depths = below
        for piece in pieces[middle + 1 :]:
            below = below + piece
            depths = depths + below
        total = pieces[0] + above + below
        based = float(SUBLANES) * (ranks - depths)
        step = lax.broadcasted_iota(jnp.int32, (SUBLANES, PATCH), 0).astype(jnp.float32)
        based = based + step * total
        rows_ref[0, pl.ds(patch, 1)] = jnp.sum(total, 0, keepdims=True)
        rows_ref[1, pl.ds(patch, 1)] = jnp.sum(based, 0, keepdims=True)
    totals = rows_ref[0]
    shift = lax.broadcasted_iota(jnp.int32, (count, PATCH), 1)
    shift = jnp.where(shift >= PATCH // 2, shift - PATCH, shift).astype(jnp.float32)
    below = jnp.sum(totals, 1, keepdims=True) + EPSILON
    flow_y = jnp.sum(rows_ref[1], 1, keepdims=True) / below
    flow_x = jnp.sum(totals * shift, 1, keepdims=True) / below
    at = lax.broadcasted_iota(jnp.int32, (count, LANES), 1)
    patch = lax.broadcasted_iota(jnp.int32, (count, LANES), 0)
    spot = (patch >> 1) + columns * (patch & 1) + side * group
    line = jnp.where(at == spot, flow_y, 0.0) + jnp.where(at == spot + 2 * count, flow_x, 0.0)
    return jnp.sum(line, 0, keepdims=True)


def early_kernel(columns, own_ref, other_ref, beyond_ref, early_side_ref, late_side_ref, beside_ref,
                 mask_ref, table_ref, line_ref, own_spectra_ref, own_side_ref, high_rows_ref,
                 low_rows_ref, high_ref, low_ref, rows_ref):
    half = lax.axis_index("gz")
    side = 1 - lax.rem(lax.axis_index("gx"), 2)
    tiles = (own_ref[0], other_ref[0])
    images = [jnp.concatenate(pair, 0) for pair in zip(tiles, edge_rows(beyond_ref))]
    upper = half == 0
    one, two = (table_ref[:PATCH, at : at + WIDE] for at in (0, WIDE))
    for section in range(2):
        pixels = jnp.where(upper, images[section], images[1 - section])
        spot = slice(section * 2 * PATCH, (section + 1) * 2 * PATCH)
        high_rows_ref[spot], low_rows_ref[spot] = halves_of(
            to_row_frequencies(table_ref, half, pixels)
        )
        high, low = high_rows_ref[spot], low_rows_ref[spot]
        own_spectra_ref[spot] = dot(high, one) + dot(high, two) + dot(low, one)
    own_side_ref[...] = to_row_frequencies(table_ref, half, late_side_ref[...])
    own_side = to_row_frequencies(table_ref, half, early_side_ref[...])
    line = finish(
        columns, side, own_spectra_ref, own_side, beside_ref, table_ref, high_ref, low_ref, rows_ref
    )
    lanes = lax.broadcasted_iota(jnp.int32, (1, LANES), 1)
    mask = mask_ref[0].astype(jnp.float32)
    for row in range(mask.shape[0]):
        for column in range(columns):
            spot = 4 * columns + row * columns + column
            line = jnp.where(lanes == spot, mask[row : row + 1, column : column + 1], line)
    line_ref[...] = line


def late_kernel(columns, line_ref, own_spectra_ref, own_side_ref, beside_ref, table_ref, out_ref,
                high_ref, low_ref, rows_ref):
    side = lax.rem(lax.axis_index("gx"), 2)
    line = finish(
        columns, side, own_spectra_ref, own_side_ref[...], beside_ref, table_ref, high_ref, low_ref, rows_ref
    )
    out_ref[...] = jnp.broadcast_to(line_ref[...] + line, out_ref.shape)


def relax_kernel(rows, columns, got_ref, flow_ref, offsets_ref):
    size_y, size_x = lax.axis_size("gy"), lax.axis_size("gx")
    half, at_y, at_x = lax.axis_index("gz"), lax.axis_index("gy"), lax.axis_index("gx")
    count = rows * columns
    tile_rows = 2 * rows
    width = columns + 2 * RADIUS
    height = tile_rows + 2 * RADIUS
    per_section = size_y * size_x
    lane = lax.broadcasted_iota(jnp.int32, (1, LANES), 1).astype(jnp.float32)
    line = jnp.floor((lane + 0.5) * (1.0 / width))
    across = lane - line * width
    node_y = line.astype(jnp.int32) - RADIUS + at_y * tile_rows
    node_x = across.astype(jnp.int32) - RADIUS + at_x * columns
    inside = (node_y >= 0) & (node_y < tile_rows * size_y) & (node_x >= 0)
    inside = inside & (node_x < columns * size_x) & (line < height)

    def parts(value, size):
        whole = jnp.floor((value.astype(jnp.float32) + 0.5) * (1.0 / size)).astype(jnp.int32)
        return whole, value - whole * size

    tile_y, in_y = parts(node_y, tile_rows)
    tile_x, in_x = parts(node_x, columns)
    side, in_half = parts(in_y, rows)
    tile = jnp.where(inside, tile_y * size_x + tile_x, -1)
    flow_spot = in_half * columns + in_x
    spots = jnp.concatenate([flow_spot, flow_spot + count, 2 * count + in_y * columns + in_x], 1)
    picked = lax.broadcasted_iota(jnp.int32, (LANES, 3 * LANES), 0) == spots
    picker = picked.astype(jnp.float32).astype(jnp.bfloat16)
    rest = got_ref[...]
    spread = jnp.zeros((rest.shape[0], 3 * LANES), jnp.float32)
    for _ in range(3):
        piece = rest.astype(jnp.bfloat16)
        rest = rest - piece.astype(jnp.float32)
        spread = spread + dot(piece, picker)
    source = lax.broadcasted_iota(jnp.int32, (2 * per_section, LANES), 0)
    chosen = source == side * per_section + tile
    chosen = chosen & (tile >= 0)
    flow_y, flow_x = (
        jnp.sum(jnp.where(chosen, spread[:, axis * LANES : (axis + 1) * LANES], 0.0), 0, keepdims=True)
        for axis in range(2)
    )
    chosen = source[:per_section] == tile
    mask_0, mask_1 = (
        jnp.sum(jnp.where(chosen, spread[start : start + per_section, 2 * LANES :], 0.0), 0, keepdims=True)
        for start in (0, per_section)
    )
    flows = jnp.concatenate([flow_y, flow_x], 0)
    weight = mask_0 * mask_1
    kept = inside.astype(jnp.float32)
    sign = jnp.where(lax.broadcasted_iota(jnp.int32, (4, LANES), 0) < 2, 1.0, -1.0)
    weight = weight * sign
    offsets = jnp.zeros((4, LANES), jnp.float32)
    for step in range(RELAX):
        lower, upper = offsets[:2], offsets[2:]
        pull = upper - lower - flows
        forces = weight * jnp.concatenate([pull, pull], 0)
        if step:
            left = jnp.where(across < 0.5, 0.0, pltpu.roll(offsets, 1, 1))
            right = jnp.where(across > width - 1.5, 0.0, pltpu.roll(offsets, LANES - 1, 1))
            laplace = pltpu.roll(offsets, width, 1) + pltpu.roll(offsets, LANES - width, 1)
            forces = STIFFNESS * (laplace + left + right - 4.0 * offsets) + forces
        offsets = (offsets + STEP_SIZE * forces) * kept
    first = half == 0
    result = jnp.where(first, offsets[:2], offsets[2:])
    flows = jnp.where(first, flows, 0.0)
    for row in range(tile_rows):
        start = (RADIUS + row) * width + RADIUS
        for axis in range(2):
            offsets_ref[axis, 0, pl.ds(row, 1)] = result[axis : axis + 1, start : start + columns]
            flow_ref[axis, 0, pl.ds(row, 1)] = flows[axis : axis + 1, start : start + columns]
    flow_ref[2:] = jnp.zeros((flow_ref.shape[0] - 2, *flow_ref.shape[1:]), jnp.float32)


def vmem(count):
    return [pl.BlockSpec(memory_space=pltpu.VMEM)] * count


def pair_body(images, tissue_mask):
    sections, size_y, size_x = (lax.axis_size(name) for name in ("gz", "gy", "gx"))
    count_y = images.shape[1] // STRIDE
    count_x = images.shape[2] // STRIDE
    rows = count_y // 2
    other = lax.ppermute(images, "gz", [(0, 1), (1, 0)])
    table = jnp.asarray(all_tables())
    own, table = pl.pallas_call(
        load_kernel,
        out_shape=(
            jax.ShapeDtypeStruct(images.shape, images.dtype),
            jax.ShapeDtypeStruct(table.shape, table.dtype),
        ),
        in_specs=[pl.BlockSpec(memory_space=pltpu.HBM)] * 2,
        out_specs=tuple(vmem(2)),
        scratch_shapes=[pltpu.SemaphoreType.DMA((2,))],
        compiler_params=pltpu.CompilerParams(vmem_limit_bytes=4 * 2**20),
        cost_estimate=pl.CostEstimate(flops=0, bytes_accessed=4 * table.size, transcendentals=0),
        name="load",
    )(images, table)
    edge = pl.pallas_call(
        edge_kernel,
        out_shape=jax.ShapeDtypeStruct((HALO, 3 * LANES), jnp.bfloat16),
        in_specs=vmem(2),
        out_specs=vmem(1)[0],
        compiler_params=pltpu.CompilerParams(vmem_limit_bytes=4 * 2**20),
        name="edge",
    )(own, other)
    onward = []
    for tile in range(1, size_y):
        onward += [(tile - 1, tile), (size_y + tile, size_y + tile - 1)]
    beyond = lax.ppermute(edge, ("gz", "gy"), onward)
    swaps = [
        [pair for left in range(offset, size_x - 1, 2) for pair in ((left, left + 1), (left + 1, left))]
        for offset in range(2)
    ]
    packed = jax.ShapeDtypeStruct((HELD, LANES), jnp.bfloat16)
    small = pltpu.CompilerParams(vmem_limit_bytes=4 * 2**20)
    sends = pl.pallas_call(
        pack_kernel,
        out_shape=(packed, packed),
        in_specs=vmem(2),
        out_specs=tuple(vmem(2)),
        compiler_params=small,
        cost_estimate=pl.CostEstimate(flops=10**6, bytes_accessed=2**18, transcendentals=0),
        name="pack",
    )(own, other)
    sends = pl.pallas_call(
        pack_edge_kernel,
        out_shape=(packed, packed),
        in_specs=vmem(3),
        out_specs=tuple(vmem(2)),
        input_output_aliases={1: 0, 2: 1},
        compiler_params=small,
        name="pack_edge",
    )(beyond, *sends)
    first, second = (lax.ppermute(send, "gx", swap) for send, swap in zip(sends, swaps))
    devices = sections * size_y * size_x

    patches = rows * count_x // 2
    common = [
        pltpu.VMEM((patches * PATCH, WIDE), jnp.bfloat16),
        pltpu.VMEM((patches * PATCH, WIDE), jnp.bfloat16),
        pltpu.VMEM((2, patches, PATCH), jnp.float32),
    ]
    params = pltpu.CompilerParams(vmem_limit_bytes=16 * 2**20)
    line, own_spectra, own_side = pl.pallas_call(
        functools.partial(early_kernel, count_x),
        out_shape=(
            jax.ShapeDtypeStruct((1, LANES), jnp.float32),
            jax.ShapeDtypeStruct((4 * PATCH, WIDE), jnp.float32),
            jax.ShapeDtypeStruct((2 * PATCH, LANES), jnp.float32),
        ),
        in_specs=vmem(8),
        out_specs=tuple(vmem(3)),
        scratch_shapes=[pltpu.VMEM((4 * PATCH, PATCH), jnp.bfloat16)] * 2 + common,
        compiler_params=params,
        cost_estimate=pl.CostEstimate(flops=2 * 10**9, bytes_accessed=2**21, transcendentals=0),
        name="early",
    )(own, other, beyond, sends[1], sends[0], first, tissue_mask, table)
    lines = pl.pallas_call(
        functools.partial(late_kernel, count_x),
        out_shape=jax.ShapeDtypeStruct((devices, LANES), jnp.float32),
        in_specs=vmem(5),
        out_specs=vmem(1)[0],
        scratch_shapes=common,
        compiler_params=params,
        cost_estimate=pl.CostEstimate(flops=10**9, bytes_accessed=2**21, transcendentals=0),
        name="late",
    )(line, own_spectra, own_side, second, table)
    got = lax.all_to_all(lines, ("gz", "gy", "gx"), 0, 0, tiled=True)
    return pl.pallas_call(
        functools.partial(relax_kernel, rows, count_x),
        out_shape=(
            jax.ShapeDtypeStruct((4, 1, count_y, count_x), jnp.float32),
            jax.ShapeDtypeStruct((2, 1, count_y, count_x), jnp.float32),
        ),
        in_specs=vmem(1),
        out_specs=tuple(vmem(2)),
        compiler_params=pltpu.CompilerParams(vmem_limit_bytes=4 * 2**20),
        name="relax",
    )(got)


def body(images, tissue_mask):
    paired = lax.axis_size("gz") == 2 and images.shape == (1, PATCH, PATCH)
    return (pair_body if paired else general_body)(images, tissue_mask)


def solution(mesh):
    placed = (P("gz", "gy", "gx"), P("gz", "gy", "gx"))
    return jax.shard_map(
        body,
        mesh=mesh,
        in_specs=placed,
        out_specs=(P(None, "gz", "gy", "gx"), P(None, "gz", "gy", "gx")),
        check_vma=False,
    )
```

```python
import functools
import math

import jax
import jax.numpy as jnp
import numpy as np
from jax import lax
from jax.experimental import pallas as pl
from jax.experimental.pallas import tpu as pltpu
from jax.sharding import PartitionSpec as P

PATCH = 160
STRIDE = 40
RELAX = 4


EPSILON = 1e-06
STIFFNESS = 0.5
STEP_SIZE = 0.2


def shifted(value, axis, steps):
    count = lax.axis_size(axis)
    initial, last = (max(0, -steps), min(count, count - steps))
    return lax.ppermute(value, axis, [(source, source + steps) for source in range(initial, last)])


def padded_2(x, sides, width):
    for axis, dim in sides:
        size, length = (lax.axis_size(axis), x.shape[dim])
        up = [(i, (i + 1) % size) for i in range(size - 1)]
        down = [(j, i) for i, j in up]
        last = lax.slice_in_dim(x, length - width, length, axis=dim)
        initial = lax.slice_in_dim(x, 0, width, axis=dim)
        before = lax.ppermute(last, axis, up)
        after = lax.ppermute(initial, axis, down)
        x = jnp.concatenate([before, x, after], axis=dim)
    return x


def windows(section):
    repeats = PATCH // STRIDE
    count_y = section.shape[0] // STRIDE - repeats + 1
    count_x = section.shape[1] // STRIDE - repeats + 1
    blocks = section.reshape(section.shape[0] // STRIDE, STRIDE, section.shape[1] // STRIDE, STRIDE)
    pieces = []
    for first in range(repeats):
        row_pieces = [
            blocks[first : first + count_y, :, second : second + count_x, :]
            for second in range(repeats)
        ]
        pieces.append(jnp.stack(row_pieces, 0))
    stacked = jnp.stack(pieces, 0)
    stacked = jnp.transpose(stacked, (2, 4, 0, 3, 1, 5))
    return stacked.reshape(count_y * count_x, PATCH, PATCH)


def tables():
    indices = jnp.arange(PATCH, dtype=jnp.int32)
    phases = indices[:, None] * indices[None, :] % PATCH
    angles = phases.astype(jnp.float32) * (2.0 * math.pi / PATCH)
    cosine_table = jnp.cos(angles)
    sine_table = jnp.sin(angles)
    left_table = jnp.concatenate([cosine_table, sine_table], 0)
    right_table = jnp.concatenate([cosine_table, sine_table], 1)
    return (left_table, right_table)


def spectrum(section, left_table, right_table):
    patches = windows(section)
    halfway = jnp.einsum("pnm,mk->pnk", patches, right_table, precision=lax.Precision.HIGHEST)
    products = jnp.einsum("kn,pnm->pkm", left_table, halfway, precision=lax.Precision.HIGHEST)
    cos_a = products[:, :PATCH, :PATCH]
    cos_b = products[:, :PATCH, PATCH:]
    sin_a = products[:, PATCH:, :PATCH]
    sin_b = products[:, PATCH:, PATCH:]
    return (cos_a - sin_b, -(cos_b + sin_a))


def flow_between(own_re, own_im, next_re, next_im, left_table, count_y, count_x):
    cross_re = next_re * own_re + next_im * own_im
    cross_im = next_im * own_re - next_re * own_im
    stacked = jnp.concatenate([cross_re, cross_im], 2)
    products = jnp.einsum("kn,pnm->pkm", left_table, stacked, precision=lax.Precision.HIGHEST)
    mixed_re = products[:, :PATCH, :PATCH] - products[:, PATCH:, PATCH:]
    mixed_im = products[:, :PATCH, PATCH:] + products[:, PATCH:, :PATCH]
    joined = jnp.concatenate([mixed_re, -mixed_im], 2)
    correl = jnp.einsum("pnm,mk->pnk", joined, left_table, precision=lax.Precision.HIGHEST) / (
        PATCH * PATCH
    )
    squared = correl * correl
    weights = squared * squared
    totals = jnp.sum(weights, axis=(1, 2)) + EPSILON
    shifts = ((jnp.arange(PATCH, dtype=jnp.int32) + PATCH // 2) % PATCH - PATCH // 2).astype(
        jnp.float32
    )
    flow_y = jnp.sum(weights * shifts[None, :, None], axis=(1, 2)) / totals
    flow_x = jnp.sum(weights * shifts[None, None, :], axis=(1, 2)) / totals
    return jnp.stack([flow_y, flow_x], 0).reshape(2, count_y, count_x)


def laplacian(widened, offsets):
    return (
        widened[:, :, :-2, 1:-1]
        + widened[:, :, 2:, 1:-1]
        + widened[:, :, 1:-1, :-2]
        + widened[:, :, 1:-1, 2:]
        - 4.0 * offsets
    )


def remote_neighbours(offsets):
    up_one = shifted(offsets, "gz", -1)
    up_two = shifted(offsets, "gz", -2)
    down_one = shifted(offsets, "gz", 1)
    down_two = shifted(offsets, "gz", 2)
    return (up_one, up_two, down_one, down_two)


def mesh_step(offsets, laplace, coeffs):
    up_one, up_two, down_one, down_two = remote_neighbours(offsets)
    forces = STIFFNESS * laplace
    forces = forces + coeffs[2:3] * (up_one - offsets - coeffs[0:2])
    forces = forces + coeffs[5:6] * (up_two - offsets - coeffs[3:5])
    forces = forces - coeffs[8:9] * (offsets - down_one - coeffs[6:8])
    forces = forces - coeffs[11:12] * (offsets - down_two - coeffs[9:11])
    return offsets + STEP_SIZE * forces


def general_body(images, tissue_mask):
    margin = (PATCH - STRIDE) // 2
    count_y = images.shape[1] // STRIDE
    count_x = images.shape[2] // STRIDE
    padded = padded_2(images, (("gy", 1), ("gx", 2)), margin)
    left_table, right_table = tables()
    own_mask = tissue_mask.astype(jnp.float32)
    own_re, own_im = spectrum(padded[0].astype(jnp.float32), left_table, right_table)
    next_re, next_im, next_mask = shifted((own_re, own_im, own_mask), "gz", -1)
    far_re, far_im, far_mask = shifted((own_re, own_im, own_mask), "gz", -2)
    flow_one = flow_between(own_re, own_im, next_re, next_im, left_table, count_y, count_x)
    flow_two = flow_between(own_re, own_im, far_re, far_im, left_table, count_y, count_x)
    weight_one = own_mask * next_mask
    weight_two = own_mask * far_mask
    low_flow_one, low_weight_one = shifted((flow_one, weight_one), "gz", 1)
    low_flow_two, low_weight_two = shifted((flow_two, weight_two), "gz", 2)
    coeffs = jnp.concatenate(
        [
            flow_one,
            weight_one,
            flow_two,
            weight_two,
            low_flow_one,
            low_weight_one,
            low_flow_two,
            low_weight_two,
        ],
        0,
    )[:, None]
    spread = padded_2(coeffs, (("gy", 2), ("gx", 3)), RELAX)
    global_y = lax.axis_index("gy") * count_y + jnp.arange(-RELAX, count_y + RELAX, dtype=jnp.int32)
    global_x = lax.axis_index("gx") * count_x + jnp.arange(-RELAX, count_x + RELAX, dtype=jnp.int32)
    inside_y = (global_y >= 0) & (global_y < count_y * lax.axis_size("gy"))
    inside_x = (global_x >= 0) & (global_x < count_x * lax.axis_size("gx"))
    inside = (inside_y[:, None] & inside_x[None, :]).astype(jnp.float32)
    offsets = jnp.zeros((2, 1, count_y + 2 * RELAX, count_x + 2 * RELAX), jnp.float32)
    for _ in range(RELAX):
        widened = jnp.pad(offsets, ((0, 0), (0, 0), (1, 1), (1, 1)))
        offsets = mesh_step(offsets, laplacian(widened, offsets), spread) * inside[None, None]
    offsets = offsets[:, :, RELAX : RELAX + count_y, RELAX : RELAX + count_x]
    flow_fields = jnp.concatenate([flow_one, flow_two], 0)[:, None]
    return (flow_fields, offsets)


MARGIN = (PATCH - STRIDE) // 2
HALF = PATCH // 2 + 1
LANES = 128
SUBLANES = 8
BAND = HALF - 1
HALO = -(-MARGIN // 16) * 16
RADIUS = RELAX - 1
WIDE = 2 * LANES
HELD = PATCH + HALO
SIDE = LANES // 2
HALO_AT = PATCH
ROWS_AT = HALO_AT + 2 * 3 * SIDE
LEFT_AT = ROWS_AT + 2 * 2 * PATCH
RIGHT_AT = LEFT_AT + PATCH


def split_table(table):
    high = table.astype(jnp.bfloat16)
    low = (table - high.astype(np.float64)).astype(jnp.bfloat16)
    return np.stack([high, low])


def trig(first, second):
    angle = 2.0 * np.pi / PATCH * ((first[:, None] * second[None, :]) % PATCH)
    return np.cos(angle), np.sin(angle)


def column_tables():
    cosine, sine = trig(np.arange(PATCH), np.arange(HALF))
    table = np.zeros((PATCH, WIDE))
    table[:, :HALF] = cosine
    table[:, LANES : LANES + HALF] = sine
    spot = np.arange(SIDE)
    before = np.where(spot < PATCH - LANES, LANES + spot, SIDE + spot)
    outer = []
    for window in range(PATCH // STRIDE):
        start = window * STRIDE - MARGIN
        column = before if start < 0 else spot
        used = column >= start + PATCH if start < 0 else column < start
        high, low = split_table(table[column] * used[:, None])
        outer.append(np.concatenate([high, high, low], 0))
    return split_table(table), outer


def stacked(table):
    high, low = split_table(table)
    return np.concatenate([high, low, high], 1)


def frequency_rows(positions):
    cosine, sine = trig(np.arange(HALF), positions)
    return np.concatenate([cosine[:BAND], cosine[BAND:], sine[1:BAND]], 0)


def row_tables():
    tables = []
    for half in range(2):
        first = PATCH - HALO if half == 0 else 0
        position = np.concatenate([np.arange(PATCH), first + np.arange(HALO)])
        image_row = position + np.where(np.arange(HELD) < PATCH, 0, -PATCH if half == 0 else PATCH)
        rows = frequency_rows(position)
        windows = []
        for window in (2 * half, 2 * half + 1):
            start = window * STRIDE - MARGIN
            windows.append(rows * ((image_row >= start) & (image_row < start + PATCH)))
        tables.append(split_table(np.concatenate(windows, 0)))
    return tables


def inverse_tables():
    cosine, sine = trig(np.arange(PATCH), np.arange(HALF))
    weight = np.full((HALF,), 2.0 / PATCH)
    weight[0] = weight[-1] = 1.0 / PATCH
    cosine, sine = cosine * weight, sine * weight
    left = np.concatenate([cosine[:, :BAND], cosine[:, BAND:], -sine[:, 1:BAND]], 1)
    right = np.zeros((2 * LANES, PATCH))
    right[:HALF] = cosine.T
    right[LANES : LANES + HALF] = -sine.T
    return stacked(left), split_table(right)


def all_tables():
    mine, outer = column_tables()
    left, right = inverse_tables()
    blocks = [mine, outer[:2], outer[2:], *row_tables(), (left,), right]
    rows = []
    for parts in blocks:
        block = np.zeros((parts[0].shape[0], 2 * WIDE), jnp.bfloat16)
        for at, part in enumerate(parts):
            block[:, at * WIDE : at * WIDE + part.shape[1]] = part
        rows.append(block)
    return np.concatenate(rows, 0)


def dot(left, right):
    return jnp.dot(left, right, preferred_element_type=jnp.float32)


def halves_of(value):
    high = value.astype(jnp.bfloat16)
    return high, (value - high.astype(jnp.float32)).astype(jnp.bfloat16)


def table_first(table, value):
    high, low = halves_of(value)
    return dot(table, jnp.concatenate([high, high, low], 0))


def cross_spectrum(first, second):
    (acc, acs, asc, ass), (bcc, bcs, bsc, bss) = (
        (value[:BAND, :LANES], value[:BAND, LANES:], value[BAND:, :LANES], value[BAND:, LANES:])
        for value in (first, second)
    )
    even_0 = acc * bcc + acs * bcs
    even_1 = asc * bsc + ass * bss
    column_0 = acs * bcc - acc * bcs
    column_1 = ass * bsc - asc * bss
    by_row = asc * bcc - acc * bsc + ass * bcs - acs * bss
    both = acc * bss + ass * bcc - asc * bcs - acs * bsc
    top = SUBLANES
    lone = lax.broadcasted_iota(jnp.int32, (top, LANES), 0) == 0

    def with_top(usual, single):
        return jnp.concatenate([jnp.where(lone, single[:top], usual[:top]), usual[top:]], 0)

    even = with_top(even_0 + even_1, even_0)
    by_row = with_top(by_row, even_1)
    by_column = with_top(column_0 + column_1, column_0)
    both = with_top(both, column_1)
    return jnp.concatenate(
        [jnp.concatenate([even, by_column], 1), jnp.concatenate([by_row, both], 1)], 0
    )


def load_kernel(own_ref, table_ref, own_out, table_out, done):
    copies = [
        pltpu.make_async_copy(source, target, done.at[at])
        for at, (source, target) in enumerate([(own_ref, own_out), (table_ref, table_out)])
    ]
    for copy in copies:
        copy.start()
    for copy in copies:
        copy.wait()


def repeated(tail):
    return jnp.concatenate([tail] * (LANES // (PATCH - LANES)), 1)


def edge_kernel(own_ref, other_ref, out_ref):
    start = pl.multiple_of(jnp.where(lax.axis_index("gz") == 0, PATCH - HALO, 0), HALO // 2)
    rows = [ref[0, pl.ds(start, HALO)].astype(jnp.float32) for ref in (own_ref, other_ref)]
    lane = lax.broadcasted_iota(jnp.int32, (HALO, LANES), 1)
    tails = [repeated(value[:, LANES:]) for value in rows]
    tail = jnp.where(lane < PATCH - LANES, *tails)
    parts = [rows[0][:, :LANES], rows[1][:, :LANES], tail]
    out_ref[...] = jnp.concatenate(parts, 1).astype(jnp.bfloat16)


def edge_rows(beyond_ref):
    tail = beyond_ref[:, 2 * LANES :].astype(jnp.float32)
    turned = pltpu.roll(tail, LANES - (PATCH - LANES), 1)
    return [
        jnp.concatenate(
            [
                beyond_ref[:, image * LANES : (image + 1) * LANES],
                value[:, : PATCH - LANES].astype(jnp.bfloat16),
            ],
            1,
        )
        for image, value in enumerate((tail, turned))
    ]


def side_columns(tiles):
    tiles = [tile.astype(jnp.float32) for tile in tiles]
    wide = [tile[:, :LANES] for tile in tiles]
    narrow = [repeated(tile[:, LANES:]) for tile in tiles]
    lane = lax.broadcasted_iota(jnp.int32, wide[0].shape, 1)
    extra = PATCH - LANES
    low = jnp.where(lane < SIDE, wide[0], pltpu.roll(wide[1], SIDE, 1))
    high = jnp.where(lane < SIDE, pltpu.roll(wide[0], SIDE, 1), wide[1])
    high = jnp.where(lane < extra, narrow[0], high)
    high = jnp.where((lane >= SIDE) & (lane < SIDE + extra), narrow[1], high)
    odd = lax.rem(lax.axis_index("gx"), 2) == 1
    return [jnp.where(odd, *pair).astype(jnp.bfloat16) for pair in ((low, high), (high, low))]


def pack_kernel(own_ref, other_ref, first_ref, second_ref):
    first_ref[:PATCH], second_ref[:PATCH] = side_columns([own_ref[0], other_ref[0]])


def pack_edge_kernel(beyond_ref, first_in, second_in, first_ref, second_ref):
    del first_in, second_in
    first_ref[PATCH:], second_ref[PATCH:] = side_columns(edge_rows(beyond_ref))


def to_row_frequencies(table_ref, half, pixels):
    start = pl.multiple_of(ROWS_AT + half * (2 * PATCH), HALO // 2)
    high = table_ref[pl.ds(start, 2 * PATCH), :HELD]
    low = table_ref[pl.ds(start, 2 * PATCH), WIDE : WIDE + HELD]
    return dot(high, pixels) + dot(low, pixels)


def finish(columns, side, own_spectra, own_side, beside_ref, table_ref, high_ref, low_ref, rows_ref):
    half = lax.axis_index("gz")
    group = columns // 2
    beside = to_row_frequencies(table_ref, half, beside_ref[...]) - own_side
    lane = lax.broadcasted_iota(jnp.int32, beside.shape, 1)
    parts = []
    for value in (beside, pltpu.roll(beside, SIDE, 1)):
        high = value.astype(jnp.bfloat16).astype(jnp.float32)
        parts.append((high, value - high))
    factors = []
    for image in range(2):
        high = parts[image][0]
        both = jnp.where(lane < SIDE, high, parts[1 - image][1])
        factors.append(jnp.concatenate([both, high[:, :SIDE]], 1).astype(jnp.bfloat16))
    upper = half == 0
    start = pl.multiple_of(HALO_AT + side * (3 * SIDE), HALO // 2)
    spectra = []
    for column in range(group):
        table = table_ref[pl.ds(start, 3 * SIDE), column * WIDE : (column + 1) * WIDE]
        for section in range(2):
            factor = jnp.where(upper, factors[section], factors[1 - section])
            spot = slice(section * 2 * PATCH, (section + 1) * 2 * PATCH)
            spectra.append(own_spectra[spot] + dot(factor, table))
    left = table_ref[LEFT_AT:RIGHT_AT, : 3 * PATCH]
    right = [table_ref[RIGHT_AT:, start : start + PATCH] for start in (0, WIDE)]
    count = 2 * group
    for patch in range(count):
        row, column = patch % 2, patch // 2
        start = row * PATCH
        cross = cross_spectrum(
            *(value[start : start + PATCH] for value in spectra[2 * column : 2 * column + 2])
        )
        high, low = halves_of(table_first(left, cross))
        high_ref[patch * PATCH : (patch + 1) * PATCH] = high
        low_ref[patch * PATCH : (patch + 1) * PATCH] = low
    for patch in range(count):
        if patch % 2 == 0:
            block = slice(patch * PATCH, (patch + 2) * PATCH)
            correl = dot(high_ref[block], right[0]) + dot(high_ref[block], right[1])
            correl = correl + dot(low_ref[block], right[0])
        squared = correl[patch % 2 * PATCH : (patch % 2 + 1) * PATCH]
        squared = squared * squared
        weights = squared * squared
        pieces = [weights[at : at + SUBLANES] for at in range(0, PATCH, SUBLANES)]
        middle = len(pieces) // 2
        above = pieces[middle - 1]
        ranks = above
        for piece in pieces[middle - 2 : 0 : -1]:
            above = above + piece
            ranks = ranks + above
        below = pieces[middle]
        depths = below
        for piece in pieces[middle + 1 :]:
            below = below + piece
            depths = depths + below
        total = pieces[0] + above + below
        based = float(SUBLANES) * (ranks - depths)
        step = lax.broadcasted_iota(jnp.int32, (SUBLANES, PATCH), 0).astype(jnp.float32)
        based = based + step * total
        rows_ref[0, pl.ds(patch, 1)] = jnp.sum(total, 0, keepdims=True)
        rows_ref[1, pl.ds(patch, 1)] = jnp.sum(based, 0, keepdims=True)
    totals = rows_ref[0]
    shift = lax.broadcasted_iota(jnp.int32, (count, PATCH), 1)
    shift = jnp.where(shift >= PATCH // 2, shift - PATCH, shift).astype(jnp.float32)
    below = jnp.sum(totals, 1, keepdims=True) + EPSILON
    flow_y = jnp.sum(rows_ref[1], 1, keepdims=True) / below
    flow_x = jnp.sum(totals * shift, 1, keepdims=True) / below
    at = lax.broadcasted_iota(jnp.int32, (count, LANES), 1)
    patch = lax.broadcasted_iota(jnp.int32, (count, LANES), 0)
    spot = (patch >> 1) + columns * (patch & 1) + side * group
    line = jnp.where(at == spot, flow_y, 0.0) + jnp.where(at == spot + 2 * count, flow_x, 0.0)
    return jnp.sum(line, 0, keepdims=True)


def early_kernel(columns, own_ref, other_ref, beyond_ref, early_side_ref, late_side_ref, beside_ref,
                 mask_ref, table_ref, line_ref, own_spectra_ref, own_side_ref, high_rows_ref,
                 low_rows_ref, high_ref, low_ref, rows_ref):
    half = lax.axis_index("gz")
    side = 1 - lax.rem(lax.axis_index("gx"), 2)
    tiles = (own_ref[0], other_ref[0])
    images = [jnp.concatenate(pair, 0) for pair in zip(tiles, edge_rows(beyond_ref))]
    upper = half == 0
    one, two = (table_ref[:PATCH, at : at + WIDE] for at in (0, WIDE))
    for section in range(2):
        pixels = jnp.where(upper, images[section], images[1 - section])
        spot = slice(section * 2 * PATCH, (section + 1) * 2 * PATCH)
        high_rows_ref[spot], low_rows_ref[spot] = halves_of(
            to_row_frequencies(table_ref, half, pixels)
        )
        high, low = high_rows_ref[spot], low_rows_ref[spot]
        own_spectra_ref[spot] = dot(high, one) + dot(high, two) + dot(low, one)
    own_side_ref[...] = to_row_frequencies(table_ref, half, late_side_ref[...])
    own_side = to_row_frequencies(table_ref, half, early_side_ref[...])
    line = finish(
        columns, side, own_spectra_ref, own_side, beside_ref, table_ref, high_ref, low_ref, rows_ref
    )
    lanes = lax.broadcasted_iota(jnp.int32, (1, LANES), 1)
    mask = mask_ref[0].astype(jnp.float32)
    for row in range(mask.shape[0]):
        for column in range(columns):
            spot = 4 * columns + row * columns + column
            line = jnp.where(lanes == spot, mask[row : row + 1, column : column + 1], line)
    line_ref[...] = line


def late_kernel(columns, line_ref, own_spectra_ref, own_side_ref, beside_ref, table_ref, out_ref,
                high_ref, low_ref, rows_ref):
    side = lax.rem(lax.axis_index("gx"), 2)
    line = finish(
        columns, side, own_spectra_ref, own_side_ref[...], beside_ref, table_ref, high_ref, low_ref, rows_ref
    )
    out_ref[...] = jnp.broadcast_to(line_ref[...] + line, out_ref.shape)


def relax_kernel(rows, columns, got_ref, flow_ref, offsets_ref):
    size_y, size_x = lax.axis_size("gy"), lax.axis_size("gx")
    half, at_y, at_x = lax.axis_index("gz"), lax.axis_index("gy"), lax.axis_index("gx")
    count = rows * columns
    tile_rows = 2 * rows
    width = columns + 2 * RADIUS
    height = tile_rows + 2 * RADIUS
    per_section = size_y * size_x
    lane = lax.broadcasted_iota(jnp.int32, (1, LANES), 1).astype(jnp.float32)
    line = jnp.floor((lane + 0.5) * (1.0 / width))
    across = lane - line * width
    node_y = line.astype(jnp.int32) - RADIUS + at_y * tile_rows
    node_x = across.astype(jnp.int32) - RADIUS + at_x * columns
    inside = (node_y >= 0) & (node_y < tile_rows * size_y) & (node_x >= 0)
    inside = inside & (node_x < columns * size_x) & (line < height)

    def parts(value, size):
        whole = jnp.floor((value.astype(jnp.float32) + 0.5) * (1.0 / size)).astype(jnp.int32)
        return whole, value - whole * size

    tile_y, in_y = parts(node_y, tile_rows)
    tile_x, in_x = parts(node_x, columns)
    side, in_half = parts(in_y, rows)
    tile = jnp.where(inside, tile_y * size_x + tile_x, -1)
    flow_spot = in_half * columns + in_x
    spots = jnp.concatenate([flow_spot, flow_spot + count, 2 * count + in_y * columns + in_x], 1)
    picked = lax.broadcasted_iota(jnp.int32, (LANES, 3 * LANES), 0) == spots
    picker = picked.astype(jnp.float32).astype(jnp.bfloat16)
    rest = got_ref[...]
    spread = jnp.zeros((rest.shape[0], 3 * LANES), jnp.float32)
    for _ in range(3):
        piece = rest.astype(jnp.bfloat16)
        rest = rest - piece.astype(jnp.float32)
        spread = spread + dot(piece, picker)
    source = lax.broadcasted_iota(jnp.int32, (2 * per_section, LANES), 0)
    chosen = source == side * per_section + tile
    chosen = chosen & (tile >= 0)
    flow_y, flow_x = (
        jnp.sum(jnp.where(chosen, spread[:, axis * LANES : (axis + 1) * LANES], 0.0), 0, keepdims=True)
        for axis in range(2)
    )
    chosen = source[:per_section] == tile
    mask_0, mask_1 = (
        jnp.sum(jnp.where(chosen, spread[start : start + per_section, 2 * LANES :], 0.0), 0, keepdims=True)
        for start in (0, per_section)
    )
    flows = jnp.concatenate([flow_y, flow_x], 0)
    weight = mask_0 * mask_1
    kept = inside.astype(jnp.float32)
    sign = jnp.where(lax.broadcasted_iota(jnp.int32, (4, LANES), 0) < 2, 1.0, -1.0)
    weight = weight * sign
    offsets = jnp.zeros((4, LANES), jnp.float32)
    for step in range(RELAX):
        lower, upper = offsets[:2], offsets[2:]
        pull = upper - lower - flows
        forces = weight * jnp.concatenate([pull, pull], 0)
        if step:
            left = jnp.where(across < 0.5, 0.0, pltpu.roll(offsets, 1, 1))
            right = jnp.where(across > width - 1.5, 0.0, pltpu.roll(offsets, LANES - 1, 1))
            laplace = pltpu.roll(offsets, width, 1) + pltpu.roll(offsets, LANES - width, 1)
            forces = STIFFNESS * (laplace + left + right - 4.0 * offsets) + forces
        offsets = (offsets + STEP_SIZE * forces) * kept
    first = half == 0
    result = jnp.where(first, offsets[:2], offsets[2:])
    flows = jnp.where(first, flows, 0.0)
    for row in range(tile_rows):
        start = (RADIUS + row) * width + RADIUS
        for axis in range(2):
            offsets_ref[axis, 0, pl.ds(row, 1)] = result[axis : axis + 1, start : start + columns]
            flow_ref[axis, 0, pl.ds(row, 1)] = flows[axis : axis + 1, start : start + columns]
    flow_ref[2:] = jnp.zeros((flow_ref.shape[0] - 2, *flow_ref.shape[1:]), jnp.float32)


def vmem(count):
    return [pl.BlockSpec(memory_space=pltpu.VMEM)] * count


def pair_body(images, tissue_mask):
    sections, size_y, size_x = (lax.axis_size(name) for name in ("gz", "gy", "gx"))
    count_y = images.shape[1] // STRIDE
    count_x = images.shape[2] // STRIDE
    rows = count_y // 2
    other = lax.ppermute(images, "gz", [(0, 1), (1, 0)])
    table = jnp.asarray(all_tables())
    own, table = pl.pallas_call(
        load_kernel,
        out_shape=(
            jax.ShapeDtypeStruct(images.shape, images.dtype),
            jax.ShapeDtypeStruct(table.shape, table.dtype),
        ),
        in_specs=[pl.BlockSpec(memory_space=pltpu.HBM)] * 2,
        out_specs=tuple(vmem(2)),
        scratch_shapes=[pltpu.SemaphoreType.DMA((2,))],
        compiler_params=pltpu.CompilerParams(vmem_limit_bytes=4 * 2**20),
        cost_estimate=pl.CostEstimate(flops=0, bytes_accessed=4 * table.size, transcendentals=0),
        name="load",
    )(images, table)
    edge = pl.pallas_call(
        edge_kernel,
        out_shape=jax.ShapeDtypeStruct((HALO, 3 * LANES), jnp.bfloat16),
        in_specs=vmem(2),
        out_specs=vmem(1)[0],
        compiler_params=pltpu.CompilerParams(vmem_limit_bytes=4 * 2**20),
        name="edge",
    )(own, other)
    onward = []
    for tile in range(1, size_y):
        onward += [(tile - 1, tile), (size_y + tile, size_y + tile - 1)]
    beyond = lax.ppermute(edge, ("gz", "gy"), onward)
    swaps = [
        [pair for left in range(offset, size_x - 1, 2) for pair in ((left, left + 1), (left + 1, left))]
        for offset in range(2)
    ]
    packed = jax.ShapeDtypeStruct((HELD, LANES), jnp.bfloat16)
    small = pltpu.CompilerParams(vmem_limit_bytes=4 * 2**20)
    sends = pl.pallas_call(
        pack_kernel,
        out_shape=(packed, packed),
        in_specs=vmem(2),
        out_specs=tuple(vmem(2)),
        compiler_params=small,
        cost_estimate=pl.CostEstimate(flops=10**6, bytes_accessed=2**18, transcendentals=0),
        name="pack",
    )(own, other)
    sends = pl.pallas_call(
        pack_edge_kernel,
        out_shape=(packed, packed),
        in_specs=vmem(3),
        out_specs=tuple(vmem(2)),
        input_output_aliases={1: 0, 2: 1},
        compiler_params=small,
        name="pack_edge",
    )(beyond, *sends)
    first, second = (lax.ppermute(send, "gx", swap) for send, swap in zip(sends, swaps))
    devices = sections * size_y * size_x

    patches = rows * count_x // 2
    common = [
        pltpu.VMEM((patches * PATCH, WIDE), jnp.bfloat16),
        pltpu.VMEM((patches * PATCH, WIDE), jnp.bfloat16),
        pltpu.VMEM((2, patches, PATCH), jnp.float32),
    ]
    params = pltpu.CompilerParams(vmem_limit_bytes=16 * 2**20)
    line, own_spectra, own_side = pl.pallas_call(
        functools.partial(early_kernel, count_x),
        out_shape=(
            jax.ShapeDtypeStruct((1, LANES), jnp.float32),
            jax.ShapeDtypeStruct((4 * PATCH, WIDE), jnp.float32),
            jax.ShapeDtypeStruct((2 * PATCH, LANES), jnp.float32),
        ),
        in_specs=vmem(8),
        out_specs=tuple(vmem(3)),
        scratch_shapes=[pltpu.VMEM((4 * PATCH, PATCH), jnp.bfloat16)] * 2 + common,
        compiler_params=params,
        cost_estimate=pl.CostEstimate(flops=2 * 10**9, bytes_accessed=2**21, transcendentals=0),
        name="early",
    )(own, other, beyond, sends[1], sends[0], first, tissue_mask, table)
    lines = pl.pallas_call(
        functools.partial(late_kernel, count_x),
        out_shape=jax.ShapeDtypeStruct((devices, LANES), jnp.float32),
        in_specs=vmem(5),
        out_specs=vmem(1)[0],
        scratch_shapes=common,
        compiler_params=params,
        cost_estimate=pl.CostEstimate(flops=10**9, bytes_accessed=2**21, transcendentals=0),
        name="late",
    )(line, own_spectra, own_side, second, table)
    got = lax.all_to_all(lines, ("gz", "gy", "gx"), 0, 0, tiled=True)
    return pl.pallas_call(
        functools.partial(relax_kernel, rows, count_x),
        out_shape=(
            jax.ShapeDtypeStruct((4, 1, count_y, count_x), jnp.float32),
            jax.ShapeDtypeStruct((2, 1, count_y, count_x), jnp.float32),
        ),
        in_specs=vmem(1),
        out_specs=tuple(vmem(2)),
        compiler_params=pltpu.CompilerParams(vmem_limit_bytes=4 * 2**20),
        name="relax",
    )(got)


def body(images, tissue_mask):
    paired = lax.axis_size("gz") == 2 and images.shape == (1, PATCH, PATCH)
    return (pair_body if paired else general_body)(images, tissue_mask)


def solution(mesh):
    placed = (P("gz", "gy", "gx"), P("gz", "gy", "gx"))
    return jax.shard_map(
        body,
        mesh=mesh,
        in_specs=placed,
        out_specs=(P(None, "gz", "gy", "gx"), P(None, "gz", "gy", "gx")),
        check_vma=False,
    )
```

```python
import functools
import math

import jax
import jax.numpy as jnp
import numpy as np
from jax import lax
from jax.experimental import pallas as pl
from jax.experimental.pallas import tpu as pltpu
from jax.sharding import PartitionSpec as P

PATCH = 160
STRIDE = 40
RELAX = 4


EPSILON = 1e-06
STIFFNESS = 0.5
STEP_SIZE = 0.2


def shifted(value, axis, steps):
    count = lax.axis_size(axis)
    initial, last = (max(0, -steps), min(count, count - steps))
    return lax.ppermute(value, axis, [(source, source + steps) for source in range(initial, last)])


def padded_2(x, sides, width):
    for axis, dim in sides:
        size, length = (lax.axis_size(axis), x.shape[dim])
        up = [(i, (i + 1) % size) for i in range(size - 1)]
        down = [(j, i) for i, j in up]
        last = lax.slice_in_dim(x, length - width, length, axis=dim)
        initial = lax.slice_in_dim(x, 0, width, axis=dim)
        before = lax.ppermute(last, axis, up)
        after = lax.ppermute(initial, axis, down)
        x = jnp.concatenate([before, x, after], axis=dim)
    return x


def windows(section):
    repeats = PATCH // STRIDE
    count_y = section.shape[0] // STRIDE - repeats + 1
    count_x = section.shape[1] // STRIDE - repeats + 1
    blocks = section.reshape(section.shape[0] // STRIDE, STRIDE, section.shape[1] // STRIDE, STRIDE)
    pieces = []
    for first in range(repeats):
        row_pieces = [
            blocks[first : first + count_y, :, second : second + count_x, :]
            for second in range(repeats)
        ]
        pieces.append(jnp.stack(row_pieces, 0))
    stacked = jnp.stack(pieces, 0)
    stacked = jnp.transpose(stacked, (2, 4, 0, 3, 1, 5))
    return stacked.reshape(count_y * count_x, PATCH, PATCH)


def tables():
    indices = jnp.arange(PATCH, dtype=jnp.int32)
    phases = indices[:, None] * indices[None, :] % PATCH
    angles = phases.astype(jnp.float32) * (2.0 * math.pi / PATCH)
    cosine_table = jnp.cos(angles)
    sine_table = jnp.sin(angles)
    left_table = jnp.concatenate([cosine_table, sine_table], 0)
    right_table = jnp.concatenate([cosine_table, sine_table], 1)
    return (left_table, right_table)


def spectrum(section, left_table, right_table):
    patches = windows(section)
    halfway = jnp.einsum("pnm,mk->pnk", patches, right_table, precision=lax.Precision.HIGHEST)
    products = jnp.einsum("kn,pnm->pkm", left_table, halfway, precision=lax.Precision.HIGHEST)
    cos_a = products[:, :PATCH, :PATCH]
    cos_b = products[:, :PATCH, PATCH:]
    sin_a = products[:, PATCH:, :PATCH]
    sin_b = products[:, PATCH:, PATCH:]
    return (cos_a - sin_b, -(cos_b + sin_a))


def flow_between(own_re, own_im, next_re, next_im, left_table, count_y, count_x):
    cross_re = next_re * own_re + next_im * own_im
    cross_im = next_im * own_re - next_re * own_im
    stacked = jnp.concatenate([cross_re, cross_im], 2)
    products = jnp.einsum("kn,pnm->pkm", left_table, stacked, precision=lax.Precision.HIGHEST)
    mixed_re = products[:, :PATCH, :PATCH] - products[:, PATCH:, PATCH:]
    mixed_im = products[:, :PATCH, PATCH:] + products[:, PATCH:, :PATCH]
    joined = jnp.concatenate([mixed_re, -mixed_im], 2)
    correl = jnp.einsum("pnm,mk->pnk", joined, left_table, precision=lax.Precision.HIGHEST) / (
        PATCH * PATCH
    )
    squared = correl * correl
    weights = squared * squared
    totals = jnp.sum(weights, axis=(1, 2)) + EPSILON
    shifts = ((jnp.arange(PATCH, dtype=jnp.int32) + PATCH // 2) % PATCH - PATCH // 2).astype(
        jnp.float32
    )
    flow_y = jnp.sum(weights * shifts[None, :, None], axis=(1, 2)) / totals
    flow_x = jnp.sum(weights * shifts[None, None, :], axis=(1, 2)) / totals
    return jnp.stack([flow_y, flow_x], 0).reshape(2, count_y, count_x)


def laplacian(widened, offsets):
    return (
        widened[:, :, :-2, 1:-1]
        + widened[:, :, 2:, 1:-1]
        + widened[:, :, 1:-1, :-2]
        + widened[:, :, 1:-1, 2:]
        - 4.0 * offsets
    )


def remote_neighbours(offsets):
    up_one = shifted(offsets, "gz", -1)
    up_two = shifted(offsets, "gz", -2)
    down_one = shifted(offsets, "gz", 1)
    down_two = shifted(offsets, "gz", 2)
    return (up_one, up_two, down_one, down_two)


def mesh_step(offsets, laplace, coeffs):
    up_one, up_two, down_one, down_two = remote_neighbours(offsets)
    forces = STIFFNESS * laplace
    forces = forces + coeffs[2:3] * (up_one - offsets - coeffs[0:2])
    forces = forces + coeffs[5:6] * (up_two - offsets - coeffs[3:5])
    forces = forces - coeffs[8:9] * (offsets - down_one - coeffs[6:8])
    forces = forces - coeffs[11:12] * (offsets - down_two - coeffs[9:11])
    return offsets + STEP_SIZE * forces


def general_body(images, tissue_mask):
    margin = (PATCH - STRIDE) // 2
    count_y = images.shape[1] // STRIDE
    count_x = images.shape[2] // STRIDE
    padded = padded_2(images, (("gy", 1), ("gx", 2)), margin)
    left_table, right_table = tables()
    own_mask = tissue_mask.astype(jnp.float32)
    own_re, own_im = spectrum(padded[0].astype(jnp.float32), left_table, right_table)
    next_re, next_im, next_mask = shifted((own_re, own_im, own_mask), "gz", -1)
    far_re, far_im, far_mask = shifted((own_re, own_im, own_mask), "gz", -2)
    flow_one = flow_between(own_re, own_im, next_re, next_im, left_table, count_y, count_x)
    flow_two = flow_between(own_re, own_im, far_re, far_im, left_table, count_y, count_x)
    weight_one = own_mask * next_mask
    weight_two = own_mask * far_mask
    low_flow_one, low_weight_one = shifted((flow_one, weight_one), "gz", 1)
    low_flow_two, low_weight_two = shifted((flow_two, weight_two), "gz", 2)
    coeffs = jnp.concatenate(
        [
            flow_one,
            weight_one,
            flow_two,
            weight_two,
            low_flow_one,
            low_weight_one,
            low_flow_two,
            low_weight_two,
        ],
        0,
    )[:, None]
    spread = padded_2(coeffs, (("gy", 2), ("gx", 3)), RELAX)
    global_y = lax.axis_index("gy") * count_y + jnp.arange(-RELAX, count_y + RELAX, dtype=jnp.int32)
    global_x = lax.axis_index("gx") * count_x + jnp.arange(-RELAX, count_x + RELAX, dtype=jnp.int32)
    inside_y = (global_y >= 0) & (global_y < count_y * lax.axis_size("gy"))
    inside_x = (global_x >= 0) & (global_x < count_x * lax.axis_size("gx"))
    inside = (inside_y[:, None] & inside_x[None, :]).astype(jnp.float32)
    offsets = jnp.zeros((2, 1, count_y + 2 * RELAX, count_x + 2 * RELAX), jnp.float32)
    for _ in range(RELAX):
        widened = jnp.pad(offsets, ((0, 0), (0, 0), (1, 1), (1, 1)))
        offsets = mesh_step(offsets, laplacian(widened, offsets), spread) * inside[None, None]
    offsets = offsets[:, :, RELAX : RELAX + count_y, RELAX : RELAX + count_x]
    flow_fields = jnp.concatenate([flow_one, flow_two], 0)[:, None]
    return (flow_fields, offsets)


MARGIN = (PATCH - STRIDE) // 2
HALF = PATCH // 2 + 1
LANES = 128
SUBLANES = 8
BAND = HALF - 1
HALO = -(-MARGIN // 16) * 16
RADIUS = RELAX - 1
WIDE = 2 * LANES
HELD = PATCH + HALO
SIDE = LANES // 2
HALO_AT = PATCH
ROWS_AT = HALO_AT + 2 * 3 * SIDE
LEFT_AT = ROWS_AT + 2 * 2 * PATCH
RIGHT_AT = LEFT_AT + PATCH


def split_table(table):
    high = table.astype(jnp.bfloat16)
    low = (table - high.astype(np.float64)).astype(jnp.bfloat16)
    return np.stack([high, low])


def trig(first, second):
    angle = 2.0 * np.pi / PATCH * ((first[:, None] * second[None, :]) % PATCH)
    return np.cos(angle), np.sin(angle)


def column_tables():
    cosine, sine = trig(np.arange(PATCH), np.arange(HALF))
    table = np.zeros((PATCH, WIDE))
    table[:, :HALF] = cosine
    table[:, LANES : LANES + HALF] = sine
    spot = np.arange(SIDE)
    before = np.where(spot < PATCH - LANES, LANES + spot, SIDE + spot)
    outer = []
    for window in range(PATCH // STRIDE):
        start = window * STRIDE - MARGIN
        column = before if start < 0 else spot
        used = column >= start + PATCH if start < 0 else column < start
        high, low = split_table(table[column] * used[:, None])
        outer.append(np.concatenate([high, high, low], 0))
    return split_table(table), outer


def stacked(table):
    high, low = split_table(table)
    return np.concatenate([high, low, high], 1)


def frequency_rows(positions):
    cosine, sine = trig(np.arange(HALF), positions)
    return np.concatenate([cosine[:BAND], cosine[BAND:], sine[1:BAND]], 0)


def row_tables():
    tables = []
    for half in range(2):
        first = PATCH - HALO if half == 0 else 0
        position = np.concatenate([np.arange(PATCH), first + np.arange(HALO)])
        image_row = position + np.where(np.arange(HELD) < PATCH, 0, -PATCH if half == 0 else PATCH)
        rows = frequency_rows(position)
        windows = []
        for window in (2 * half, 2 * half + 1):
            start = window * STRIDE - MARGIN
            windows.append(rows * ((image_row >= start) & (image_row < start + PATCH)))
        tables.append(split_table(np.concatenate(windows, 0)))
    return tables


def inverse_tables():
    cosine, sine = trig(np.arange(PATCH), np.arange(HALF))
    weight = np.full((HALF,), 2.0 / PATCH)
    weight[0] = weight[-1] = 1.0 / PATCH
    cosine, sine = cosine * weight, sine * weight
    left = np.concatenate([cosine[:, :BAND], cosine[:, BAND:], -sine[:, 1:BAND]], 1)
    right = np.zeros((2 * LANES, PATCH))
    right[:HALF] = cosine.T
    right[LANES : LANES + HALF] = -sine.T
    return stacked(left), split_table(right)


def all_tables():
    mine, outer = column_tables()
    left, right = inverse_tables()
    blocks = [mine, outer[:2], outer[2:], *row_tables(), (left,), right]
    rows = []
    for parts in blocks:
        block = np.zeros((parts[0].shape[0], 2 * WIDE), jnp.bfloat16)
        for at, part in enumerate(parts):
            block[:, at * WIDE : at * WIDE + part.shape[1]] = part
        rows.append(block)
    return np.concatenate(rows, 0)


def dot(left, right):
    return jnp.dot(left, right, preferred_element_type=jnp.float32)


def halves_of(value):
    high = value.astype(jnp.bfloat16)
    return high, (value - high.astype(jnp.float32)).astype(jnp.bfloat16)


def table_first(table, value):
    high, low = halves_of(value)
    return dot(table, jnp.concatenate([high, high, low], 0))


def cross_spectrum(first, second):
    (acc, acs, asc, ass), (bcc, bcs, bsc, bss) = (
        (value[:BAND, :LANES], value[:BAND, LANES:], value[BAND:, :LANES], value[BAND:, LANES:])
        for value in (first, second)
    )
    even_0 = acc * bcc + acs * bcs
    even_1 = asc * bsc + ass * bss
    column_0 = acs * bcc - acc * bcs
    column_1 = ass * bsc - asc * bss
    by_row = asc * bcc - acc * bsc + ass * bcs - acs * bss
    both = acc * bss + ass * bcc - asc * bcs - acs * bsc
    top = SUBLANES
    lone = lax.broadcasted_iota(jnp.int32, (top, LANES), 0) == 0

    def with_top(usual, single):
        return jnp.concatenate([jnp.where(lone, single[:top], usual[:top]), usual[top:]], 0)

    even = with_top(even_0 + even_1, even_0)
    by_row = with_top(by_row, even_1)
    by_column = with_top(column_0 + column_1, column_0)
    both = with_top(both, column_1)
    return jnp.concatenate(
        [jnp.concatenate([even, by_column], 1), jnp.concatenate([by_row, both], 1)], 0
    )


def load_kernel(own_ref, table_ref, own_out, table_out, done):
    copies = [
        pltpu.make_async_copy(source, target, done.at[at])
        for at, (source, target) in enumerate([(own_ref, own_out), (table_ref, table_out)])
    ]
    for copy in copies:
        copy.start()
    for copy in copies:
        copy.wait()


def repeated(tail):
    return jnp.concatenate([tail] * (LANES // (PATCH - LANES)), 1)


def edge_kernel(own_ref, other_ref, out_ref):
    start = pl.multiple_of(jnp.where(lax.axis_index("gz") == 0, PATCH - HALO, 0), HALO // 2)
    rows = [ref[0, pl.ds(start, HALO)].astype(jnp.float32) for ref in (own_ref, other_ref)]
    lane = lax.broadcasted_iota(jnp.int32, (HALO, LANES), 1)
    tails = [repeated(value[:, LANES:]) for value in rows]
    tail = jnp.where(lane < PATCH - LANES, *tails)
    parts = [rows[0][:, :LANES], rows[1][:, :LANES], tail]
    out_ref[...] = jnp.concatenate(parts, 1).astype(jnp.bfloat16)


def edge_rows(beyond_ref):
    tail = beyond_ref[:, 2 * LANES :].astype(jnp.float32)
    turned = pltpu.roll(tail, LANES - (PATCH - LANES), 1)
    return [
        jnp.concatenate(
            [
                beyond_ref[:, image * LANES : (image + 1) * LANES],
                value[:, : PATCH - LANES].astype(jnp.bfloat16),
            ],
            1,
        )
        for image, value in enumerate((tail, turned))
    ]


def side_columns(tiles):
    tiles = [tile.astype(jnp.float32) for tile in tiles]
    wide = [tile[:, :LANES] for tile in tiles]
    narrow = [repeated(tile[:, LANES:]) for tile in tiles]
    lane = lax.broadcasted_iota(jnp.int32, wide[0].shape, 1)
    extra = PATCH - LANES
    low = jnp.where(lane < SIDE, wide[0], pltpu.roll(wide[1], SIDE, 1))
    high = jnp.where(lane < SIDE, pltpu.roll(wide[0], SIDE, 1), wide[1])
    high = jnp.where(lane < extra, narrow[0], high)
    high = jnp.where((lane >= SIDE) & (lane < SIDE + extra), narrow[1], high)
    odd = lax.rem(lax.axis_index("gx"), 2) == 1
    return [jnp.where(odd, *pair).astype(jnp.bfloat16) for pair in ((low, high), (high, low))]


def pack_kernel(own_ref, other_ref, first_ref, second_ref):
    first_ref[:PATCH], second_ref[:PATCH] = side_columns([own_ref[0], other_ref[0]])


def pack_edge_kernel(beyond_ref, first_in, second_in, first_ref, second_ref):
    del first_in, second_in
    first_ref[PATCH:], second_ref[PATCH:] = side_columns(edge_rows(beyond_ref))


def to_row_frequencies(table_ref, half, pixels):
    start = pl.multiple_of(ROWS_AT + half * (2 * PATCH), HALO // 2)
    high = table_ref[pl.ds(start, 2 * PATCH), :HELD]
    low = table_ref[pl.ds(start, 2 * PATCH), WIDE : WIDE + HELD]
    return dot(high, pixels) + dot(low, pixels)


def finish(columns, side, own_spectra, own_side, beside_ref, table_ref, high_ref, low_ref, rows_ref):
    half = lax.axis_index("gz")
    group = columns // 2
    beside = to_row_frequencies(table_ref, half, beside_ref[...]) - own_side
    lane = lax.broadcasted_iota(jnp.int32, beside.shape, 1)
    parts = []
    for value in (beside, pltpu.roll(beside, SIDE, 1)):
        high = value.astype(jnp.bfloat16).astype(jnp.float32)
        parts.append((high, value - high))
    factors = []
    for image in range(2):
        high = parts[image][0]
        both = jnp.where(lane < SIDE, high, parts[1 - image][1])
        factors.append(jnp.concatenate([both, high[:, :SIDE]], 1).astype(jnp.bfloat16))
    upper = half == 0
    start = pl.multiple_of(HALO_AT + side * (3 * SIDE), HALO // 2)
    spectra = []
    for column in range(group):
        table = table_ref[pl.ds(start, 3 * SIDE), column * WIDE : (column + 1) * WIDE]
        for section in range(2):
            factor = jnp.where(upper, factors[section], factors[1 - section])
            spot = slice(section * 2 * PATCH, (section + 1) * 2 * PATCH)
            spectra.append(own_spectra[spot] + dot(factor, table))
    left = table_ref[LEFT_AT:RIGHT_AT, : 3 * PATCH]
    right = [table_ref[RIGHT_AT:, start : start + PATCH] for start in (0, WIDE)]
    count = 2 * group
    for patch in range(count):
        row, column = patch % 2, patch // 2
        start = row * PATCH
        cross = cross_spectrum(
            *(value[start : start + PATCH] for value in spectra[2 * column : 2 * column + 2])
        )
        high, low = halves_of(table_first(left, cross))
        high_ref[patch * PATCH : (patch + 1) * PATCH] = high
        low_ref[patch * PATCH : (patch + 1) * PATCH] = low
    for patch in range(count):
        if patch % 2 == 0:
            block = slice(patch * PATCH, (patch + 2) * PATCH)
            correl = dot(high_ref[block], right[0]) + dot(high_ref[block], right[1])
            correl = correl + dot(low_ref[block], right[0])
        squared = correl[patch % 2 * PATCH : (patch % 2 + 1) * PATCH]
        squared = squared * squared
        weights = squared * squared
        pieces = [weights[at : at + SUBLANES] for at in range(0, PATCH, SUBLANES)]
        middle = len(pieces) // 2
        above = pieces[middle - 1]
        ranks = above
        for piece in pieces[middle - 2 : 0 : -1]:
            above = above + piece
            ranks = ranks + above
        below = pieces[middle]
        depths = below
        for piece in pieces[middle + 1 :]:
            below = below + piece
            depths = depths + below
        total = pieces[0] + above + below
        based = float(SUBLANES) * (ranks - depths)
        step = lax.broadcasted_iota(jnp.int32, (SUBLANES, PATCH), 0).astype(jnp.float32)
        based = based + step * total
        rows_ref[0, pl.ds(patch, 1)] = jnp.sum(total, 0, keepdims=True)
        rows_ref[1, pl.ds(patch, 1)] = jnp.sum(based, 0, keepdims=True)
    totals = rows_ref[0]
    shift = lax.broadcasted_iota(jnp.int32, (count, PATCH), 1)
    shift = jnp.where(shift >= PATCH // 2, shift - PATCH, shift).astype(jnp.float32)
    below = jnp.sum(totals, 1, keepdims=True) + EPSILON
    flow_y = jnp.sum(rows_ref[1], 1, keepdims=True) / below
    flow_x = jnp.sum(totals * shift, 1, keepdims=True) / below
    at = lax.broadcasted_iota(jnp.int32, (count, LANES), 1)
    patch = lax.broadcasted_iota(jnp.int32, (count, LANES), 0)
    spot = (patch >> 1) + columns * (patch & 1) + side * group
    line = jnp.where(at == spot, flow_y, 0.0) + jnp.where(at == spot + 2 * count, flow_x, 0.0)
    return jnp.sum(line, 0, keepdims=True)


def early_kernel(columns, own_ref, other_ref, beyond_ref, early_side_ref, late_side_ref, beside_ref,
                 mask_ref, table_ref, line_ref, own_spectra_ref, own_side_ref, high_rows_ref,
                 low_rows_ref, high_ref, low_ref, rows_ref):
    half = lax.axis_index("gz")
    side = 1 - lax.rem(lax.axis_index("gx"), 2)
    tiles = (own_ref[0], other_ref[0])
    images = [jnp.concatenate(pair, 0) for pair in zip(tiles, edge_rows(beyond_ref))]
    upper = half == 0
    one, two = (table_ref[:PATCH, at : at + WIDE] for at in (0, WIDE))
    for section in range(2):
        pixels = jnp.where(upper, images[section], images[1 - section])
        spot = slice(section * 2 * PATCH, (section + 1) * 2 * PATCH)
        high_rows_ref[spot], low_rows_ref[spot] = halves_of(
            to_row_frequencies(table_ref, half, pixels)
        )
        high, low = high_rows_ref[spot], low_rows_ref[spot]
        own_spectra_ref[spot] = dot(high, one) + dot(high, two) + dot(low, one)
    own_side_ref[...] = to_row_frequencies(table_ref, half, late_side_ref[...])
    own_side = to_row_frequencies(table_ref, half, early_side_ref[...])
    line = finish(
        columns, side, own_spectra_ref, own_side, beside_ref, table_ref, high_ref, low_ref, rows_ref
    )
    lanes = lax.broadcasted_iota(jnp.int32, (1, LANES), 1)
    mask = mask_ref[0].astype(jnp.float32)
    for row in range(mask.shape[0]):
        for column in range(columns):
            spot = 4 * columns + row * columns + column
            line = jnp.where(lanes == spot, mask[row : row + 1, column : column + 1], line)
    line_ref[...] = line


def late_kernel(columns, line_ref, own_spectra_ref, own_side_ref, beside_ref, table_ref, out_ref,
                high_ref, low_ref, rows_ref):
    side = lax.rem(lax.axis_index("gx"), 2)
    line = finish(
        columns, side, own_spectra_ref, own_side_ref[...], beside_ref, table_ref, high_ref, low_ref, rows_ref
    )
    out_ref[...] = jnp.broadcast_to(line_ref[...] + line, out_ref.shape)


def relax_kernel(rows, columns, got_ref, flow_ref, offsets_ref):
    size_y, size_x = lax.axis_size("gy"), lax.axis_size("gx")
    half, at_y, at_x = lax.axis_index("gz"), lax.axis_index("gy"), lax.axis_index("gx")
    count = rows * columns
    tile_rows = 2 * rows
    width = columns + 2 * RADIUS
    height = tile_rows + 2 * RADIUS
    per_section = size_y * size_x
    lane = lax.broadcasted_iota(jnp.int32, (1, LANES), 1).astype(jnp.float32)
    line = jnp.floor((lane + 0.5) * (1.0 / width))
    across = lane - line * width
    node_y = line.astype(jnp.int32) - RADIUS + at_y * tile_rows
    node_x = across.astype(jnp.int32) - RADIUS + at_x * columns
    inside = (node_y >= 0) & (node_y < tile_rows * size_y) & (node_x >= 0)
    inside = inside & (node_x < columns * size_x) & (line < height)

    def parts(value, size):
        whole = jnp.floor((value.astype(jnp.float32) + 0.5) * (1.0 / size)).astype(jnp.int32)
        return whole, value - whole * size

    tile_y, in_y = parts(node_y, tile_rows)
    tile_x, in_x = parts(node_x, columns)
    side, in_half = parts(in_y, rows)
    tile = jnp.where(inside, tile_y * size_x + tile_x, -1)
    flow_spot = in_half * columns + in_x
    got = got_ref[...]
    spread = []
    for spot in (flow_spot, flow_spot + count, 2 * count + in_y * columns + in_x):
        lanes = jnp.broadcast_to(jnp.where(inside, spot, 0), got.shape)
        spread.append(jnp.take_along_axis(got, lanes, axis=1, mode="promise_in_bounds"))
    source = lax.broadcasted_iota(jnp.int32, (2 * per_section, LANES), 0)
    chosen = source == side * per_section + tile
    chosen = chosen & (tile >= 0)
    flow_y, flow_x = (
        jnp.sum(jnp.where(chosen, spread[axis], 0.0), 0, keepdims=True)
        for axis in range(2)
    )
    chosen = source[:per_section] == tile
    mask_0, mask_1 = (
        jnp.sum(jnp.where(chosen, spread[2][start : start + per_section], 0.0), 0, keepdims=True)
        for start in (0, per_section)
    )
    flows = jnp.concatenate([flow_y, flow_x], 0)
    weight = mask_0 * mask_1
    kept = inside.astype(jnp.float32)
    sign = jnp.where(lax.broadcasted_iota(jnp.int32, (4, LANES), 0) < 2, 1.0, -1.0)
    weight = weight * sign
    offsets = jnp.zeros((4, LANES), jnp.float32)
    for step in range(RELAX):
        lower, upper = offsets[:2], offsets[2:]
        pull = upper - lower - flows
        forces = weight * jnp.concatenate([pull, pull], 0)
        if step:
            left = jnp.where(across < 0.5, 0.0, pltpu.roll(offsets, 1, 1))
            right = jnp.where(across > width - 1.5, 0.0, pltpu.roll(offsets, LANES - 1, 1))
            laplace = pltpu.roll(offsets, width, 1) + pltpu.roll(offsets, LANES - width, 1)
            forces = STIFFNESS * (laplace + left + right - 4.0 * offsets) + forces
        offsets = (offsets + STEP_SIZE * forces) * kept
    first = half == 0
    result = jnp.where(first, offsets[:2], offsets[2:])
    flows = jnp.where(first, flows, 0.0)
    for row in range(tile_rows):
        start = (RADIUS + row) * width + RADIUS
        for axis in range(2):
            offsets_ref[axis, 0, pl.ds(row, 1)] = result[axis : axis + 1, start : start + columns]
            flow_ref[axis, 0, pl.ds(row, 1)] = flows[axis : axis + 1, start : start + columns]
    flow_ref[2:] = jnp.zeros((flow_ref.shape[0] - 2, *flow_ref.shape[1:]), jnp.float32)


def vmem(count):
    return [pl.BlockSpec(memory_space=pltpu.VMEM)] * count


def pair_body(images, tissue_mask):
    sections, size_y, size_x = (lax.axis_size(name) for name in ("gz", "gy", "gx"))
    count_y = images.shape[1] // STRIDE
    count_x = images.shape[2] // STRIDE
    rows = count_y // 2
    other = lax.ppermute(images, "gz", [(0, 1), (1, 0)])
    table = jnp.asarray(all_tables())
    own, table = pl.pallas_call(
        load_kernel,
        out_shape=(
            jax.ShapeDtypeStruct(images.shape, images.dtype),
            jax.ShapeDtypeStruct(table.shape, table.dtype),
        ),
        in_specs=[pl.BlockSpec(memory_space=pltpu.HBM)] * 2,
        out_specs=tuple(vmem(2)),
        scratch_shapes=[pltpu.SemaphoreType.DMA((2,))],
        compiler_params=pltpu.CompilerParams(vmem_limit_bytes=4 * 2**20),
        cost_estimate=pl.CostEstimate(flops=0, bytes_accessed=4 * table.size, transcendentals=0),
        name="load",
    )(images, table)
    edge = pl.pallas_call(
        edge_kernel,
        out_shape=jax.ShapeDtypeStruct((HALO, 3 * LANES), jnp.bfloat16),
        in_specs=vmem(2),
        out_specs=vmem(1)[0],
        compiler_params=pltpu.CompilerParams(vmem_limit_bytes=4 * 2**20),
        name="edge",
    )(own, other)
    onward = []
    for tile in range(1, size_y):
        onward += [(tile - 1, tile), (size_y + tile, size_y + tile - 1)]
    beyond = lax.ppermute(edge, ("gz", "gy"), onward)
    swaps = [
        [pair for left in range(offset, size_x - 1, 2) for pair in ((left, left + 1), (left + 1, left))]
        for offset in range(2)
    ]
    packed = jax.ShapeDtypeStruct((HELD, LANES), jnp.bfloat16)
    small = pltpu.CompilerParams(vmem_limit_bytes=4 * 2**20)
    sends = pl.pallas_call(
        pack_kernel,
        out_shape=(packed, packed),
        in_specs=vmem(2),
        out_specs=tuple(vmem(2)),
        compiler_params=small,
        cost_estimate=pl.CostEstimate(flops=10**6, bytes_accessed=2**18, transcendentals=0),
        name="pack",
    )(own, other)
    sends = pl.pallas_call(
        pack_edge_kernel,
        out_shape=(packed, packed),
        in_specs=vmem(3),
        out_specs=tuple(vmem(2)),
        input_output_aliases={1: 0, 2: 1},
        compiler_params=small,
        name="pack_edge",
    )(beyond, *sends)
    first, second = (lax.ppermute(send, "gx", swap) for send, swap in zip(sends, swaps))
    devices = sections * size_y * size_x

    patches = rows * count_x // 2
    common = [
        pltpu.VMEM((patches * PATCH, WIDE), jnp.bfloat16),
        pltpu.VMEM((patches * PATCH, WIDE), jnp.bfloat16),
        pltpu.VMEM((2, patches, PATCH), jnp.float32),
    ]
    params = pltpu.CompilerParams(vmem_limit_bytes=16 * 2**20)
    line, own_spectra, own_side = pl.pallas_call(
        functools.partial(early_kernel, count_x),
        out_shape=(
            jax.ShapeDtypeStruct((1, LANES), jnp.float32),
            jax.ShapeDtypeStruct((4 * PATCH, WIDE), jnp.float32),
            jax.ShapeDtypeStruct((2 * PATCH, LANES), jnp.float32),
        ),
        in_specs=vmem(8),
        out_specs=tuple(vmem(3)),
        scratch_shapes=[pltpu.VMEM((4 * PATCH, PATCH), jnp.bfloat16)] * 2 + common,
        compiler_params=params,
        cost_estimate=pl.CostEstimate(flops=2 * 10**9, bytes_accessed=2**21, transcendentals=0),
        name="early",
    )(own, other, beyond, sends[1], sends[0], first, tissue_mask, table)
    lines = pl.pallas_call(
        functools.partial(late_kernel, count_x),
        out_shape=jax.ShapeDtypeStruct((devices, LANES), jnp.float32),
        in_specs=vmem(5),
        out_specs=vmem(1)[0],
        scratch_shapes=common,
        compiler_params=params,
        cost_estimate=pl.CostEstimate(flops=10**9, bytes_accessed=2**21, transcendentals=0),
        name="late",
    )(line, own_spectra, own_side, second, table)
    got = lax.all_to_all(lines, ("gz", "gy", "gx"), 0, 0, tiled=True)
    return pl.pallas_call(
        functools.partial(relax_kernel, rows, count_x),
        out_shape=(
            jax.ShapeDtypeStruct((4, 1, count_y, count_x), jnp.float32),
            jax.ShapeDtypeStruct((2, 1, count_y, count_x), jnp.float32),
        ),
        in_specs=vmem(1),
        out_specs=tuple(vmem(2)),
        compiler_params=pltpu.CompilerParams(vmem_limit_bytes=4 * 2**20),
        name="relax",
    )(got)


def body(images, tissue_mask):
    paired = lax.axis_size("gz") == 2 and images.shape == (1, PATCH, PATCH)
    return (pair_body if paired else general_body)(images, tissue_mask)


def solution(mesh):
    placed = (P("gz", "gy", "gx"), P("gz", "gy", "gx"))
    return jax.shard_map(
        body,
        mesh=mesh,
        in_specs=placed,
        out_specs=(P(None, "gz", "gy", "gx"), P(None, "gz", "gy", "gx")),
        check_vma=False,
    )
```

```python
import functools
import math

import jax
import jax.numpy as jnp
import numpy as np
from jax import lax
from jax.experimental import pallas as pl
from jax.experimental.pallas import tpu as pltpu
from jax.sharding import PartitionSpec as P

PATCH = 160
STRIDE = 40
RELAX = 4


EPSILON = 1e-06
STIFFNESS = 0.5
STEP_SIZE = 0.2


def shifted(value, axis, steps):
    count = lax.axis_size(axis)
    initial, last = (max(0, -steps), min(count, count - steps))
    return lax.ppermute(value, axis, [(source, source + steps) for source in range(initial, last)])


def padded_2(x, sides, width):
    for axis, dim in sides:
        size, length = (lax.axis_size(axis), x.shape[dim])
        up = [(i, (i + 1) % size) for i in range(size - 1)]
        down = [(j, i) for i, j in up]
        last = lax.slice_in_dim(x, length - width, length, axis=dim)
        initial = lax.slice_in_dim(x, 0, width, axis=dim)
        before = lax.ppermute(last, axis, up)
        after = lax.ppermute(initial, axis, down)
        x = jnp.concatenate([before, x, after], axis=dim)
    return x


def windows(section):
    repeats = PATCH // STRIDE
    count_y = section.shape[0] // STRIDE - repeats + 1
    count_x = section.shape[1] // STRIDE - repeats + 1
    blocks = section.reshape(section.shape[0] // STRIDE, STRIDE, section.shape[1] // STRIDE, STRIDE)
    pieces = []
    for first in range(repeats):
        row_pieces = [
            blocks[first : first + count_y, :, second : second + count_x, :]
            for second in range(repeats)
        ]
        pieces.append(jnp.stack(row_pieces, 0))
    stacked = jnp.stack(pieces, 0)
    stacked = jnp.transpose(stacked, (2, 4, 0, 3, 1, 5))
    return stacked.reshape(count_y * count_x, PATCH, PATCH)


def tables():
    indices = jnp.arange(PATCH, dtype=jnp.int32)
    phases = indices[:, None] * indices[None, :] % PATCH
    angles = phases.astype(jnp.float32) * (2.0 * math.pi / PATCH)
    cosine_table = jnp.cos(angles)
    sine_table = jnp.sin(angles)
    left_table = jnp.concatenate([cosine_table, sine_table], 0)
    right_table = jnp.concatenate([cosine_table, sine_table], 1)
    return (left_table, right_table)


def spectrum(section, left_table, right_table):
    patches = windows(section)
    halfway = jnp.einsum("pnm,mk->pnk", patches, right_table, precision=lax.Precision.HIGHEST)
    products = jnp.einsum("kn,pnm->pkm", left_table, halfway, precision=lax.Precision.HIGHEST)
    cos_a = products[:, :PATCH, :PATCH]
    cos_b = products[:, :PATCH, PATCH:]
    sin_a = products[:, PATCH:, :PATCH]
    sin_b = products[:, PATCH:, PATCH:]
    return (cos_a - sin_b, -(cos_b + sin_a))


def flow_between(own_re, own_im, next_re, next_im, left_table, count_y, count_x):
    cross_re = next_re * own_re + next_im * own_im
    cross_im = next_im * own_re - next_re * own_im
    stacked = jnp.concatenate([cross_re, cross_im], 2)
    products = jnp.einsum("kn,pnm->pkm", left_table, stacked, precision=lax.Precision.HIGHEST)
    mixed_re = products[:, :PATCH, :PATCH] - products[:, PATCH:, PATCH:]
    mixed_im = products[:, :PATCH, PATCH:] + products[:, PATCH:, :PATCH]
    joined = jnp.concatenate([mixed_re, -mixed_im], 2)
    correl = jnp.einsum("pnm,mk->pnk", joined, left_table, precision=lax.Precision.HIGHEST) / (
        PATCH * PATCH
    )
    squared = correl * correl
    weights = squared * squared
    totals = jnp.sum(weights, axis=(1, 2)) + EPSILON
    shifts = ((jnp.arange(PATCH, dtype=jnp.int32) + PATCH // 2) % PATCH - PATCH // 2).astype(
        jnp.float32
    )
    flow_y = jnp.sum(weights * shifts[None, :, None], axis=(1, 2)) / totals
    flow_x = jnp.sum(weights * shifts[None, None, :], axis=(1, 2)) / totals
    return jnp.stack([flow_y, flow_x], 0).reshape(2, count_y, count_x)


def laplacian(widened, offsets):
    return (
        widened[:, :, :-2, 1:-1]
        + widened[:, :, 2:, 1:-1]
        + widened[:, :, 1:-1, :-2]
        + widened[:, :, 1:-1, 2:]
        - 4.0 * offsets
    )


def remote_neighbours(offsets):
    up_one = shifted(offsets, "gz", -1)
    up_two = shifted(offsets, "gz", -2)
    down_one = shifted(offsets, "gz", 1)
    down_two = shifted(offsets, "gz", 2)
    return (up_one, up_two, down_one, down_two)


def mesh_step(offsets, laplace, coeffs):
    up_one, up_two, down_one, down_two = remote_neighbours(offsets)
    forces = STIFFNESS * laplace
    forces = forces + coeffs[2:3] * (up_one - offsets - coeffs[0:2])
    forces = forces + coeffs[5:6] * (up_two - offsets - coeffs[3:5])
    forces = forces - coeffs[8:9] * (offsets - down_one - coeffs[6:8])
    forces = forces - coeffs[11:12] * (offsets - down_two - coeffs[9:11])
    return offsets + STEP_SIZE * forces


def general_body(images, tissue_mask):
    margin = (PATCH - STRIDE) // 2
    count_y = images.shape[1] // STRIDE
    count_x = images.shape[2] // STRIDE
    padded = padded_2(images, (("gy", 1), ("gx", 2)), margin)
    left_table, right_table = tables()
    own_mask = tissue_mask.astype(jnp.float32)
    own_re, own_im = spectrum(padded[0].astype(jnp.float32), left_table, right_table)
    next_re, next_im, next_mask = shifted((own_re, own_im, own_mask), "gz", -1)
    far_re, far_im, far_mask = shifted((own_re, own_im, own_mask), "gz", -2)
    flow_one = flow_between(own_re, own_im, next_re, next_im, left_table, count_y, count_x)
    flow_two = flow_between(own_re, own_im, far_re, far_im, left_table, count_y, count_x)
    weight_one = own_mask * next_mask
    weight_two = own_mask * far_mask
    low_flow_one, low_weight_one = shifted((flow_one, weight_one), "gz", 1)
    low_flow_two, low_weight_two = shifted((flow_two, weight_two), "gz", 2)
    coeffs = jnp.concatenate(
        [
            flow_one,
            weight_one,
            flow_two,
            weight_two,
            low_flow_one,
            low_weight_one,
            low_flow_two,
            low_weight_two,
        ],
        0,
    )[:, None]
    spread = padded_2(coeffs, (("gy", 2), ("gx", 3)), RELAX)
    global_y = lax.axis_index("gy") * count_y + jnp.arange(-RELAX, count_y + RELAX, dtype=jnp.int32)
    global_x = lax.axis_index("gx") * count_x + jnp.arange(-RELAX, count_x + RELAX, dtype=jnp.int32)
    inside_y = (global_y >= 0) & (global_y < count_y * lax.axis_size("gy"))
    inside_x = (global_x >= 0) & (global_x < count_x * lax.axis_size("gx"))
    inside = (inside_y[:, None] & inside_x[None, :]).astype(jnp.float32)
    offsets = jnp.zeros((2, 1, count_y + 2 * RELAX, count_x + 2 * RELAX), jnp.float32)
    for _ in range(RELAX):
        widened = jnp.pad(offsets, ((0, 0), (0, 0), (1, 1), (1, 1)))
        offsets = mesh_step(offsets, laplacian(widened, offsets), spread) * inside[None, None]
    offsets = offsets[:, :, RELAX : RELAX + count_y, RELAX : RELAX + count_x]
    flow_fields = jnp.concatenate([flow_one, flow_two], 0)[:, None]
    return (flow_fields, offsets)


MARGIN = (PATCH - STRIDE) // 2
HALF = PATCH // 2 + 1
LANES = 128
SUBLANES = 8
BAND = HALF - 1
HALO = -(-MARGIN // 16) * 16
RADIUS = RELAX - 1
WIDE = 2 * LANES
HELD = PATCH + HALO
SIDE = LANES // 2
HALO_AT = PATCH
ROWS_AT = HALO_AT + 2 * 3 * SIDE
LEFT_AT = ROWS_AT + 2 * 2 * PATCH
RIGHT_AT = LEFT_AT + PATCH


def split_table(table):
    high = table.astype(jnp.bfloat16)
    low = (table - high.astype(np.float64)).astype(jnp.bfloat16)
    return np.stack([high, low])


def trig(first, second):
    angle = 2.0 * np.pi / PATCH * ((first[:, None] * second[None, :]) % PATCH)
    return np.cos(angle), np.sin(angle)


def column_tables():
    cosine, sine = trig(np.arange(PATCH), np.arange(HALF))
    table = np.zeros((PATCH, WIDE))
    table[:, :HALF] = cosine
    table[:, LANES : LANES + HALF] = sine
    spot = np.arange(SIDE)
    before = np.where(spot < PATCH - LANES, LANES + spot, SIDE + spot)
    outer = []
    for window in range(PATCH // STRIDE):
        start = window * STRIDE - MARGIN
        column = before if start < 0 else spot
        used = column >= start + PATCH if start < 0 else column < start
        high, low = split_table(table[column] * used[:, None])
        outer.append(np.concatenate([high, high, low], 0))
    return split_table(table), outer


def stacked(table):
    high, low = split_table(table)
    return np.concatenate([high, low, high], 1)


def frequency_rows(positions):
    cosine, sine = trig(np.arange(HALF), positions)
    return np.concatenate([cosine[:BAND], cosine[BAND:], sine[1:BAND]], 0)


def row_tables():
    tables = []
    for half in range(2):
        first = PATCH - HALO if half == 0 else 0
        position = np.concatenate([np.arange(PATCH), first + np.arange(HALO)])
        image_row = position + np.where(np.arange(HELD) < PATCH, 0, -PATCH if half == 0 else PATCH)
        rows = frequency_rows(position)
        windows = []
        for window in (2 * half, 2 * half + 1):
            start = window * STRIDE - MARGIN
            windows.append(rows * ((image_row >= start) & (image_row < start + PATCH)))
        tables.append(split_table(np.concatenate(windows, 0)))
    return tables


def inverse_tables():
    cosine, sine = trig(np.arange(PATCH), np.arange(HALF))
    weight = np.full((HALF,), 2.0 / PATCH)
    weight[0] = weight[-1] = 1.0 / PATCH
    cosine, sine = cosine * weight, sine * weight
    left = np.concatenate([cosine[:, :BAND], cosine[:, BAND:], -sine[:, 1:BAND]], 1)
    right = np.zeros((2 * LANES, PATCH))
    right[:HALF] = cosine.T
    right[LANES : LANES + HALF] = -sine.T
    return stacked(left), split_table(right)


def all_tables():
    mine, outer = column_tables()
    left, right = inverse_tables()
    blocks = [mine, outer[:2], outer[2:], *row_tables(), (left,), right]
    rows = []
    for parts in blocks:
        block = np.zeros((parts[0].shape[0], 2 * WIDE), jnp.bfloat16)
        for at, part in enumerate(parts):
            block[:, at * WIDE : at * WIDE + part.shape[1]] = part
        rows.append(block)
    return np.concatenate(rows, 0)


def dot(left, right):
    return jnp.dot(left, right, preferred_element_type=jnp.float32)


def halves_of(value):
    high = value.astype(jnp.bfloat16)
    return high, (value - high.astype(jnp.float32)).astype(jnp.bfloat16)


def table_first(table, value):
    high, low = halves_of(value)
    return dot(table, jnp.concatenate([high, high, low], 0))


def cross_spectrum(first, second):
    (acc, acs, asc, ass), (bcc, bcs, bsc, bss) = (
        (value[:BAND, :LANES], value[:BAND, LANES:], value[BAND:, :LANES], value[BAND:, LANES:])
        for value in (first, second)
    )
    even_0 = acc * bcc + acs * bcs
    even_1 = asc * bsc + ass * bss
    column_0 = acs * bcc - acc * bcs
    column_1 = ass * bsc - asc * bss
    by_row = asc * bcc - acc * bsc + ass * bcs - acs * bss
    both = acc * bss + ass * bcc - asc * bcs - acs * bsc
    top = SUBLANES
    lone = lax.broadcasted_iota(jnp.int32, (top, LANES), 0) == 0

    def with_top(usual, single):
        return jnp.concatenate([jnp.where(lone, single[:top], usual[:top]), usual[top:]], 0)

    even = with_top(even_0 + even_1, even_0)
    by_row = with_top(by_row, even_1)
    by_column = with_top(column_0 + column_1, column_0)
    both = with_top(both, column_1)
    return jnp.concatenate(
        [jnp.concatenate([even, by_column], 1), jnp.concatenate([by_row, both], 1)], 0
    )


def load_kernel(own_ref, table_ref, own_out, table_out, done):
    copies = [
        pltpu.make_async_copy(source, target, done.at[at])
        for at, (source, target) in enumerate([(own_ref, own_out), (table_ref, table_out)])
    ]
    for copy in copies:
        copy.start()
    for copy in copies:
        copy.wait()


def repeated(tail):
    return jnp.concatenate([tail] * (LANES // (PATCH - LANES)), 1)


def edge_kernel(own_ref, other_ref, out_ref):
    start = pl.multiple_of(jnp.where(lax.axis_index("gz") == 0, PATCH - HALO, 0), HALO // 2)
    rows = [ref[0, pl.ds(start, HALO)].astype(jnp.float32) for ref in (own_ref, other_ref)]
    lane = lax.broadcasted_iota(jnp.int32, (HALO, LANES), 1)
    tails = [repeated(value[:, LANES:]) for value in rows]
    tail = jnp.where(lane < PATCH - LANES, *tails)
    parts = [rows[0][:, :LANES], rows[1][:, :LANES], tail]
    out_ref[...] = jnp.concatenate(parts, 1).astype(jnp.bfloat16)


def edge_rows(beyond_ref):
    tail = beyond_ref[:, 2 * LANES :].astype(jnp.float32)
    turned = pltpu.roll(tail, LANES - (PATCH - LANES), 1)
    return [
        jnp.concatenate(
            [
                beyond_ref[:, image * LANES : (image + 1) * LANES],
                value[:, : PATCH - LANES].astype(jnp.bfloat16),
            ],
            1,
        )
        for image, value in enumerate((tail, turned))
    ]


def side_columns(tiles):
    tiles = [tile.astype(jnp.float32) for tile in tiles]
    wide = [tile[:, :LANES] for tile in tiles]
    narrow = [repeated(tile[:, LANES:]) for tile in tiles]
    lane = lax.broadcasted_iota(jnp.int32, wide[0].shape, 1)
    extra = PATCH - LANES
    low = jnp.where(lane < SIDE, wide[0], pltpu.roll(wide[1], SIDE, 1))
    high = jnp.where(lane < SIDE, pltpu.roll(wide[0], SIDE, 1), wide[1])
    high = jnp.where(lane < extra, narrow[0], high)
    high = jnp.where((lane >= SIDE) & (lane < SIDE + extra), narrow[1], high)
    odd = lax.rem(lax.axis_index("gx"), 2) == 1
    return [jnp.where(odd, *pair).astype(jnp.bfloat16) for pair in ((low, high), (high, low))]


def pack_kernel(own_ref, other_ref, first_ref, second_ref):
    first_ref[:PATCH], second_ref[:PATCH] = side_columns([own_ref[0], other_ref[0]])


def pack_edge_kernel(beyond_ref, first_in, second_in, first_ref, second_ref):
    del first_in, second_in
    first_ref[PATCH:], second_ref[PATCH:] = side_columns(edge_rows(beyond_ref))


def to_row_frequencies(table_ref, half, pixels):
    start = pl.multiple_of(ROWS_AT + half * (2 * PATCH), HALO // 2)
    high = table_ref[pl.ds(start, 2 * PATCH), :HELD]
    low = table_ref[pl.ds(start, 2 * PATCH), WIDE : WIDE + HELD]
    return dot(high, pixels) + dot(low, pixels)


def finish(columns, side, own_spectra, own_side, beside_ref, table_ref, high_ref, low_ref, rows_ref):
    half = lax.axis_index("gz")
    group = columns // 2
    beside = to_row_frequencies(table_ref, half, beside_ref[...]) - own_side
    lane = lax.broadcasted_iota(jnp.int32, beside.shape, 1)
    parts = []
    for value in (beside, pltpu.roll(beside, SIDE, 1)):
        high = value.astype(jnp.bfloat16).astype(jnp.float32)
        parts.append((high, value - high))
    factors = []
    for image in range(2):
        high = parts[image][0]
        both = jnp.where(lane < SIDE, high, parts[1 - image][1])
        factors.append(jnp.concatenate([both, high[:, :SIDE]], 1).astype(jnp.bfloat16))
    upper = half == 0
    start = pl.multiple_of(HALO_AT + side * (3 * SIDE), HALO // 2)
    spectra = []
    for column in range(group):
        table = table_ref[pl.ds(start, 3 * SIDE), column * WIDE : (column + 1) * WIDE]
        for section in range(2):
            factor = jnp.where(upper, factors[section], factors[1 - section])
            spot = slice(section * 2 * PATCH, (section + 1) * 2 * PATCH)
            spectra.append(own_spectra[spot] + dot(factor, table))
    left = table_ref[LEFT_AT:RIGHT_AT, : 3 * PATCH]
    right = [table_ref[RIGHT_AT:, start : start + PATCH] for start in (0, WIDE)]
    count = 2 * group
    for patch in range(count):
        row, column = patch % 2, patch // 2
        start = row * PATCH
        cross = cross_spectrum(
            *(value[start : start + PATCH] for value in spectra[2 * column : 2 * column + 2])
        )
        high, low = halves_of(table_first(left, cross))
        high_ref[patch * PATCH : (patch + 1) * PATCH] = high
        low_ref[patch * PATCH : (patch + 1) * PATCH] = low
    for patch in range(count):
        if patch in (0, 3):
            first = patch
            ahead = [start for start in (0, 3) if start > patch] + [count]
            block = slice(first * PATCH, ahead[0] * PATCH)
            correl = dot(high_ref[block], right[0]) + dot(high_ref[block], right[1])
            correl = correl + dot(low_ref[block], right[0])
        squared = correl[(patch - first) * PATCH : (patch - first + 1) * PATCH]
        squared = squared * squared
        weights = squared * squared
        pieces = [weights[at : at + SUBLANES] for at in range(0, PATCH, SUBLANES)]
        middle = len(pieces) // 2
        above = pieces[middle - 1]
        ranks = above
        for piece in pieces[middle - 2 : 0 : -1]:
            above = above + piece
            ranks = ranks + above
        below = pieces[middle]
        depths = below
        for piece in pieces[middle + 1 :]:
            below = below + piece
            depths = depths + below
        total = pieces[0] + above + below
        based = float(SUBLANES) * (ranks - depths)
        step = lax.broadcasted_iota(jnp.int32, (SUBLANES, PATCH), 0).astype(jnp.float32)
        based = based + step * total
        rows_ref[0, pl.ds(patch, 1)] = jnp.sum(total, 0, keepdims=True)
        rows_ref[1, pl.ds(patch, 1)] = jnp.sum(based, 0, keepdims=True)
    totals = rows_ref[0]
    shift = lax.broadcasted_iota(jnp.int32, (count, PATCH), 1)
    shift = jnp.where(shift >= PATCH // 2, shift - PATCH, shift).astype(jnp.float32)
    below = jnp.sum(totals, 1, keepdims=True) + EPSILON
    flow_y = jnp.sum(rows_ref[1], 1, keepdims=True) / below
    flow_x = jnp.sum(totals * shift, 1, keepdims=True) / below
    at = lax.broadcasted_iota(jnp.int32, (count, LANES), 1)
    patch = lax.broadcasted_iota(jnp.int32, (count, LANES), 0)
    spot = (patch >> 1) + columns * (patch & 1) + side * group
    line = jnp.where(at == spot, flow_y, 0.0) + jnp.where(at == spot + 2 * count, flow_x, 0.0)
    return jnp.sum(line, 0, keepdims=True)


def early_kernel(columns, own_ref, other_ref, beyond_ref, early_side_ref, late_side_ref, beside_ref,
                 mask_ref, table_ref, line_ref, own_spectra_ref, own_side_ref, high_rows_ref,
                 low_rows_ref, high_ref, low_ref, rows_ref):
    half = lax.axis_index("gz")
    side = 1 - lax.rem(lax.axis_index("gx"), 2)
    tiles = (own_ref[0], other_ref[0])
    images = [jnp.concatenate(pair, 0) for pair in zip(tiles, edge_rows(beyond_ref))]
    upper = half == 0
    one, two = (table_ref[:PATCH, at : at + WIDE] for at in (0, WIDE))
    for section in range(2):
        pixels = jnp.where(upper, images[section], images[1 - section])
        spot = slice(section * 2 * PATCH, (section + 1) * 2 * PATCH)
        high_rows_ref[spot], low_rows_ref[spot] = halves_of(
            to_row_frequencies(table_ref, half, pixels)
        )
        high, low = high_rows_ref[spot], low_rows_ref[spot]
        own_spectra_ref[spot] = dot(high, one) + dot(high, two) + dot(low, one)
    own_side_ref[...] = to_row_frequencies(table_ref, half, late_side_ref[...])
    own_side = to_row_frequencies(table_ref, half, early_side_ref[...])
    line = finish(
        columns, side, own_spectra_ref, own_side, beside_ref, table_ref, high_ref, low_ref, rows_ref
    )
    lanes = lax.broadcasted_iota(jnp.int32, (1, LANES), 1)
    mask = mask_ref[0].astype(jnp.float32)
    for row in range(mask.shape[0]):
        for column in range(columns):
            spot = 4 * columns + row * columns + column
            line = jnp.where(lanes == spot, mask[row : row + 1, column : column + 1], line)
    line_ref[...] = line


def late_kernel(columns, line_ref, own_spectra_ref, own_side_ref, beside_ref, table_ref, out_ref,
                high_ref, low_ref, rows_ref):
    side = lax.rem(lax.axis_index("gx"), 2)
    line = finish(
        columns, side, own_spectra_ref, own_side_ref[...], beside_ref, table_ref, high_ref, low_ref, rows_ref
    )
    out_ref[...] = jnp.broadcast_to(line_ref[...] + line, out_ref.shape)


def relax_kernel(rows, columns, got_ref, flow_ref, offsets_ref):
    size_y, size_x = lax.axis_size("gy"), lax.axis_size("gx")
    half, at_y, at_x = lax.axis_index("gz"), lax.axis_index("gy"), lax.axis_index("gx")
    count = rows * columns
    tile_rows = 2 * rows
    width = columns + 2 * RADIUS
    height = tile_rows + 2 * RADIUS
    per_section = size_y * size_x
    lane = lax.broadcasted_iota(jnp.int32, (1, LANES), 1).astype(jnp.float32)
    line = jnp.floor((lane + 0.5) * (1.0 / width))
    across = lane - line * width
    node_y = line.astype(jnp.int32) - RADIUS + at_y * tile_rows
    node_x = across.astype(jnp.int32) - RADIUS + at_x * columns
    inside = (node_y >= 0) & (node_y < tile_rows * size_y) & (node_x >= 0)
    inside = inside & (node_x < columns * size_x) & (line < height)

    def parts(value, size):
        whole = jnp.floor((value.astype(jnp.float32) + 0.5) * (1.0 / size)).astype(jnp.int32)
        return whole, value - whole * size

    tile_y, in_y = parts(node_y, tile_rows)
    tile_x, in_x = parts(node_x, columns)
    side, in_half = parts(in_y, rows)
    tile = jnp.where(inside, tile_y * size_x + tile_x, -1)
    flow_spot = in_half * columns + in_x
    got = got_ref[...]
    spread = []
    for spot in (flow_spot, flow_spot + count, 2 * count + in_y * columns + in_x):
        lanes = jnp.broadcast_to(jnp.where(inside, spot, 0), got.shape)
        spread.append(jnp.take_along_axis(got, lanes, axis=1, mode="promise_in_bounds"))
    source = lax.broadcasted_iota(jnp.int32, (2 * per_section, LANES), 0)
    chosen = source == side * per_section + tile
    chosen = chosen & (tile >= 0)
    flow_y, flow_x = (
        jnp.sum(jnp.where(chosen, spread[axis], 0.0), 0, keepdims=True)
        for axis in range(2)
    )
    chosen = source[:per_section] == tile
    mask_0, mask_1 = (
        jnp.sum(jnp.where(chosen, spread[2][start : start + per_section], 0.0), 0, keepdims=True)
        for start in (0, per_section)
    )
    flows = jnp.concatenate([flow_y, flow_x], 0)
    weight = mask_0 * mask_1
    kept = inside.astype(jnp.float32)
    sign = jnp.where(lax.broadcasted_iota(jnp.int32, (4, LANES), 0) < 2, 1.0, -1.0)
    weight = weight * sign
    offsets = jnp.zeros((4, LANES), jnp.float32)
    for step in range(RELAX):
        lower, upper = offsets[:2], offsets[2:]
        pull = upper - lower - flows
        forces = weight * jnp.concatenate([pull, pull], 0)
        if step:
            left = jnp.where(across < 0.5, 0.0, pltpu.roll(offsets, 1, 1))
            right = jnp.where(across > width - 1.5, 0.0, pltpu.roll(offsets, LANES - 1, 1))
            laplace = pltpu.roll(offsets, width, 1) + pltpu.roll(offsets, LANES - width, 1)
            forces = STIFFNESS * (laplace + left + right - 4.0 * offsets) + forces
        offsets = (offsets + STEP_SIZE * forces) * kept
    first = half == 0
    result = jnp.where(first, offsets[:2], offsets[2:])
    flows = jnp.where(first, flows, 0.0)
    for row in range(tile_rows):
        start = (RADIUS + row) * width + RADIUS
        for axis in range(2):
            offsets_ref[axis, 0, pl.ds(row, 1)] = result[axis : axis + 1, start : start + columns]
            flow_ref[axis, 0, pl.ds(row, 1)] = flows[axis : axis + 1, start : start + columns]
    flow_ref[2:] = jnp.zeros((flow_ref.shape[0] - 2, *flow_ref.shape[1:]), jnp.float32)


def vmem(count):
    return [pl.BlockSpec(memory_space=pltpu.VMEM)] * count


def pair_body(images, tissue_mask):
    sections, size_y, size_x = (lax.axis_size(name) for name in ("gz", "gy", "gx"))
    count_y = images.shape[1] // STRIDE
    count_x = images.shape[2] // STRIDE
    rows = count_y // 2
    other = lax.ppermute(images, "gz", [(0, 1), (1, 0)])
    table = jnp.asarray(all_tables())
    own, table = pl.pallas_call(
        load_kernel,
        out_shape=(
            jax.ShapeDtypeStruct(images.shape, images.dtype),
            jax.ShapeDtypeStruct(table.shape, table.dtype),
        ),
        in_specs=[pl.BlockSpec(memory_space=pltpu.HBM)] * 2,
        out_specs=tuple(vmem(2)),
        scratch_shapes=[pltpu.SemaphoreType.DMA((2,))],
        compiler_params=pltpu.CompilerParams(vmem_limit_bytes=4 * 2**20),
        cost_estimate=pl.CostEstimate(flops=0, bytes_accessed=4 * table.size, transcendentals=0),
        name="load",
    )(images, table)
    edge = pl.pallas_call(
        edge_kernel,
        out_shape=jax.ShapeDtypeStruct((HALO, 3 * LANES), jnp.bfloat16),
        in_specs=vmem(2),
        out_specs=vmem(1)[0],
        compiler_params=pltpu.CompilerParams(vmem_limit_bytes=4 * 2**20),
        name="edge",
    )(own, other)
    onward = []
    for tile in range(1, size_y):
        onward += [(tile - 1, tile), (size_y + tile, size_y + tile - 1)]
    beyond = lax.ppermute(edge, ("gz", "gy"), onward)
    swaps = [
        [pair for left in range(offset, size_x - 1, 2) for pair in ((left, left + 1), (left + 1, left))]
        for offset in range(2)
    ]
    packed = jax.ShapeDtypeStruct((HELD, LANES), jnp.bfloat16)
    small = pltpu.CompilerParams(vmem_limit_bytes=4 * 2**20)
    sends = pl.pallas_call(
        pack_kernel,
        out_shape=(packed, packed),
        in_specs=vmem(2),
        out_specs=tuple(vmem(2)),
        compiler_params=small,
        cost_estimate=pl.CostEstimate(flops=10**6, bytes_accessed=2**18, transcendentals=0),
        name="pack",
    )(own, other)
    sends = pl.pallas_call(
        pack_edge_kernel,
        out_shape=(packed, packed),
        in_specs=vmem(3),
        out_specs=tuple(vmem(2)),
        input_output_aliases={1: 0, 2: 1},
        compiler_params=small,
        name="pack_edge",
    )(beyond, *sends)
    first, second = (lax.ppermute(send, "gx", swap) for send, swap in zip(sends, swaps))
    devices = sections * size_y * size_x

    patches = rows * count_x // 2
    common = [
        pltpu.VMEM((patches * PATCH, WIDE), jnp.bfloat16),
        pltpu.VMEM((patches * PATCH, WIDE), jnp.bfloat16),
        pltpu.VMEM((2, patches, PATCH), jnp.float32),
    ]
    params = pltpu.CompilerParams(vmem_limit_bytes=16 * 2**20)
    line, own_spectra, own_side = pl.pallas_call(
        functools.partial(early_kernel, count_x),
        out_shape=(
            jax.ShapeDtypeStruct((1, LANES), jnp.float32),
            jax.ShapeDtypeStruct((4 * PATCH, WIDE), jnp.float32),
            jax.ShapeDtypeStruct((2 * PATCH, LANES), jnp.float32),
        ),
        in_specs=vmem(8),
        out_specs=tuple(vmem(3)),
        scratch_shapes=[pltpu.VMEM((4 * PATCH, PATCH), jnp.bfloat16)] * 2 + common,
        compiler_params=params,
        cost_estimate=pl.CostEstimate(flops=2 * 10**9, bytes_accessed=2**21, transcendentals=0),
        name="early",
    )(own, other, beyond, sends[1], sends[0], first, tissue_mask, table)
    lines = pl.pallas_call(
        functools.partial(late_kernel, count_x),
        out_shape=jax.ShapeDtypeStruct((devices, LANES), jnp.float32),
        in_specs=vmem(5),
        out_specs=vmem(1)[0],
        scratch_shapes=common,
        compiler_params=params,
        cost_estimate=pl.CostEstimate(flops=10**9, bytes_accessed=2**21, transcendentals=0),
        name="late",
    )(line, own_spectra, own_side, second, table)
    got = lax.all_to_all(lines, ("gz", "gy", "gx"), 0, 0, tiled=True)
    return pl.pallas_call(
        functools.partial(relax_kernel, rows, count_x),
        out_shape=(
            jax.ShapeDtypeStruct((4, 1, count_y, count_x), jnp.float32),
            jax.ShapeDtypeStruct((2, 1, count_y, count_x), jnp.float32),
        ),
        in_specs=vmem(1),
        out_specs=tuple(vmem(2)),
        compiler_params=pltpu.CompilerParams(vmem_limit_bytes=4 * 2**20),
        name="relax",
    )(got)


def body(images, tissue_mask):
    paired = lax.axis_size("gz") == 2 and images.shape == (1, PATCH, PATCH)
    return (pair_body if paired else general_body)(images, tissue_mask)


def solution(mesh):
    placed = (P("gz", "gy", "gx"), P("gz", "gy", "gx"))
    return jax.shard_map(
        body,
        mesh=mesh,
        in_specs=placed,
        out_specs=(P(None, "gz", "gy", "gx"), P(None, "gz", "gy", "gx")),
        check_vma=False,
    )
```

```python
import functools
import math

import jax
import jax.numpy as jnp
import numpy as np
from jax import lax
from jax.experimental import pallas as pl
from jax.experimental.pallas import tpu as pltpu
from jax.sharding import PartitionSpec as P

PATCH = 160
STRIDE = 40
RELAX = 4


EPSILON = 1e-06
STIFFNESS = 0.5
STEP_SIZE = 0.2


def shifted(value, axis, steps):
    count = lax.axis_size(axis)
    initial, last = (max(0, -steps), min(count, count - steps))
    return lax.ppermute(value, axis, [(source, source + steps) for source in range(initial, last)])


def padded_2(x, sides, width):
    for axis, dim in sides:
        size, length = (lax.axis_size(axis), x.shape[dim])
        up = [(i, (i + 1) % size) for i in range(size - 1)]
        down = [(j, i) for i, j in up]
        last = lax.slice_in_dim(x, length - width, length, axis=dim)
        initial = lax.slice_in_dim(x, 0, width, axis=dim)
        before = lax.ppermute(last, axis, up)
        after = lax.ppermute(initial, axis, down)
        x = jnp.concatenate([before, x, after], axis=dim)
    return x


def windows(section):
    repeats = PATCH // STRIDE
    count_y = section.shape[0] // STRIDE - repeats + 1
    count_x = section.shape[1] // STRIDE - repeats + 1
    blocks = section.reshape(section.shape[0] // STRIDE, STRIDE, section.shape[1] // STRIDE, STRIDE)
    pieces = []
    for first in range(repeats):
        row_pieces = [
            blocks[first : first + count_y, :, second : second + count_x, :]
            for second in range(repeats)
        ]
        pieces.append(jnp.stack(row_pieces, 0))
    stacked = jnp.stack(pieces, 0)
    stacked = jnp.transpose(stacked, (2, 4, 0, 3, 1, 5))
    return stacked.reshape(count_y * count_x, PATCH, PATCH)


def tables():
    indices = jnp.arange(PATCH, dtype=jnp.int32)
    phases = indices[:, None] * indices[None, :] % PATCH
    angles = phases.astype(jnp.float32) * (2.0 * math.pi / PATCH)
    cosine_table = jnp.cos(angles)
    sine_table = jnp.sin(angles)
    left_table = jnp.concatenate([cosine_table, sine_table], 0)
    right_table = jnp.concatenate([cosine_table, sine_table], 1)
    return (left_table, right_table)


def spectrum(section, left_table, right_table):
    patches = windows(section)
    halfway = jnp.einsum("pnm,mk->pnk", patches, right_table, precision=lax.Precision.HIGHEST)
    products = jnp.einsum("kn,pnm->pkm", left_table, halfway, precision=lax.Precision.HIGHEST)
    cos_a = products[:, :PATCH, :PATCH]
    cos_b = products[:, :PATCH, PATCH:]
    sin_a = products[:, PATCH:, :PATCH]
    sin_b = products[:, PATCH:, PATCH:]
    return (cos_a - sin_b, -(cos_b + sin_a))


def flow_between(own_re, own_im, next_re, next_im, left_table, count_y, count_x):
    cross_re = next_re * own_re + next_im * own_im
    cross_im = next_im * own_re - next_re * own_im
    stacked = jnp.concatenate([cross_re, cross_im], 2)
    products = jnp.einsum("kn,pnm->pkm", left_table, stacked, precision=lax.Precision.HIGHEST)
    mixed_re = products[:, :PATCH, :PATCH] - products[:, PATCH:, PATCH:]
    mixed_im = products[:, :PATCH, PATCH:] + products[:, PATCH:, :PATCH]
    joined = jnp.concatenate([mixed_re, -mixed_im], 2)
    correl = jnp.einsum("pnm,mk->pnk", joined, left_table, precision=lax.Precision.HIGHEST) / (
        PATCH * PATCH
    )
    squared = correl * correl
    weights = squared * squared
    totals = jnp.sum(weights, axis=(1, 2)) + EPSILON
    shifts = ((jnp.arange(PATCH, dtype=jnp.int32) + PATCH // 2) % PATCH - PATCH // 2).astype(
        jnp.float32
    )
    flow_y = jnp.sum(weights * shifts[None, :, None], axis=(1, 2)) / totals
    flow_x = jnp.sum(weights * shifts[None, None, :], axis=(1, 2)) / totals
    return jnp.stack([flow_y, flow_x], 0).reshape(2, count_y, count_x)


def laplacian(widened, offsets):
    return (
        widened[:, :, :-2, 1:-1]
        + widened[:, :, 2:, 1:-1]
        + widened[:, :, 1:-1, :-2]
        + widened[:, :, 1:-1, 2:]
        - 4.0 * offsets
    )


def remote_neighbours(offsets):
    up_one = shifted(offsets, "gz", -1)
    up_two = shifted(offsets, "gz", -2)
    down_one = shifted(offsets, "gz", 1)
    down_two = shifted(offsets, "gz", 2)
    return (up_one, up_two, down_one, down_two)


def mesh_step(offsets, laplace, coeffs):
    up_one, up_two, down_one, down_two = remote_neighbours(offsets)
    forces = STIFFNESS * laplace
    forces = forces + coeffs[2:3] * (up_one - offsets - coeffs[0:2])
    forces = forces + coeffs[5:6] * (up_two - offsets - coeffs[3:5])
    forces = forces - coeffs[8:9] * (offsets - down_one - coeffs[6:8])
    forces = forces - coeffs[11:12] * (offsets - down_two - coeffs[9:11])
    return offsets + STEP_SIZE * forces


def general_body(images, tissue_mask):
    margin = (PATCH - STRIDE) // 2
    count_y = images.shape[1] // STRIDE
    count_x = images.shape[2] // STRIDE
    padded = padded_2(images, (("gy", 1), ("gx", 2)), margin)
    left_table, right_table = tables()
    own_mask = tissue_mask.astype(jnp.float32)
    own_re, own_im = spectrum(padded[0].astype(jnp.float32), left_table, right_table)
    next_re, next_im, next_mask = shifted((own_re, own_im, own_mask), "gz", -1)
    far_re, far_im, far_mask = shifted((own_re, own_im, own_mask), "gz", -2)
    flow_one = flow_between(own_re, own_im, next_re, next_im, left_table, count_y, count_x)
    flow_two = flow_between(own_re, own_im, far_re, far_im, left_table, count_y, count_x)
    weight_one = own_mask * next_mask
    weight_two = own_mask * far_mask
    low_flow_one, low_weight_one = shifted((flow_one, weight_one), "gz", 1)
    low_flow_two, low_weight_two = shifted((flow_two, weight_two), "gz", 2)
    coeffs = jnp.concatenate(
        [
            flow_one,
            weight_one,
            flow_two,
            weight_two,
            low_flow_one,
            low_weight_one,
            low_flow_two,
            low_weight_two,
        ],
        0,
    )[:, None]
    spread = padded_2(coeffs, (("gy", 2), ("gx", 3)), RELAX)
    global_y = lax.axis_index("gy") * count_y + jnp.arange(-RELAX, count_y + RELAX, dtype=jnp.int32)
    global_x = lax.axis_index("gx") * count_x + jnp.arange(-RELAX, count_x + RELAX, dtype=jnp.int32)
    inside_y = (global_y >= 0) & (global_y < count_y * lax.axis_size("gy"))
    inside_x = (global_x >= 0) & (global_x < count_x * lax.axis_size("gx"))
    inside = (inside_y[:, None] & inside_x[None, :]).astype(jnp.float32)
    offsets = jnp.zeros((2, 1, count_y + 2 * RELAX, count_x + 2 * RELAX), jnp.float32)
    for _ in range(RELAX):
        widened = jnp.pad(offsets, ((0, 0), (0, 0), (1, 1), (1, 1)))
        offsets = mesh_step(offsets, laplacian(widened, offsets), spread) * inside[None, None]
    offsets = offsets[:, :, RELAX : RELAX + count_y, RELAX : RELAX + count_x]
    flow_fields = jnp.concatenate([flow_one, flow_two], 0)[:, None]
    return (flow_fields, offsets)


MARGIN = (PATCH - STRIDE) // 2
HALF = PATCH // 2 + 1
LANES = 128
SUBLANES = 8
BAND = HALF - 1
HALO = -(-MARGIN // 16) * 16
RADIUS = RELAX - 1
WIDE = 2 * LANES
HELD = PATCH + HALO
SIDE = LANES // 2
HALO_AT = PATCH
ROWS_AT = HALO_AT + 2 * 3 * SIDE
LEFT_AT = ROWS_AT + 2 * 2 * PATCH
RIGHT_AT = LEFT_AT + PATCH


def split_table(table):
    high = table.astype(jnp.bfloat16)
    low = (table - high.astype(np.float64)).astype(jnp.bfloat16)
    return np.stack([high, low])


def trig(first, second):
    angle = 2.0 * np.pi / PATCH * ((first[:, None] * second[None, :]) % PATCH)
    return np.cos(angle), np.sin(angle)


def column_tables():
    cosine, sine = trig(np.arange(PATCH), np.arange(HALF))
    table = np.zeros((PATCH, WIDE))
    table[:, :HALF] = cosine
    table[:, LANES : LANES + HALF] = sine
    spot = np.arange(SIDE)
    before = np.where(spot < PATCH - LANES, LANES + spot, SIDE + spot)
    outer = []
    for window in range(PATCH // STRIDE):
        start = window * STRIDE - MARGIN
        column = before if start < 0 else spot
        used = column >= start + PATCH if start < 0 else column < start
        high, low = split_table(table[column] * used[:, None])
        outer.append(np.concatenate([high, high, low], 0))
    return split_table(table), outer


def stacked(table):
    high, low = split_table(table)
    return np.concatenate([high, low, high], 1)


def frequency_rows(positions):
    cosine, sine = trig(np.arange(HALF), positions)
    return np.concatenate([cosine[:BAND], cosine[BAND:], sine[1:BAND]], 0)


def row_tables():
    tables = []
    for half in range(2):
        first = PATCH - HALO if half == 0 else 0
        position = np.concatenate([np.arange(PATCH), first + np.arange(HALO)])
        image_row = position + np.where(np.arange(HELD) < PATCH, 0, -PATCH if half == 0 else PATCH)
        rows = frequency_rows(position)
        windows = []
        for window in (2 * half, 2 * half + 1):
            start = window * STRIDE - MARGIN
            windows.append(rows * ((image_row >= start) & (image_row < start + PATCH)))
        tables.append(split_table(np.concatenate(windows, 0)))
    return tables


def inverse_tables():
    cosine, sine = trig(np.arange(PATCH), np.arange(HALF))
    weight = np.full((HALF,), 2.0 / PATCH)
    weight[0] = weight[-1] = 1.0 / PATCH
    cosine, sine = cosine * weight, sine * weight
    left = np.concatenate([cosine[:, :BAND], cosine[:, BAND:], -sine[:, 1:BAND]], 1)
    right = np.zeros((2 * LANES, PATCH))
    right[:HALF] = cosine.T
    right[LANES : LANES + HALF] = -sine.T
    return stacked(left), split_table(right)


def all_tables():
    mine, outer = column_tables()
    left, right = inverse_tables()
    blocks = [mine, outer[:2], outer[2:], *row_tables(), (left,), right]
    rows = []
    for parts in blocks:
        block = np.zeros((parts[0].shape[0], 2 * WIDE), jnp.bfloat16)
        for at, part in enumerate(parts):
            block[:, at * WIDE : at * WIDE + part.shape[1]] = part
        rows.append(block)
    return np.concatenate(rows, 0)


def dot(left, right):
    return jnp.dot(left, right, preferred_element_type=jnp.float32)


def halves_of(value):
    high = value.astype(jnp.bfloat16)
    return high, (value - high.astype(jnp.float32)).astype(jnp.bfloat16)


def table_first(table, value):
    high, low = halves_of(value)
    return dot(table, jnp.concatenate([high, high, low], 0))


def cross_spectrum(first, second):
    (acc, acs, asc, ass), (bcc, bcs, bsc, bss) = (
        (value[:BAND, :LANES], value[:BAND, LANES:], value[BAND:, :LANES], value[BAND:, LANES:])
        for value in (first, second)
    )
    even_0 = acc * bcc + acs * bcs
    even_1 = asc * bsc + ass * bss
    column_0 = acs * bcc - acc * bcs
    column_1 = ass * bsc - asc * bss
    by_row = asc * bcc - acc * bsc + ass * bcs - acs * bss
    both = acc * bss + ass * bcc - asc * bcs - acs * bsc
    top = SUBLANES
    lone = lax.broadcasted_iota(jnp.int32, (top, LANES), 0) == 0

    def with_top(usual, single):
        return jnp.concatenate([jnp.where(lone, single[:top], usual[:top]), usual[top:]], 0)

    even = with_top(even_0 + even_1, even_0)
    by_row = with_top(by_row, even_1)
    by_column = with_top(column_0 + column_1, column_0)
    both = with_top(both, column_1)
    return jnp.concatenate(
        [jnp.concatenate([even, by_column], 1), jnp.concatenate([by_row, both], 1)], 0
    )


def load_kernel(own_ref, table_ref, own_out, table_out, done):
    copies = [
        pltpu.make_async_copy(source, target, done.at[at])
        for at, (source, target) in enumerate([(own_ref, own_out), (table_ref, table_out)])
    ]
    for copy in copies:
        copy.start()
    for copy in copies:
        copy.wait()


def repeated(tail):
    return jnp.concatenate([tail] * (LANES // (PATCH - LANES)), 1)


def edge_kernel(own_ref, other_ref, out_ref):
    start = pl.multiple_of(jnp.where(lax.axis_index("gz") == 0, PATCH - HALO, 0), HALO // 2)
    rows = [ref[0, pl.ds(start, HALO)].astype(jnp.float32) for ref in (own_ref, other_ref)]
    lane = lax.broadcasted_iota(jnp.int32, (HALO, LANES), 1)
    tails = [repeated(value[:, LANES:]) for value in rows]
    tail = jnp.where(lane < PATCH - LANES, *tails)
    parts = [rows[0][:, :LANES], rows[1][:, :LANES], tail]
    out_ref[...] = jnp.concatenate(parts, 1).astype(jnp.bfloat16)


def edge_rows(beyond_ref):
    tail = beyond_ref[:, 2 * LANES :].astype(jnp.float32)
    turned = pltpu.roll(tail, LANES - (PATCH - LANES), 1)
    return [
        jnp.concatenate(
            [
                beyond_ref[:, image * LANES : (image + 1) * LANES],
                value[:, : PATCH - LANES].astype(jnp.bfloat16),
            ],
            1,
        )
        for image, value in enumerate((tail, turned))
    ]


def side_columns(tiles):
    tiles = [tile.astype(jnp.float32) for tile in tiles]
    wide = [tile[:, :LANES] for tile in tiles]
    narrow = [repeated(tile[:, LANES:]) for tile in tiles]
    lane = lax.broadcasted_iota(jnp.int32, wide[0].shape, 1)
    extra = PATCH - LANES
    low = jnp.where(lane < SIDE, wide[0], pltpu.roll(wide[1], SIDE, 1))
    high = jnp.where(lane < SIDE, pltpu.roll(wide[0], SIDE, 1), wide[1])
    high = jnp.where(lane < extra, narrow[0], high)
    high = jnp.where((lane >= SIDE) & (lane < SIDE + extra), narrow[1], high)
    odd = lax.rem(lax.axis_index("gx"), 2) == 1
    return [jnp.where(odd, *pair).astype(jnp.bfloat16) for pair in ((low, high), (high, low))]


def pack_kernel(rows, columns, own_ref, other_ref, first_ref, second_ref, *plan_refs):
    first_ref[:PATCH], second_ref[:PATCH] = side_columns([own_ref[0], other_ref[0]])
    plan_nodes(rows, columns, *plan_refs)


def pack_edge_kernel(beyond_ref, first_in, second_in, first_ref, second_ref):
    del first_in, second_in
    first_ref[PATCH:], second_ref[PATCH:] = side_columns(edge_rows(beyond_ref))


def to_row_frequencies(table_ref, half, pixels):
    start = pl.multiple_of(ROWS_AT + half * (2 * PATCH), HALO // 2)
    high = table_ref[pl.ds(start, 2 * PATCH), :HELD]
    low = table_ref[pl.ds(start, 2 * PATCH), WIDE : WIDE + HELD]
    return dot(high, pixels) + dot(low, pixels)


def finish(columns, side, own_spectra, own_side, beside_ref, table_ref, high_ref, low_ref, rows_ref):
    half = lax.axis_index("gz")
    group = columns // 2
    beside = to_row_frequencies(table_ref, half, beside_ref[...]) - own_side
    lane = lax.broadcasted_iota(jnp.int32, beside.shape, 1)
    parts = []
    for value in (beside, pltpu.roll(beside, SIDE, 1)):
        high = value.astype(jnp.bfloat16).astype(jnp.float32)
        parts.append((high, value - high))
    factors = []
    for image in range(2):
        high = parts[image][0]
        both = jnp.where(lane < SIDE, high, parts[1 - image][1])
        factors.append(jnp.concatenate([both, high[:, :SIDE]], 1).astype(jnp.bfloat16))
    upper = half == 0
    start = pl.multiple_of(HALO_AT + side * (3 * SIDE), HALO // 2)
    spectra = []
    for column in range(group):
        table = table_ref[pl.ds(start, 3 * SIDE), column * WIDE : (column + 1) * WIDE]
        for section in range(2):
            factor = jnp.where(upper, factors[section], factors[1 - section])
            spot = slice(section * 2 * PATCH, (section + 1) * 2 * PATCH)
            spectra.append(own_spectra[spot] + dot(factor, table))
    left = table_ref[LEFT_AT:RIGHT_AT, : 3 * PATCH]
    right = [table_ref[RIGHT_AT:, start : start + PATCH] for start in (0, WIDE)]
    count = 2 * group
    for patch in range(count):
        row, column = patch % 2, patch // 2
        start = row * PATCH
        cross = cross_spectrum(
            *(value[start : start + PATCH] for value in spectra[2 * column : 2 * column + 2])
        )
        high, low = halves_of(table_first(left, cross))
        high_ref[patch * PATCH : (patch + 1) * PATCH] = high
        low_ref[patch * PATCH : (patch + 1) * PATCH] = low
    for patch in range(count):
        if patch in (0, 3):
            first = patch
            ahead = [start for start in (0, 3) if start > patch] + [count]
            block = slice(first * PATCH, ahead[0] * PATCH)
            correl = dot(high_ref[block], right[0]) + dot(high_ref[block], right[1])
            correl = correl + dot(low_ref[block], right[0])
        squared = correl[(patch - first) * PATCH : (patch - first + 1) * PATCH]
        squared = squared * squared
        weights = squared * squared
        pieces = [weights[at : at + SUBLANES] for at in range(0, PATCH, SUBLANES)]
        middle = len(pieces) // 2
        above = pieces[middle - 1]
        ranks = above
        for piece in pieces[middle - 2 : 0 : -1]:
            above = above + piece
            ranks = ranks + above
        below = pieces[middle]
        depths = below
        for piece in pieces[middle + 1 :]:
            below = below + piece
            depths = depths + below
        total = pieces[0] + above + below
        based = float(SUBLANES) * (ranks - depths)
        step = lax.broadcasted_iota(jnp.int32, (SUBLANES, PATCH), 0).astype(jnp.float32)
        based = based + step * total
        rows_ref[0, pl.ds(patch, 1)] = jnp.sum(total, 0, keepdims=True)
        rows_ref[1, pl.ds(patch, 1)] = jnp.sum(based, 0, keepdims=True)
    totals = rows_ref[0]
    shift = lax.broadcasted_iota(jnp.int32, (count, PATCH), 1)
    shift = jnp.where(shift >= PATCH // 2, shift - PATCH, shift).astype(jnp.float32)
    below = jnp.sum(totals, 1, keepdims=True) + EPSILON
    flow_y = jnp.sum(rows_ref[1], 1, keepdims=True) / below
    flow_x = jnp.sum(totals * shift, 1, keepdims=True) / below
    at = lax.broadcasted_iota(jnp.int32, (count, LANES), 1)
    patch = lax.broadcasted_iota(jnp.int32, (count, LANES), 0)
    spot = (patch >> 1) + columns * (patch & 1) + side * group
    line = jnp.where(at == spot, flow_y, 0.0) + jnp.where(at == spot + 2 * count, flow_x, 0.0)
    return jnp.sum(line, 0, keepdims=True)


def early_kernel(columns, own_ref, other_ref, beyond_ref, early_side_ref, late_side_ref, beside_ref,
                 mask_ref, table_ref, line_ref, own_spectra_ref, own_side_ref, high_rows_ref,
                 low_rows_ref, high_ref, low_ref, rows_ref):
    half = lax.axis_index("gz")
    side = 1 - lax.rem(lax.axis_index("gx"), 2)
    tiles = (own_ref[0], other_ref[0])
    images = [jnp.concatenate(pair, 0) for pair in zip(tiles, edge_rows(beyond_ref))]
    upper = half == 0
    one, two = (table_ref[:PATCH, at : at + WIDE] for at in (0, WIDE))
    for section in range(2):
        pixels = jnp.where(upper, images[section], images[1 - section])
        spot = slice(section * 2 * PATCH, (section + 1) * 2 * PATCH)
        high_rows_ref[spot], low_rows_ref[spot] = halves_of(
            to_row_frequencies(table_ref, half, pixels)
        )
        high, low = high_rows_ref[spot], low_rows_ref[spot]
        own_spectra_ref[spot] = dot(high, one) + dot(high, two) + dot(low, one)
    own_side_ref[...] = to_row_frequencies(table_ref, half, late_side_ref[...])
    own_side = to_row_frequencies(table_ref, half, early_side_ref[...])
    line = finish(
        columns, side, own_spectra_ref, own_side, beside_ref, table_ref, high_ref, low_ref, rows_ref
    )
    lanes = lax.broadcasted_iota(jnp.int32, (1, LANES), 1)
    mask = mask_ref[0].astype(jnp.float32)
    for row in range(mask.shape[0]):
        for column in range(columns):
            spot = 4 * columns + row * columns + column
            line = jnp.where(lanes == spot, mask[row : row + 1, column : column + 1], line)
    line_ref[...] = line


def late_kernel(columns, line_ref, own_spectra_ref, own_side_ref, beside_ref, table_ref, out_ref,
                high_ref, low_ref, rows_ref):
    side = lax.rem(lax.axis_index("gx"), 2)
    line = finish(
        columns, side, own_spectra_ref, own_side_ref[...], beside_ref, table_ref, high_ref, low_ref, rows_ref
    )
    out_ref[...] = jnp.broadcast_to(line_ref[...] + line, out_ref.shape)


def plan_nodes(rows, columns, spots_ref, chosen_ref, masks_ref):
    size_y, size_x = lax.axis_size("gy"), lax.axis_size("gx")
    at_y, at_x = lax.axis_index("gy"), lax.axis_index("gx")
    count = rows * columns
    tile_rows = 2 * rows
    width = columns + 2 * RADIUS
    height = tile_rows + 2 * RADIUS
    per_section = size_y * size_x
    lane = lax.broadcasted_iota(jnp.int32, (1, LANES), 1).astype(jnp.float32)
    line = jnp.floor((lane + 0.5) * (1.0 / width))
    across = lane - line * width
    node_y = line.astype(jnp.int32) - RADIUS + at_y * tile_rows
    node_x = across.astype(jnp.int32) - RADIUS + at_x * columns
    inside = (node_y >= 0) & (node_y < tile_rows * size_y) & (node_x >= 0)
    inside = inside & (node_x < columns * size_x) & (line < height)

    def parts(value, size):
        whole = jnp.floor((value.astype(jnp.float32) + 0.5) * (1.0 / size)).astype(jnp.int32)
        return whole, value - whole * size

    tile_y, in_y = parts(node_y, tile_rows)
    tile_x, in_x = parts(node_x, columns)
    side, in_half = parts(in_y, rows)
    tile = tile_y * size_x + tile_x
    flow_spot = in_half * columns + in_x
    spots = [flow_spot, flow_spot + count, 2 * count + in_y * columns + in_x]
    spots_ref[...] = jnp.concatenate([jnp.where(inside, spot, 0) for spot in spots], 0)
    source = lax.broadcasted_iota(jnp.int32, (2 * per_section, LANES), 0)
    flow_source = (source == side * per_section + tile) & inside
    mask_source = ((source == tile) | (source == per_section + tile)) & inside
    chosen_ref[...] = jnp.concatenate(
        [flow_source.astype(jnp.float32), mask_source.astype(jnp.float32)], 1
    )
    not_first = (across > 0.5).astype(jnp.float32)
    not_last = (across < width - 1.5).astype(jnp.float32)
    masks_ref[...] = jnp.concatenate([inside.astype(jnp.float32), not_first, not_last], 0)


def relax_kernel(rows, columns, got_ref, spots_ref, chosen_ref, masks_ref, flow_ref, offsets_ref):
    half = lax.axis_index("gz")
    tile_rows = 2 * rows
    width = columns + 2 * RADIUS
    devices = got_ref.shape[0]
    got = got_ref[...]
    spread = [
        jnp.take_along_axis(
            got, jnp.broadcast_to(spots_ref[at : at + 1], got.shape), axis=1, mode="promise_in_bounds"
        )
        for at in range(3)
    ]
    from_one, from_both = chosen_ref[:, :LANES], chosen_ref[:, LANES:]
    flow_y, flow_x = (jnp.sum(spread[axis] * from_one, 0, keepdims=True) for axis in range(2))
    masks = spread[2] * from_both
    middle = devices // 2
    weight = jnp.sum(masks[:middle], 0, keepdims=True) * jnp.sum(masks[middle:], 0, keepdims=True)
    flows = jnp.concatenate([flow_y, flow_x], 0)
    kept, not_first, not_last = (masks_ref[at : at + 1] for at in range(3))
    sign = jnp.where(lax.broadcasted_iota(jnp.int32, (4, LANES), 0) < 2, 1.0, -1.0)
    weight = weight * sign
    offsets = jnp.zeros((4, LANES), jnp.float32)
    for step in range(RELAX):
        lower, upper = offsets[:2], offsets[2:]
        pull = upper - lower - flows
        forces = weight * jnp.concatenate([pull, pull], 0)
        if step:
            left = pltpu.roll(offsets, 1, 1) * not_first
            right = pltpu.roll(offsets, LANES - 1, 1) * not_last
            laplace = pltpu.roll(offsets, width, 1) + pltpu.roll(offsets, LANES - width, 1)
            forces = STIFFNESS * (laplace + left + right - 4.0 * offsets) + forces
        offsets = (offsets + STEP_SIZE * forces) * kept
    first = half == 0
    result = jnp.where(first, offsets[:2], offsets[2:])
    result = jnp.concatenate([result, jnp.where(first, flows, 0.0)], 0)
    flow_ref[2:] = jnp.zeros((flow_ref.shape[0] - 2, *flow_ref.shape[1:]), jnp.float32)
    for row in range(tile_rows):
        start = (RADIUS + row) * width + RADIUS
        part = result[:, start : start + columns]
        offsets_ref[:, 0, row, :] = part[:2]
        flow_ref[:2, 0, row, :] = part[2:]


def vmem(count):
    return [pl.BlockSpec(memory_space=pltpu.VMEM)] * count


def pair_body(images, tissue_mask):
    sections, size_y, size_x = (lax.axis_size(name) for name in ("gz", "gy", "gx"))
    count_y = images.shape[1] // STRIDE
    count_x = images.shape[2] // STRIDE
    rows = count_y // 2
    other = lax.ppermute(images, "gz", [(0, 1), (1, 0)])
    table = jnp.asarray(all_tables())
    own, table = pl.pallas_call(
        load_kernel,
        out_shape=(
            jax.ShapeDtypeStruct(images.shape, images.dtype),
            jax.ShapeDtypeStruct(table.shape, table.dtype),
        ),
        in_specs=[pl.BlockSpec(memory_space=pltpu.HBM)] * 2,
        out_specs=tuple(vmem(2)),
        scratch_shapes=[pltpu.SemaphoreType.DMA((2,))],
        compiler_params=pltpu.CompilerParams(vmem_limit_bytes=4 * 2**20),
        cost_estimate=pl.CostEstimate(flops=0, bytes_accessed=4 * table.size, transcendentals=0),
        name="load",
    )(images, table)
    edge = pl.pallas_call(
        edge_kernel,
        out_shape=jax.ShapeDtypeStruct((HALO, 3 * LANES), jnp.bfloat16),
        in_specs=vmem(2),
        out_specs=vmem(1)[0],
        compiler_params=pltpu.CompilerParams(vmem_limit_bytes=4 * 2**20),
        name="edge",
    )(own, other)
    onward = []
    for tile in range(1, size_y):
        onward += [(tile - 1, tile), (size_y + tile, size_y + tile - 1)]
    beyond = lax.ppermute(edge, ("gz", "gy"), onward)
    swaps = [
        [pair for left in range(offset, size_x - 1, 2) for pair in ((left, left + 1), (left + 1, left))]
        for offset in range(2)
    ]
    packed = jax.ShapeDtypeStruct((HELD, LANES), jnp.bfloat16)
    small = pltpu.CompilerParams(vmem_limit_bytes=4 * 2**20)
    devices = sections * size_y * size_x
    *sends, spots, chosen, masks = pl.pallas_call(
        functools.partial(pack_kernel, rows, count_x),
        out_shape=(
            packed,
            packed,
            jax.ShapeDtypeStruct((3, LANES), jnp.int32),
            jax.ShapeDtypeStruct((devices, 2 * LANES), jnp.float32),
            jax.ShapeDtypeStruct((3, LANES), jnp.float32),
        ),
        in_specs=vmem(2),
        out_specs=tuple(vmem(5)),
        compiler_params=small,
        cost_estimate=pl.CostEstimate(flops=10**6, bytes_accessed=2**18, transcendentals=0),
        name="pack",
    )(own, other)
    sends = pl.pallas_call(
        pack_edge_kernel,
        out_shape=(packed, packed),
        in_specs=vmem(3),
        out_specs=tuple(vmem(2)),
        input_output_aliases={1: 0, 2: 1},
        compiler_params=small,
        name="pack_edge",
    )(beyond, *sends)
    first, second = (lax.ppermute(send, "gx", swap) for send, swap in zip(sends, swaps))

    patches = rows * count_x // 2
    common = [
        pltpu.VMEM((patches * PATCH, WIDE), jnp.bfloat16),
        pltpu.VMEM((patches * PATCH, WIDE), jnp.bfloat16),
        pltpu.VMEM((2, patches, PATCH), jnp.float32),
    ]
    params = pltpu.CompilerParams(vmem_limit_bytes=16 * 2**20)
    line, own_spectra, own_side = pl.pallas_call(
        functools.partial(early_kernel, count_x),
        out_shape=(
            jax.ShapeDtypeStruct((1, LANES), jnp.float32),
            jax.ShapeDtypeStruct((4 * PATCH, WIDE), jnp.float32),
            jax.ShapeDtypeStruct((2 * PATCH, LANES), jnp.float32),
        ),
        in_specs=vmem(8),
        out_specs=tuple(vmem(3)),
        scratch_shapes=[pltpu.VMEM((4 * PATCH, PATCH), jnp.bfloat16)] * 2 + common,
        compiler_params=params,
        cost_estimate=pl.CostEstimate(flops=2 * 10**9, bytes_accessed=2**21, transcendentals=0),
        name="early",
    )(own, other, beyond, sends[1], sends[0], first, tissue_mask, table)
    lines = pl.pallas_call(
        functools.partial(late_kernel, count_x),
        out_shape=jax.ShapeDtypeStruct((devices, LANES), jnp.float32),
        in_specs=vmem(5),
        out_specs=vmem(1)[0],
        scratch_shapes=common,
        compiler_params=params,
        cost_estimate=pl.CostEstimate(flops=10**9, bytes_accessed=2**21, transcendentals=0),
        name="late",
    )(line, own_spectra, own_side, second, table)
    got = lax.all_to_all(lines, ("gz", "gy", "gx"), 0, 0, tiled=True)
    return pl.pallas_call(
        functools.partial(relax_kernel, rows, count_x),
        out_shape=(
            jax.ShapeDtypeStruct((4, 1, count_y, count_x), jnp.float32),
            jax.ShapeDtypeStruct((2, 1, count_y, count_x), jnp.float32),
        ),
        in_specs=vmem(4),
        out_specs=tuple(vmem(2)),
        compiler_params=small,
        name="relax",
    )(got, spots, chosen, masks)


def body(images, tissue_mask):
    paired = lax.axis_size("gz") == 2 and images.shape == (1, PATCH, PATCH)
    return (pair_body if paired else general_body)(images, tissue_mask)


def solution(mesh):
    placed = (P("gz", "gy", "gx"), P("gz", "gy", "gx"))
    return jax.shard_map(
        body,
        mesh=mesh,
        in_specs=placed,
        out_specs=(P(None, "gz", "gy", "gx"), P(None, "gz", "gy", "gx")),
        check_vma=False,
    )
```

```python
import functools
import math

import jax
import jax.numpy as jnp
import numpy as np
from jax import lax
from jax.experimental import pallas as pl
from jax.experimental.pallas import tpu as pltpu
from jax.sharding import PartitionSpec as P

PATCH = 160
STRIDE = 40
RELAX = 4


EPSILON = 1e-06
STIFFNESS = 0.5
STEP_SIZE = 0.2


def shifted(value, axis, steps):
    count = lax.axis_size(axis)
    initial, last = (max(0, -steps), min(count, count - steps))
    return lax.ppermute(value, axis, [(source, source + steps) for source in range(initial, last)])


def padded_2(x, sides, width):
    for axis, dim in sides:
        size, length = (lax.axis_size(axis), x.shape[dim])
        up = [(i, (i + 1) % size) for i in range(size - 1)]
        down = [(j, i) for i, j in up]
        last = lax.slice_in_dim(x, length - width, length, axis=dim)
        initial = lax.slice_in_dim(x, 0, width, axis=dim)
        before = lax.ppermute(last, axis, up)
        after = lax.ppermute(initial, axis, down)
        x = jnp.concatenate([before, x, after], axis=dim)
    return x


def windows(section):
    repeats = PATCH // STRIDE
    count_y = section.shape[0] // STRIDE - repeats + 1
    count_x = section.shape[1] // STRIDE - repeats + 1
    blocks = section.reshape(section.shape[0] // STRIDE, STRIDE, section.shape[1] // STRIDE, STRIDE)
    pieces = []
    for first in range(repeats):
        row_pieces = [
            blocks[first : first + count_y, :, second : second + count_x, :]
            for second in range(repeats)
        ]
        pieces.append(jnp.stack(row_pieces, 0))
    stacked = jnp.stack(pieces, 0)
    stacked = jnp.transpose(stacked, (2, 4, 0, 3, 1, 5))
    return stacked.reshape(count_y * count_x, PATCH, PATCH)


def tables():
    indices = jnp.arange(PATCH, dtype=jnp.int32)
    phases = indices[:, None] * indices[None, :] % PATCH
    angles = phases.astype(jnp.float32) * (2.0 * math.pi / PATCH)
    cosine_table = jnp.cos(angles)
    sine_table = jnp.sin(angles)
    left_table = jnp.concatenate([cosine_table, sine_table], 0)
    right_table = jnp.concatenate([cosine_table, sine_table], 1)
    return (left_table, right_table)


def spectrum(section, left_table, right_table):
    patches = windows(section)
    halfway = jnp.einsum("pnm,mk->pnk", patches, right_table, precision=lax.Precision.HIGHEST)
    products = jnp.einsum("kn,pnm->pkm", left_table, halfway, precision=lax.Precision.HIGHEST)
    cos_a = products[:, :PATCH, :PATCH]
    cos_b = products[:, :PATCH, PATCH:]
    sin_a = products[:, PATCH:, :PATCH]
    sin_b = products[:, PATCH:, PATCH:]
    return (cos_a - sin_b, -(cos_b + sin_a))


def flow_between(own_re, own_im, next_re, next_im, left_table, count_y, count_x):
    cross_re = next_re * own_re + next_im * own_im
    cross_im = next_im * own_re - next_re * own_im
    stacked = jnp.concatenate([cross_re, cross_im], 2)
    products = jnp.einsum("kn,pnm->pkm", left_table, stacked, precision=lax.Precision.HIGHEST)
    mixed_re = products[:, :PATCH, :PATCH] - products[:, PATCH:, PATCH:]
    mixed_im = products[:, :PATCH, PATCH:] + products[:, PATCH:, :PATCH]
    joined = jnp.concatenate([mixed_re, -mixed_im], 2)
    correl = jnp.einsum("pnm,mk->pnk", joined, left_table, precision=lax.Precision.HIGHEST) / (
        PATCH * PATCH
    )
    squared = correl * correl
    weights = squared * squared
    totals = jnp.sum(weights, axis=(1, 2)) + EPSILON
    shifts = ((jnp.arange(PATCH, dtype=jnp.int32) + PATCH // 2) % PATCH - PATCH // 2).astype(
        jnp.float32
    )
    flow_y = jnp.sum(weights * shifts[None, :, None], axis=(1, 2)) / totals
    flow_x = jnp.sum(weights * shifts[None, None, :], axis=(1, 2)) / totals
    return jnp.stack([flow_y, flow_x], 0).reshape(2, count_y, count_x)


def laplacian(widened, offsets):
    return (
        widened[:, :, :-2, 1:-1]
        + widened[:, :, 2:, 1:-1]
        + widened[:, :, 1:-1, :-2]
        + widened[:, :, 1:-1, 2:]
        - 4.0 * offsets
    )


def remote_neighbours(offsets):
    up_one = shifted(offsets, "gz", -1)
    up_two = shifted(offsets, "gz", -2)
    down_one = shifted(offsets, "gz", 1)
    down_two = shifted(offsets, "gz", 2)
    return (up_one, up_two, down_one, down_two)


def mesh_step(offsets, laplace, coeffs):
    up_one, up_two, down_one, down_two = remote_neighbours(offsets)
    forces = STIFFNESS * laplace
    forces = forces + coeffs[2:3] * (up_one - offsets - coeffs[0:2])
    forces = forces + coeffs[5:6] * (up_two - offsets - coeffs[3:5])
    forces = forces - coeffs[8:9] * (offsets - down_one - coeffs[6:8])
    forces = forces - coeffs[11:12] * (offsets - down_two - coeffs[9:11])
    return offsets + STEP_SIZE * forces


def general_body(images, tissue_mask):
    margin = (PATCH - STRIDE) // 2
    count_y = images.shape[1] // STRIDE
    count_x = images.shape[2] // STRIDE
    padded = padded_2(images, (("gy", 1), ("gx", 2)), margin)
    left_table, right_table = tables()
    own_mask = tissue_mask.astype(jnp.float32)
    own_re, own_im = spectrum(padded[0].astype(jnp.float32), left_table, right_table)
    next_re, next_im, next_mask = shifted((own_re, own_im, own_mask), "gz", -1)
    far_re, far_im, far_mask = shifted((own_re, own_im, own_mask), "gz", -2)
    flow_one = flow_between(own_re, own_im, next_re, next_im, left_table, count_y, count_x)
    flow_two = flow_between(own_re, own_im, far_re, far_im, left_table, count_y, count_x)
    weight_one = own_mask * next_mask
    weight_two = own_mask * far_mask
    low_flow_one, low_weight_one = shifted((flow_one, weight_one), "gz", 1)
    low_flow_two, low_weight_two = shifted((flow_two, weight_two), "gz", 2)
    coeffs = jnp.concatenate(
        [
            flow_one,
            weight_one,
            flow_two,
            weight_two,
            low_flow_one,
            low_weight_one,
            low_flow_two,
            low_weight_two,
        ],
        0,
    )[:, None]
    spread = padded_2(coeffs, (("gy", 2), ("gx", 3)), RELAX)
    global_y = lax.axis_index("gy") * count_y + jnp.arange(-RELAX, count_y + RELAX, dtype=jnp.int32)
    global_x = lax.axis_index("gx") * count_x + jnp.arange(-RELAX, count_x + RELAX, dtype=jnp.int32)
    inside_y = (global_y >= 0) & (global_y < count_y * lax.axis_size("gy"))
    inside_x = (global_x >= 0) & (global_x < count_x * lax.axis_size("gx"))
    inside = (inside_y[:, None] & inside_x[None, :]).astype(jnp.float32)
    offsets = jnp.zeros((2, 1, count_y + 2 * RELAX, count_x + 2 * RELAX), jnp.float32)
    for _ in range(RELAX):
        widened = jnp.pad(offsets, ((0, 0), (0, 0), (1, 1), (1, 1)))
        offsets = mesh_step(offsets, laplacian(widened, offsets), spread) * inside[None, None]
    offsets = offsets[:, :, RELAX : RELAX + count_y, RELAX : RELAX + count_x]
    flow_fields = jnp.concatenate([flow_one, flow_two], 0)[:, None]
    return (flow_fields, offsets)


MARGIN = (PATCH - STRIDE) // 2
HALF = PATCH // 2 + 1
LANES = 128
SUBLANES = 8
BAND = HALF - 1
HALO = -(-MARGIN // 16) * 16
RADIUS = RELAX - 1
WIDE = 2 * LANES
HELD = PATCH + HALO
SIDE = LANES // 2
HALO_AT = PATCH
ROWS_AT = HALO_AT + 2 * 3 * SIDE
LEFT_AT = ROWS_AT + 2 * 2 * PATCH
RIGHT_AT = LEFT_AT + PATCH


def split_table(table):
    high = table.astype(jnp.bfloat16)
    low = (table - high.astype(np.float64)).astype(jnp.bfloat16)
    return np.stack([high, low])


def trig(first, second):
    angle = 2.0 * np.pi / PATCH * ((first[:, None] * second[None, :]) % PATCH)
    return np.cos(angle), np.sin(angle)


def column_tables():
    cosine, sine = trig(np.arange(PATCH), np.arange(HALF))
    table = np.zeros((PATCH, WIDE))
    table[:, :HALF] = cosine
    table[:, LANES : LANES + HALF] = sine
    spot = np.arange(SIDE)
    before = np.where(spot < PATCH - LANES, LANES + spot, SIDE + spot)
    outer = []
    for window in range(PATCH // STRIDE):
        start = window * STRIDE - MARGIN
        column = before if start < 0 else spot
        used = column >= start + PATCH if start < 0 else column < start
        high, low = split_table(table[column] * used[:, None])
        outer.append(np.concatenate([high, high, low], 0))
    return split_table(table), outer


def stacked(table):
    high, low = split_table(table)
    return np.concatenate([high, low, high], 1)


def frequency_rows(positions):
    cosine, sine = trig(np.arange(HALF), positions)
    return np.concatenate([cosine[:BAND], cosine[BAND:], sine[1:BAND]], 0)


def row_tables():
    tables = []
    for half in range(2):
        first = PATCH - HALO if half == 0 else 0
        position = np.concatenate([np.arange(PATCH), first + np.arange(HALO)])
        image_row = position + np.where(np.arange(HELD) < PATCH, 0, -PATCH if half == 0 else PATCH)
        rows = frequency_rows(position)
        windows = []
        for window in (2 * half, 2 * half + 1):
            start = window * STRIDE - MARGIN
            windows.append(rows * ((image_row >= start) & (image_row < start + PATCH)))
        tables.append(split_table(np.concatenate(windows, 0)))
    return tables


def inverse_tables():
    cosine, sine = trig(np.arange(PATCH), np.arange(HALF))
    weight = np.full((HALF,), 2.0 / PATCH)
    weight[0] = weight[-1] = 1.0 / PATCH
    cosine, sine = cosine * weight, sine * weight
    left = np.concatenate([cosine[:, :BAND], cosine[:, BAND:], -sine[:, 1:BAND]], 1)
    right = np.zeros((2 * LANES, PATCH))
    right[:HALF] = cosine.T
    right[LANES : LANES + HALF] = -sine.T
    return stacked(left), split_table(right)


def all_tables():
    mine, outer = column_tables()
    left, right = inverse_tables()
    blocks = [mine, outer[:2], outer[2:], *row_tables(), (left,), right]
    rows = []
    for parts in blocks:
        block = np.zeros((parts[0].shape[0], 2 * WIDE), jnp.bfloat16)
        for at, part in enumerate(parts):
            block[:, at * WIDE : at * WIDE + part.shape[1]] = part
        rows.append(block)
    return np.concatenate(rows, 0)


def dot(left, right):
    return jnp.dot(left, right, preferred_element_type=jnp.float32)


def halves_of(value):
    high = value.astype(jnp.bfloat16)
    return high, (value - high.astype(jnp.float32)).astype(jnp.bfloat16)


def table_first(table, value):
    high, low = halves_of(value)
    return dot(table, jnp.concatenate([high, high, low], 0))


def cross_spectrum(first, second):
    (acc, acs, asc, ass), (bcc, bcs, bsc, bss) = (
        (value[:BAND, :LANES], value[:BAND, LANES:], value[BAND:, :LANES], value[BAND:, LANES:])
        for value in (first, second)
    )
    even_0 = acc * bcc + acs * bcs
    even_1 = asc * bsc + ass * bss
    column_0 = acs * bcc - acc * bcs
    column_1 = ass * bsc - asc * bss
    by_row = asc * bcc - acc * bsc + ass * bcs - acs * bss
    both = acc * bss + ass * bcc - asc * bcs - acs * bsc
    top = SUBLANES
    lone = lax.broadcasted_iota(jnp.int32, (top, LANES), 0) == 0

    def with_top(usual, single):
        return jnp.concatenate([jnp.where(lone, single[:top], usual[:top]), usual[top:]], 0)

    even = with_top(even_0 + even_1, even_0)
    by_row = with_top(by_row, even_1)
    by_column = with_top(column_0 + column_1, column_0)
    both = with_top(both, column_1)
    return jnp.concatenate(
        [jnp.concatenate([even, by_column], 1), jnp.concatenate([by_row, both], 1)], 0
    )


def load_kernel(own_ref, table_ref, own_out, table_out, done):
    copies = [
        pltpu.make_async_copy(source, target, done.at[at])
        for at, (source, target) in enumerate([(own_ref, own_out), (table_ref, table_out)])
    ]
    for copy in copies:
        copy.start()
    for copy in copies:
        copy.wait()


def repeated(tail):
    return jnp.concatenate([tail] * (LANES // (PATCH - LANES)), 1)


def edge_kernel(own_ref, other_ref, out_ref):
    start = pl.multiple_of(jnp.where(lax.axis_index("gz") == 0, PATCH - HALO, 0), HALO // 2)
    lane = lax.broadcasted_iota(jnp.int32, (HALO, LANES), 1)
    tails = []
    for image, ref in enumerate((own_ref, other_ref)):
        rows = ref[0, pl.ds(start, HALO)]
        out_ref[:, image * LANES : (image + 1) * LANES] = rows[:, :LANES]
        tails.append(repeated(rows[:, LANES:].astype(jnp.float32)))
    tail = jnp.where(lane < PATCH - LANES, *tails)
    out_ref[:, 2 * LANES :] = tail.astype(jnp.bfloat16)


def edge_rows(beyond_ref):
    tail = beyond_ref[:, 2 * LANES :].astype(jnp.float32)
    turned = pltpu.roll(tail, LANES - (PATCH - LANES), 1)
    return [
        jnp.concatenate(
            [
                beyond_ref[:, image * LANES : (image + 1) * LANES],
                value[:, : PATCH - LANES].astype(jnp.bfloat16),
            ],
            1,
        )
        for image, value in enumerate((tail, turned))
    ]


def side_columns(tiles):
    tiles = [tile.astype(jnp.float32) for tile in tiles]
    wide = [tile[:, :LANES] for tile in tiles]
    narrow = [repeated(tile[:, LANES:]) for tile in tiles]
    lane = lax.broadcasted_iota(jnp.int32, wide[0].shape, 1)
    extra = PATCH - LANES
    low = jnp.where(lane < SIDE, wide[0], pltpu.roll(wide[1], SIDE, 1))
    high = jnp.where(lane < SIDE, pltpu.roll(wide[0], SIDE, 1), wide[1])
    high = jnp.where(lane < extra, narrow[0], high)
    high = jnp.where((lane >= SIDE) & (lane < SIDE + extra), narrow[1], high)
    low, high = low.astype(jnp.bfloat16), high.astype(jnp.bfloat16)
    odd = lax.rem(lax.axis_index("gx"), 2) == 1
    return [jnp.where(odd, *pair) for pair in ((low, high), (high, low))]


def pack_kernel(own_ref, other_ref, first_ref, second_ref):
    first_ref[:PATCH], second_ref[:PATCH] = side_columns([own_ref[0], other_ref[0]])


def pack_edge_kernel(beyond_ref, first_in, second_in, first_ref, second_ref):
    del first_in, second_in
    first_ref[PATCH:], second_ref[PATCH:] = side_columns(edge_rows(beyond_ref))


def to_row_frequencies(table_ref, half, pixels):
    start = pl.multiple_of(ROWS_AT + half * (2 * PATCH), HALO // 2)
    high = table_ref[pl.ds(start, 2 * PATCH), :HELD]
    low = table_ref[pl.ds(start, 2 * PATCH), WIDE : WIDE + HELD]
    return dot(high, pixels) + dot(low, pixels)


def finish(columns, side, own_spectra, own_side, beside_ref, table_ref, high_ref, low_ref, rows_ref):
    half = lax.axis_index("gz")
    group = columns // 2
    beside = to_row_frequencies(table_ref, half, beside_ref[...]) - own_side
    lane = lax.broadcasted_iota(jnp.int32, beside.shape, 1)
    parts = []
    for value in (beside, pltpu.roll(beside, SIDE, 1)):
        high = value.astype(jnp.bfloat16).astype(jnp.float32)
        parts.append((high, value - high))
    factors = []
    for image in range(2):
        high = parts[image][0]
        both = jnp.where(lane < SIDE, high, parts[1 - image][1])
        factors.append(jnp.concatenate([both, high[:, :SIDE]], 1).astype(jnp.bfloat16))
    upper = half == 0
    start = pl.multiple_of(HALO_AT + side * (3 * SIDE), HALO // 2)
    spectra = []
    for column in range(group):
        table = table_ref[pl.ds(start, 3 * SIDE), column * WIDE : (column + 1) * WIDE]
        for section in range(2):
            factor = jnp.where(upper, factors[section], factors[1 - section])
            spot = slice(section * 2 * PATCH, (section + 1) * 2 * PATCH)
            spectra.append(own_spectra[spot] + dot(factor, table))
    left = table_ref[LEFT_AT:RIGHT_AT, : 3 * PATCH]
    right = [table_ref[RIGHT_AT:, start : start + PATCH] for start in (0, WIDE)]
    count = 2 * group
    for patch in range(count):
        row, column = patch % 2, patch // 2
        start = row * PATCH
        cross = cross_spectrum(
            *(value[start : start + PATCH] for value in spectra[2 * column : 2 * column + 2])
        )
        high, low = halves_of(table_first(left, cross))
        high_ref[patch * PATCH : (patch + 1) * PATCH] = high
        low_ref[patch * PATCH : (patch + 1) * PATCH] = low
    for patch in range(count):
        if patch in (0, 3):
            first = patch
            ahead = [start for start in (0, 3) if start > patch] + [count]
            block = slice(first * PATCH, ahead[0] * PATCH)
            correl = dot(high_ref[block], right[0]) + dot(high_ref[block], right[1])
            correl = correl + dot(low_ref[block], right[0])
        squared = correl[(patch - first) * PATCH : (patch - first + 1) * PATCH]
        squared = squared * squared
        weights = squared * squared
        pieces = [weights[at : at + SUBLANES] for at in range(0, PATCH, SUBLANES)]
        middle = len(pieces) // 2
        above = pieces[middle - 1]
        ranks = above
        for piece in pieces[middle - 2 : 0 : -1]:
            above = above + piece
            ranks = ranks + above
        below = pieces[middle]
        depths = below
        for piece in pieces[middle + 1 :]:
            below = below + piece
            depths = depths + below
        total = pieces[0] + above + below
        based = float(SUBLANES) * (ranks - depths)
        step = lax.broadcasted_iota(jnp.int32, (SUBLANES, PATCH), 0).astype(jnp.float32)
        based = based + step * total
        rows_ref[0, pl.ds(patch, 1)] = jnp.sum(total, 0, keepdims=True)
        rows_ref[1, pl.ds(patch, 1)] = jnp.sum(based, 0, keepdims=True)
    totals = rows_ref[0]
    shift = lax.broadcasted_iota(jnp.int32, (count, PATCH), 1)
    shift = jnp.where(shift >= PATCH // 2, shift - PATCH, shift).astype(jnp.float32)
    below = jnp.sum(totals, 1, keepdims=True) + EPSILON
    flow_y = jnp.sum(rows_ref[1], 1, keepdims=True) / below
    flow_x = jnp.sum(totals * shift, 1, keepdims=True) / below
    at = lax.broadcasted_iota(jnp.int32, (count, LANES), 1)
    patch = lax.broadcasted_iota(jnp.int32, (count, LANES), 0)
    spot = (patch >> 1) + columns * (patch & 1) + side * group
    line = jnp.where(at == spot, flow_y, 0.0) + jnp.where(at == spot + 2 * count, flow_x, 0.0)
    return jnp.sum(line, 0, keepdims=True)


def early_kernel(columns, own_ref, other_ref, beyond_ref, early_side_ref, late_side_ref, beside_ref,
                 mask_ref, table_ref, line_ref, own_spectra_ref, own_side_ref, high_rows_ref,
                 low_rows_ref, high_ref, low_ref, rows_ref):
    half = lax.axis_index("gz")
    side = 1 - lax.rem(lax.axis_index("gx"), 2)
    tiles = (own_ref[0], other_ref[0])
    images = [jnp.concatenate(pair, 0) for pair in zip(tiles, edge_rows(beyond_ref))]
    upper = half == 0
    one, two = (table_ref[:PATCH, at : at + WIDE] for at in (0, WIDE))
    for section in range(2):
        pixels = jnp.where(upper, images[section], images[1 - section])
        spot = slice(section * 2 * PATCH, (section + 1) * 2 * PATCH)
        high_rows_ref[spot], low_rows_ref[spot] = halves_of(
            to_row_frequencies(table_ref, half, pixels)
        )
        high, low = high_rows_ref[spot], low_rows_ref[spot]
        own_spectra_ref[spot] = dot(high, one) + dot(high, two) + dot(low, one)
    own_side_ref[...] = to_row_frequencies(table_ref, half, late_side_ref[...])
    own_side = to_row_frequencies(table_ref, half, early_side_ref[...])
    line = finish(
        columns, side, own_spectra_ref, own_side, beside_ref, table_ref, high_ref, low_ref, rows_ref
    )
    lanes = lax.broadcasted_iota(jnp.int32, (1, LANES), 1)
    mask = mask_ref[0].astype(jnp.float32)
    for row in range(mask.shape[0]):
        for column in range(columns):
            spot = 4 * columns + row * columns + column
            line = jnp.where(lanes == spot, mask[row : row + 1, column : column + 1], line)
    line_ref[...] = line


def late_kernel(columns, line_ref, own_spectra_ref, own_side_ref, beside_ref, table_ref, out_ref,
                high_ref, low_ref, rows_ref):
    side = lax.rem(lax.axis_index("gx"), 2)
    line = finish(
        columns, side, own_spectra_ref, own_side_ref[...], beside_ref, table_ref, high_ref, low_ref, rows_ref
    )
    out_ref[...] = jnp.broadcast_to(line_ref[...] + line, out_ref.shape)


def relax_kernel(rows, columns, got_ref, flow_ref, offsets_ref):
    size_y, size_x = lax.axis_size("gy"), lax.axis_size("gx")
    half, at_y, at_x = lax.axis_index("gz"), lax.axis_index("gy"), lax.axis_index("gx")
    count = rows * columns
    tile_rows = 2 * rows
    width = columns + 2 * RADIUS
    height = tile_rows + 2 * RADIUS
    per_section = size_y * size_x
    lane = lax.broadcasted_iota(jnp.int32, (1, LANES), 1).astype(jnp.float32)
    line = jnp.floor((lane + 0.5) * (1.0 / width))
    across = lane - line * width
    node_y = line.astype(jnp.int32) - RADIUS + at_y * tile_rows
    node_x = across.astype(jnp.int32) - RADIUS + at_x * columns
    inside = (node_y >= 0) & (node_y < tile_rows * size_y) & (node_x >= 0)
    inside = inside & (node_x < columns * size_x) & (line < height)

    def parts(value, size):
        whole = jnp.floor((value.astype(jnp.float32) + 0.5) * (1.0 / size)).astype(jnp.int32)
        return whole, value - whole * size

    tile_y, in_y = parts(node_y, tile_rows)
    tile_x, in_x = parts(node_x, columns)
    side, in_half = parts(in_y, rows)
    tile = jnp.where(inside, tile_y * size_x + tile_x, -1)
    flow_spot = in_half * columns + in_x
    got = got_ref[...]
    spread = []
    for spot in (flow_spot, flow_spot + count, 2 * count + in_y * columns + in_x):
        lanes = jnp.broadcast_to(jnp.where(inside, spot, 0), got.shape)
        spread.append(jnp.take_along_axis(got, lanes, axis=1, mode="promise_in_bounds"))
    source = lax.broadcasted_iota(jnp.int32, (2 * per_section, LANES), 0)
    chosen = source == side * per_section + tile
    chosen = chosen & (tile >= 0)
    flow_y, flow_x = (
        jnp.sum(jnp.where(chosen, spread[axis], 0.0), 0, keepdims=True)
        for axis in range(2)
    )
    chosen = source[:per_section] == tile
    mask_0, mask_1 = (
        jnp.sum(jnp.where(chosen, spread[2][start : start + per_section], 0.0), 0, keepdims=True)
        for start in (0, per_section)
    )
    flows = jnp.concatenate([flow_y, flow_x], 0)
    weight = mask_0 * mask_1
    kept = inside.astype(jnp.float32)
    sign = jnp.where(lax.broadcasted_iota(jnp.int32, (4, LANES), 0) < 2, 1.0, -1.0)
    weight = weight * sign
    offsets = jnp.zeros((4, LANES), jnp.float32)
    for step in range(RELAX):
        lower, upper = offsets[:2], offsets[2:]
        pull = upper - lower - flows
        forces = weight * jnp.concatenate([pull, pull], 0)
        if step:
            left = jnp.where(across < 0.5, 0.0, pltpu.roll(offsets, 1, 1))
            right = jnp.where(across > width - 1.5, 0.0, pltpu.roll(offsets, LANES - 1, 1))
            laplace = pltpu.roll(offsets, width, 1) + pltpu.roll(offsets, LANES - width, 1)
            forces = STIFFNESS * (laplace + left + right - 4.0 * offsets) + forces
        offsets = (offsets + STEP_SIZE * forces) * kept
    first = half == 0
    result = jnp.where(first, offsets[:2], offsets[2:])
    flows = jnp.where(first, flows, 0.0)
    for row in range(tile_rows):
        start = (RADIUS + row) * width + RADIUS
        for axis in range(2):
            offsets_ref[axis, 0, pl.ds(row, 1)] = result[axis : axis + 1, start : start + columns]
            flow_ref[axis, 0, pl.ds(row, 1)] = flows[axis : axis + 1, start : start + columns]
    flow_ref[2:] = jnp.zeros((flow_ref.shape[0] - 2, *flow_ref.shape[1:]), jnp.float32)


def vmem(count):
    return [pl.BlockSpec(memory_space=pltpu.VMEM)] * count


def pair_body(images, tissue_mask):
    sections, size_y, size_x = (lax.axis_size(name) for name in ("gz", "gy", "gx"))
    count_y = images.shape[1] // STRIDE
    count_x = images.shape[2] // STRIDE
    rows = count_y // 2
    other = lax.ppermute(images, "gz", [(0, 1), (1, 0)])
    table = jnp.asarray(all_tables())
    own, table = pl.pallas_call(
        load_kernel,
        out_shape=(
            jax.ShapeDtypeStruct(images.shape, images.dtype),
            jax.ShapeDtypeStruct(table.shape, table.dtype),
        ),
        in_specs=[pl.BlockSpec(memory_space=pltpu.HBM)] * 2,
        out_specs=tuple(vmem(2)),
        scratch_shapes=[pltpu.SemaphoreType.DMA((2,))],
        compiler_params=pltpu.CompilerParams(vmem_limit_bytes=4 * 2**20),
        cost_estimate=pl.CostEstimate(flops=0, bytes_accessed=4 * table.size, transcendentals=0),
        name="load",
    )(images, table)
    edge = pl.pallas_call(
        edge_kernel,
        out_shape=jax.ShapeDtypeStruct((HALO, 3 * LANES), jnp.bfloat16),
        in_specs=vmem(2),
        out_specs=vmem(1)[0],
        compiler_params=pltpu.CompilerParams(vmem_limit_bytes=4 * 2**20),
        name="edge",
    )(own, other)
    onward = []
    for tile in range(1, size_y):
        onward += [(tile - 1, tile), (size_y + tile, size_y + tile - 1)]
    beyond = lax.ppermute(edge, ("gz", "gy"), onward)
    swaps = [
        [pair for left in range(offset, size_x - 1, 2) for pair in ((left, left + 1), (left + 1, left))]
        for offset in range(2)
    ]
    packed = jax.ShapeDtypeStruct((HELD, LANES), jnp.bfloat16)
    small = pltpu.CompilerParams(vmem_limit_bytes=4 * 2**20)
    sends = pl.pallas_call(
        pack_kernel,
        out_shape=(packed, packed),
        in_specs=vmem(2),
        out_specs=tuple(vmem(2)),
        compiler_params=small,
        cost_estimate=pl.CostEstimate(flops=10**6, bytes_accessed=2**18, transcendentals=0),
        name="pack",
    )(own, other)
    sends = pl.pallas_call(
        pack_edge_kernel,
        out_shape=(packed, packed),
        in_specs=vmem(3),
        out_specs=tuple(vmem(2)),
        input_output_aliases={1: 0, 2: 1},
        compiler_params=small,
        name="pack_edge",
    )(beyond, *sends)
    first, second = (lax.ppermute(send, "gx", swap) for send, swap in zip(sends, swaps))
    devices = sections * size_y * size_x

    patches = rows * count_x // 2
    common = [
        pltpu.VMEM((patches * PATCH, WIDE), jnp.bfloat16),
        pltpu.VMEM((patches * PATCH, WIDE), jnp.bfloat16),
        pltpu.VMEM((2, patches, PATCH), jnp.float32),
    ]
    params = pltpu.CompilerParams(vmem_limit_bytes=16 * 2**20)
    line, own_spectra, own_side = pl.pallas_call(
        functools.partial(early_kernel, count_x),
        out_shape=(
            jax.ShapeDtypeStruct((1, LANES), jnp.float32),
            jax.ShapeDtypeStruct((4 * PATCH, WIDE), jnp.float32),
            jax.ShapeDtypeStruct((2 * PATCH, LANES), jnp.float32),
        ),
        in_specs=vmem(8),
        out_specs=tuple(vmem(3)),
        scratch_shapes=[pltpu.VMEM((4 * PATCH, PATCH), jnp.bfloat16)] * 2 + common,
        compiler_params=params,
        cost_estimate=pl.CostEstimate(flops=2 * 10**9, bytes_accessed=2**21, transcendentals=0),
        name="early",
    )(own, other, beyond, sends[1], sends[0], first, tissue_mask, table)
    lines = pl.pallas_call(
        functools.partial(late_kernel, count_x),
        out_shape=jax.ShapeDtypeStruct((devices, LANES), jnp.float32),
        in_specs=vmem(5),
        out_specs=vmem(1)[0],
        scratch_shapes=common,
        compiler_params=params,
        cost_estimate=pl.CostEstimate(flops=10**9, bytes_accessed=2**21, transcendentals=0),
        name="late",
    )(line, own_spectra, own_side, second, table)
    got = lax.all_to_all(lines, ("gz", "gy", "gx"), 0, 0, tiled=True)
    return pl.pallas_call(
        functools.partial(relax_kernel, rows, count_x),
        out_shape=(
            jax.ShapeDtypeStruct((4, 1, count_y, count_x), jnp.float32),
            jax.ShapeDtypeStruct((2, 1, count_y, count_x), jnp.float32),
        ),
        in_specs=vmem(1),
        out_specs=tuple(vmem(2)),
        compiler_params=pltpu.CompilerParams(vmem_limit_bytes=4 * 2**20),
        name="relax",
    )(got)


def body(images, tissue_mask):
    paired = lax.axis_size("gz") == 2 and images.shape == (1, PATCH, PATCH)
    return (pair_body if paired else general_body)(images, tissue_mask)


def solution(mesh):
    placed = (P("gz", "gy", "gx"), P("gz", "gy", "gx"))
    return jax.shard_map(
        body,
        mesh=mesh,
        in_specs=placed,
        out_specs=(P(None, "gz", "gy", "gx"), P(None, "gz", "gy", "gx")),
        check_vma=False,
    )
```
